32 devices in a mesh: dp: 8 (over y, x, core), tensor: 4 (over z).
Axes of the slice: x: 2, y: 2, z: 4, core: 2. Of those that a mesh axis runs over, the one named last changes fastest.
Arguments:
- layer_input: bfloat16 [32768, 768], P('dp'), may hold values from -6 to 6
- segments: int32 [32, 1024], P('dp'), may hold values from 0 to 7, never falling along the last dimension, each value on 1 to 512 neighbouring positions
- query_weight: bfloat16 [768, 768], P(None, 'tensor'), may hold values from -0.21875 to 0.21875
- query_bias: float32 [768], P('tensor'), may hold values from -3 to 3
- key_weight: bfloat16 [768, 768], P(None, 'tensor'), may hold values from -0.21875 to 0.21875
- value_weight: bfloat16 [768, 768], P(None, 'tensor'), may hold values from -0.21875 to 0.21875
- value_bias: float32 [768], P('tensor'), may hold values from -3 to 3
- output_weight: bfloat16 [768, 768], P('tensor'), may hold values from -0.875 to 0.875
- output_bias: float32 [768], replicated, may hold values from -3 to 3
- first_gain: float32 [768], replicated, may hold values from 0.5 to 1.5
- first_shift: float32 [768], replicated, may hold values from -3 to 3
- up_weight: bfloat16 [768, 3072], P(None, 'tensor'), may hold values from -0.21875 to 0.21875
- up_bias: float32 [3072], P('tensor'), may hold values from -3 to 3
- down_weight: bfloat16 [3072, 768], P('tensor'), may hold values from -0.109375 to 0.109375
- down_bias: float32 [768], replicated, may hold values from -3 to 3
- second_gain: float32 [768], replicated, may hold values from 0.5 to 1.5
- second_shift: float32 [768], replicated, may hold values from -3 to 3
- output_grad: bfloat16 [32768, 768], P('dp'), may hold values from -6 to 6
Outputs:
- layer_output: bfloat16 [32768, 768], P(('dp', 'tensor'))
- input_grad: float32 [32768, 768], P(('dp', 'tensor'))
- grad_query_weight: float32 [768, 768], P('dp', 'tensor')
- grad_query_bias: float32 [768], P('tensor')
- grad_key_weight: float32 [768, 768], P('dp', 'tensor')
- grad_value_weight: float32 [768, 768], P('dp', 'tensor')
- grad_value_bias: float32 [768], P('tensor')
- grad_output_weight: float32 [768, 768], P('tensor', 'dp')
- grad_output_bias: float32 [768], P(('dp', 'tensor'))
- grad_first_gain: float32 [768], P(('dp', 'tensor'))
- grad_first_shift: float32 [768], P(('dp', 'tensor'))
- grad_up_weight: float32 [768, 3072], P('dp', 'tensor')
- grad_up_bias: float32 [3072], P('tensor')
- grad_down_weight: float32 [3072, 768], P('tensor', 'dp')
- grad_down_bias: float32 [768], P(('dp', 'tensor'))
- grad_second_gain: float32 [768], P(('dp', 'tensor'))
- grad_second_shift: float32 [768], P(('dp', 'tensor'))
The draws below stay inside these ranges and needn't reach their ends.
Inputs may be any that keep to these rules, and one draw needn't show every extreme that they name: `segments`: segment numbers restart in every packed row; a token attends exactly to the tokens of its own row that carry its segment number.
All inputs are finite; a program needn't handle non-finite values.
Results may differ from the reference program's by a relative error of at most 0.02.
The reference program's roundings to bfloat16 on the way count: a program that leaves them out, or rounds other values in their place, can miss the bound.
Values may be sent and summed in bfloat16 or wider, within the bound.
A program may use at most 256 MiB of HBM per device.

```python
import math
from functools import partial
import jax
import jax.numpy as jnp
import numpy as np
from jax import lax

D = 768
HEADS = 12
HEAD_DIM = 64
FF = 3072
SEQ = 1024
PACKED = 32
TOKENS = 32768
N_TENSOR = 4


def with_spikes(result, key, source, target, blocks, factor):
    def block_of(position):
        return (jnp.arange(result.shape[position]) // (result.shape[position] // blocks)).reshape((-1,) + (1,) * (result.ndim - 1 - position))

    first = jax.random.permutation(key, blocks)[block_of(target)]
    far = (block_of(target) + blocks // 2) % blocks
    return jnp.where((block_of(source) == first) | (block_of(source) == far), factor * result, result)


def level_of(own_key, extent, shards, low, top_value):
    gain, own = 1.0, jax.random.fold_in(own_key, 6)
    for axis_at, shards_of in shards:
        heights = jnp.exp(jax.random.uniform(jax.random.fold_in(own, axis_at), (shards_of,), jnp.float32, low / len(shards), top_value / len(shards)))
        gain = gain * jnp.repeat(heights, extent[axis_at] // shards_of).reshape([-1 if axis == axis_at else 1 for axis in range(len(extent))])
    return gain


def profile(count, total, reach, skew):
    loads = [(1 << 20) // math.isqrt(grade ** skew) + 1 for grade in range(2, count + 1)]
    rest, holding = total - reach - (count - 1), [1] * (count - 1)
    while rest > 0:
        candidates = [i for i in range(count - 1) if holding[i] < reach]
        whole, left = sum([loads[i] for i in candidates]), rest
        for i in candidates:
            more = min(reach - holding[i], max(1, left * loads[i] // whole), rest)
            holding[i] = holding[i] + more
            rest = rest - more
    return np.array([reach] + holding)


def ragged(rng, number_of, total, reach, skew):
    if number_of == 2:
        one = jax.random.randint(rng, (), max(1, total - reach), min(reach, total - 1) + 1)
        return jnp.stack([one, total - one])
    tallies = jnp.asarray(profile(number_of, total, reach, skew), jnp.int32)
    couples = (number_of - 1) // 2
    donor, taker = tallies[1:1 + 2 * couples:2], tallies[2:2 + 2 * couples:2]
    room = jnp.minimum(donor - 1, reach - taker)
    passed = jax.random.randint(jax.random.fold_in(rng, 1), (couples,), 0, 1 << 20) % (room + 1)
    tallies = tallies.at[1:1 + 2 * couples:2].set(donor - passed).at[2:2 + 2 * couples:2].set(taker + passed)
    return tallies[jax.random.permutation(jax.random.fold_in(rng, 2), number_of)]


def gaussian(rng, dims, width, limit, cuts=(), kind=jnp.bfloat16):
    drawn = width * jax.random.normal(rng, dims, jnp.float32)
    if cuts:
        drawn = drawn * level_of(rng, dims, cuts, -0.22, 0.18)
    return jnp.clip(drawn, -limit, limit).astype(kind)


def noise_with(key, dims, deviation, reach, cuts, heavy, kind=jnp.bfloat16):
    array = deviation * jax.random.normal(key, dims, jnp.float32)
    if cuts:
        array = array * level_of(key, dims, cuts, -0.22, 0.18)
    return jnp.clip(with_spikes(array, jax.random.fold_in(key, 3), *heavy), -reach, reach).astype(kind)


def setup_inputs(seed: int = 0) -> dict:
    arg_keys = jax.random.split(jax.random.key(seed), 19)
    layer_input = noise_with(arg_keys[0], (TOKENS, D), 1.0, 6.0, ((0, 8),), (0, 1, 8, 2.0))
    segments = jax.vmap(lambda own: jnp.searchsorted(jnp.cumsum(ragged(own, 8, SEQ, SEQ // 2, 2)), jnp.arange(SEQ), side="right"))(jax.random.split(arg_keys[1], PACKED)).reshape((PACKED, SEQ)).astype(jnp.int32)
    query_weight = gaussian(arg_keys[2], (D, D), D ** -0.5, 0.21875, ((1, 4),))
    query_bias = gaussian(arg_keys[3], (D,), 0.5, 3.0, ((0, 4),), jnp.float32)
    key_weight = gaussian(arg_keys[4], (D, D), D ** -0.5, 0.21875, ((1, 4),))
    value_weight = gaussian(arg_keys[5], (D, D), D ** -0.5, 0.21875, ((1, 4),))
    value_bias = gaussian(arg_keys[6], (D,), 0.5, 3.0, ((0, 4),), jnp.float32)
    output_weight = gaussian(arg_keys[7], (D, D), (D // 16) ** -0.5, 0.875, ((0, 4),))
    output_bias = gaussian(arg_keys[8], (D,), 0.5, 3.0, (), jnp.float32)
    first_gain = jnp.clip(1.0 + 0.1 * jax.random.normal(arg_keys[9], (D,), jnp.float32), 0.5, 1.5)
    first_shift = gaussian(arg_keys[10], (D,), 0.5, 3.0, (), jnp.float32)
    up_weight = gaussian(arg_keys[11], (D, FF), D ** -0.5, 0.21875, ((1, 4),))
    up_bias = gaussian(arg_keys[12], (FF,), 0.5, 3.0, ((0, 4),), jnp.float32)
    down_weight = gaussian(arg_keys[13], (FF, D), FF ** -0.5, 0.109375, ((0, 4),))
    down_bias = gaussian(arg_keys[14], (D,), 0.5, 3.0, (), jnp.float32)
    second_gain = jnp.clip(1.0 + 0.1 * jax.random.normal(arg_keys[15], (D,), jnp.float32), 0.5, 1.5)
    second_shift = gaussian(arg_keys[16], (D,), 0.5, 3.0, (), jnp.float32)
    output_grad = noise_with(arg_keys[17], (TOKENS, D), 1.0, 6.0, ((0, 8),), (0, 1, 8, 2.0))
    return dict(layer_input=layer_input, segments=segments, query_weight=query_weight, query_bias=query_bias, key_weight=key_weight, value_weight=value_weight, value_bias=value_bias, output_weight=output_weight, output_bias=output_bias, first_gain=first_gain, first_shift=first_shift, up_weight=up_weight, up_bias=up_bias, down_weight=down_weight, down_bias=down_bias, second_gain=second_gain, second_shift=second_shift, output_grad=output_grad)


@jax.custom_vjp
def low(v):
    return lax.optimization_barrier(v.astype(jnp.bfloat16)).astype(jnp.float32)

@jax.custom_vjp
def low_back(v):
    return v

def low_keep(v):
    return (low(v), None)

def low_pass(kept, grad):
    return (grad,)

def back_keep(v):
    return (v, None)

def back_low(kept, grad):
    return (low(grad),)
low.defvjp(low_keep, low_pass)
low_back.defvjp(back_keep, back_low)
norm_eps = 1e-06
highest = lax.Precision.HIGHEST

def matmul(left_side, right_side):
    return jnp.dot(left_side, right_side, precision=highest, preferred_element_type=jnp.float32)

def layer_norm(summed, norm_gain, offset):
    mean_row = lax.optimization_barrier(jnp.mean(summed, -1, keepdims=True))
    centred = summed - mean_row
    spread = lax.optimization_barrier(jnp.mean(centred * centred, -1, keepdims=True))
    return centred * lax.rsqrt(spread + norm_eps) * norm_gain + offset

def attend_row(queries, key_side, value_proj, segment_row):
    length = queries.shape[0]
    query_heads = queries.reshape(length, HEADS, HEAD_DIM)
    key_heads = key_side.reshape(length, HEADS, HEAD_DIM)
    value_heads = value_proj.reshape(length, HEADS, HEAD_DIM)
    scores = jnp.einsum('qhd,khd->hqk', query_heads, key_heads, precision=highest) * HEAD_DIM ** (-0.5)
    scores = low_back(scores)
    linked = segment_row[:, None] == segment_row[None, :]
    scores = jnp.where(linked[None], scores, -1e+30)
    softmaxed = low(jax.nn.softmax(scores, axis=-1))
    context = jnp.einsum('hqk,khd->qhd', softmaxed, value_heads, precision=highest)
    return low(low_back(context.reshape(length, HEADS * HEAD_DIM)))

def attend_packed(inputs):
    return jax.checkpoint(attend_row)(inputs[0], inputs[1], inputs[2], inputs[3])

def forward(layer_input, query_weight, query_bias, key_weight, value_weight, value_bias, output_weight, output_bias, first_gain, first_shift, up_weight, up_bias, down_weight, down_bias, second_gain, second_shift, segments):
    input_low = low(layer_input)
    queries = low(low_back(matmul(input_low, query_weight) + query_bias))
    key_side = low(low_back(matmul(input_low, key_weight)))
    value_proj = low(low_back(matmul(input_low, value_weight) + value_bias))
    row_count = segments.shape[0]
    shaped = (row_count, SEQ, D)
    context = lax.map(attend_packed, (queries.reshape(shaped), key_side.reshape(shaped), value_proj.reshape(shaped), segments))
    context = context.reshape(row_count * SEQ, D)
    group_width = D // N_TENSOR
    attn_total = sum((low(matmul(context[:, member * group_width:(member + 1) * group_width], output_weight[member * group_width:(member + 1) * group_width])) for member in range(N_TENSOR)))
    first_in = layer_input + low_back(attn_total) + output_bias
    first_out = layer_norm(first_in, first_gain, first_shift)
    first_low = low(first_out)
    pre_act = low_back(matmul(first_low, up_weight) + up_bias)
    hidden_low = low(jax.nn.gelu(pre_act, approximate=True))
    unit_width = FF // N_TENSOR
    down_total = sum((low(matmul(hidden_low[:, member * unit_width:(member + 1) * unit_width], down_weight[member * unit_width:(member + 1) * unit_width])) for member in range(N_TENSOR)))
    second_in = first_out + low_back(down_total) + down_bias
    return layer_norm(second_in, second_gain, second_shift)

def reference(layer_input, segments, query_weight, query_bias, key_weight, value_weight, value_bias, output_weight, output_bias, first_gain, first_shift, up_weight, up_bias, down_weight, down_bias, second_gain, second_shift, output_grad):
    params = (layer_input.astype(jnp.float32), query_weight.astype(jnp.float32), query_bias.astype(jnp.float32), key_weight.astype(jnp.float32), value_weight.astype(jnp.float32), value_bias.astype(jnp.float32), output_weight.astype(jnp.float32), output_bias.astype(jnp.float32), first_gain.astype(jnp.float32), first_shift.astype(jnp.float32), up_weight.astype(jnp.float32), up_bias.astype(jnp.float32), down_weight.astype(jnp.float32), down_bias.astype(jnp.float32), second_gain.astype(jnp.float32), second_shift.astype(jnp.float32))
    layer_output, pull_back = jax.vjp(partial(forward, segments=segments), *params)
    gradients = pull_back(output_grad.astype(jnp.float32))
    return (layer_output.astype(jnp.bfloat16), gradients[0], gradients[1], gradients[2], gradients[3], gradients[4], gradients[5], gradients[6], gradients[7], gradients[8], gradients[9], gradients[10], gradients[11], gradients[12], gradients[13], gradients[14], gradients[15])
```

```python
import jax
import jax.numpy as jnp
from jax import lax
from jax.sharding import PartitionSpec as P

HEAD_DIM = 64
GROUP_HEADS = 3

norm_eps = 1e-06


def product(left_side, right_side):
    return jnp.dot(left_side, right_side, preferred_element_type=jnp.float32)


def contract_rows(left_side, right_side):
    return lax.dot_general(
        left_side, right_side, (((0,), (0,)), ((), ())), preferred_element_type=jnp.float32
    )


def contract_last(left_side, right_side):
    return lax.dot_general(
        left_side, right_side, (((1,), (1,)), ((), ())), preferred_element_type=jnp.float32
    )


def normalize(summed, norm_gain, offset):
    centred = summed - jnp.mean(summed, -1, keepdims=True)
    inverse = lax.rsqrt(jnp.mean(centred * centred, -1, keepdims=True) + norm_eps)
    scaled = centred * inverse
    return (scaled * norm_gain + offset, scaled, inverse)


def normalize_back(grad_out, scaled, inverse, norm_gain):
    grad_scaled = grad_out * norm_gain
    mean_grad = jnp.mean(grad_scaled, -1, keepdims=True)
    mean_cross = jnp.mean(grad_scaled * scaled, -1, keepdims=True)
    return inverse * (grad_scaled - mean_grad - scaled * mean_cross)


def gelu_tanh(pre_act):
    return jax.nn.gelu(pre_act, approximate=True)


def score_group(query_group, key_group, segment_row):
    scores = jnp.einsum(
        "qhd,khd->hqk", query_group, key_group, preferred_element_type=jnp.float32
    ) * HEAD_DIM ** (-0.5)
    linked = segment_row[:, None] == segment_row[None, :]
    return jnp.where(linked[None], scores, -1e30)


def split_groups(rows_by_width):
    length, width = rows_by_width.shape
    groups = width // (GROUP_HEADS * HEAD_DIM)
    return rows_by_width.reshape(length, groups, GROUP_HEADS, HEAD_DIM).transpose(1, 0, 2, 3)


def join_groups(grouped):
    groups, length, heads, dim = grouped.shape
    return grouped.transpose(1, 0, 2, 3).reshape(length, groups * heads * dim)


def attend(queries, key_side, value_proj, segment_row):
    def one_group(inputs):
        query_group, key_group, value_group = inputs
        scores = score_group(query_group, key_group, segment_row)
        row_max = jnp.max(scores, -1, keepdims=True)
        exp_scores = jnp.exp(scores - row_max)
        row_total = jnp.sum(exp_scores, -1, keepdims=True)
        prob_low = (exp_scores / row_total).astype(jnp.bfloat16)
        context = jnp.einsum(
            "hqk,khd->qhd", prob_low, value_group, preferred_element_type=jnp.float32
        )
        return (context.astype(jnp.bfloat16), (row_max + jnp.log(row_total))[..., 0])

    context, log_total = lax.map(
        one_group, (split_groups(queries), split_groups(key_side), split_groups(value_proj))
    )
    return (join_groups(context), log_total)


def attend_back(queries, key_side, value_proj, segment_row, log_total, grad_context):
    def one_group(inputs):
        query_group, key_group, value_group, log_group, grad_group = inputs
        scores = score_group(query_group, key_group, segment_row)
        probs_full = jnp.exp(scores - log_group[..., None])
        grad_probs = jnp.einsum(
            "qhd,khd->hqk", grad_group, value_group, preferred_element_type=jnp.float32
        )
        inner_sum = jnp.sum(probs_full * grad_probs, -1, keepdims=True)
        grad_scores = (probs_full * (grad_probs - inner_sum)).astype(jnp.bfloat16)
        grad_query = jnp.einsum(
            "hqk,khd->qhd", grad_scores, key_group, preferred_element_type=jnp.float32
        ) * HEAD_DIM ** (-0.5)
        grad_key = jnp.einsum(
            "hqk,qhd->khd", grad_scores, query_group, preferred_element_type=jnp.float32
        ) * HEAD_DIM ** (-0.5)
        grad_value = jnp.einsum(
            "hqk,qhd->khd",
            probs_full.astype(jnp.bfloat16),
            grad_group,
            preferred_element_type=jnp.float32,
        )
        return (
            grad_query.astype(jnp.bfloat16),
            grad_key.astype(jnp.bfloat16),
            grad_value.astype(jnp.bfloat16),
        )

    grad_query, grad_key, grad_value = lax.map(
        one_group,
        (
            split_groups(queries),
            split_groups(key_side),
            split_groups(value_proj),
            log_total,
            split_groups(grad_context),
        ),
    )
    return (join_groups(grad_query), join_groups(grad_key), join_groups(grad_value))


def gather_shards(pieces):
    flat = jnp.concatenate([piece.reshape(-1) for piece in pieces])
    dp_count = lax.axis_size("dp")
    core = lax.rem(lax.axis_index("dp"), 2)
    half = flat.shape[0] // 2
    mine = lax.dynamic_slice_in_dim(flat, core * half, half, 0)
    gathered = lax.all_gather(mine, "tensor", axis=0, tiled=False)
    other = lax.ppermute(gathered, "dp", perm=[(i, i ^ 1) for i in range(dp_count)])
    both = jnp.where(
        core == 0,
        jnp.concatenate([gathered, other], axis=1),
        jnp.concatenate([other, gathered], axis=1),
    )
    shards = []
    start = 0
    for piece in pieces:
        size = piece.size
        shards.append(both[:, start : start + size].reshape((both.shape[0],) + piece.shape))
        start += size
    return shards


def join_columns(shards):
    count, rows, cols = shards.shape
    return shards.transpose(1, 0, 2).reshape(rows, count * cols)


def join_rows(shards):
    count, rows, cols = shards.shape
    return shards.reshape(count * rows, cols)


def scatter_blocks(full, row_axis, col_axis):
    row_parts = lax.axis_size(row_axis)
    col_parts = lax.axis_size(col_axis)
    rows, cols = full.shape
    blocks = full.reshape(row_parts, rows // row_parts, col_parts, cols // col_parts)
    if row_axis == "dp":
        blocks = blocks.transpose(0, 2, 1, 3)
    else:
        blocks = blocks.transpose(2, 0, 1, 3)
    blocks = blocks.reshape(row_parts * col_parts * (rows // row_parts), cols // col_parts)
    return lax.psum_scatter(blocks, ("dp", "tensor"), scatter_dimension=0, tiled=True)


def on_device(
    layer_input,
    segments,
    query_weight,
    query_bias,
    key_weight,
    value_weight,
    value_bias,
    output_weight,
    output_bias,
    first_gain,
    first_shift,
    up_weight,
    up_bias,
    down_weight,
    down_bias,
    second_gain,
    second_shift,
    output_grad,
):
    part_count = lax.axis_size("tensor")
    part_id = lax.axis_index("tensor")
    row_len = segments.shape[1]
    dp_count = lax.axis_size("dp")

    input_rows = lax.dynamic_slice_in_dim(layer_input, part_id * row_len, row_len, 0)
    segment_row = lax.dynamic_index_in_dim(segments, part_id, 0, keepdims=False)
    grad_out = lax.dynamic_slice_in_dim(output_grad, part_id * row_len, row_len, 0).astype(
        jnp.float32
    )

    q_sh, k_sh, v_sh, o_sh = gather_shards([query_weight, key_weight, value_weight, output_weight])
    u_sh, d_sh = gather_shards([up_weight, down_weight])
    bias_sh = lax.all_gather(
        jnp.concatenate([query_bias, value_bias, up_bias]), "tensor", axis=0, tiled=False
    )
    qw = join_columns(q_sh)
    kw = join_columns(k_sh)
    vw = join_columns(v_sh)
    ow = join_rows(o_sh)
    uw = join_columns(u_sh)
    dw = join_rows(d_sh)
    head_width = query_bias.shape[0]
    qb = bias_sh[:, :head_width].reshape(-1)
    vb = bias_sh[:, head_width : 2 * head_width].reshape(-1)
    ub = bias_sh[:, 2 * head_width :].reshape(-1)

    input_f32 = input_rows.astype(jnp.float32)
    queries = (product(input_rows, qw) + qb).astype(jnp.bfloat16)
    key_side = product(input_rows, kw).astype(jnp.bfloat16)
    value_proj = (product(input_rows, vw) + vb).astype(jnp.bfloat16)
    context, log_total = attend(queries, key_side, value_proj, segment_row)

    group_width = ow.shape[0] // part_count
    attn_total = input_f32
    for member in range(part_count):
        cols = slice(member * group_width, (member + 1) * group_width)
        attn_total = attn_total + product(context[:, cols], ow[cols]).astype(
            jnp.bfloat16
        ).astype(jnp.float32)
    first_in = attn_total + output_bias
    first_out, first_unit, first_inv = normalize(first_in, first_gain, first_shift)
    first_low = first_out.astype(jnp.bfloat16)
    pre_act = product(first_low, uw) + ub
    gelu_out, pull_gelu = jax.vjp(gelu_tanh, pre_act)
    hidden_low = gelu_out.astype(jnp.bfloat16)
    unit_width = dw.shape[0] // part_count
    second_in = first_out
    for member in range(part_count):
        units = slice(member * unit_width, (member + 1) * unit_width)
        second_in = second_in + product(hidden_low[:, units], dw[units]).astype(
            jnp.bfloat16
        ).astype(jnp.float32)
    second_in = second_in + down_bias
    second_out, second_unit, second_inv = normalize(second_in, second_gain, second_shift)
    layer_output = second_out.astype(jnp.bfloat16)

    grad_second = normalize_back(grad_out, second_unit, second_inv, second_gain)
    grad_second_gain = jnp.sum(grad_out * second_unit, 0)
    grad_second_shift = jnp.sum(grad_out, 0)
    grad_down_bias = jnp.sum(grad_second, 0)
    down_low = grad_second.astype(jnp.bfloat16)
    grad_down_weight = contract_rows(hidden_low, down_low)
    grad_hidden = contract_last(down_low, dw)
    grad_pre = pull_gelu(grad_hidden)[0].astype(jnp.bfloat16)
    grad_up_weight = contract_rows(first_low, grad_pre)
    grad_up_bias = jnp.sum(grad_pre, 0, dtype=jnp.float32)
    first_grad = contract_last(grad_pre, uw) + grad_second
    grad_first_gain = jnp.sum(first_grad * first_unit, 0)
    grad_first_shift = jnp.sum(first_grad, 0)
    attn_grad = normalize_back(first_grad, first_unit, first_inv, first_gain)
    grad_output_bias = jnp.sum(attn_grad, 0)
    attn_grad_low = attn_grad.astype(jnp.bfloat16)
    grad_output_weight = contract_rows(context, attn_grad_low)
    grad_context = contract_last(attn_grad_low, ow).astype(jnp.bfloat16)
    query_low, key_low, value_low = attend_back(
        queries, key_side, value_proj, segment_row, log_total, grad_context
    )
    grad_query_weight = contract_rows(input_rows, query_low)
    grad_key_weight = contract_rows(input_rows, key_low)
    grad_value_weight = contract_rows(input_rows, value_low)
    grad_query_bias = jnp.sum(query_low, 0, dtype=jnp.float32)
    grad_value_bias = jnp.sum(value_low, 0, dtype=jnp.float32)
    input_grad = (
        attn_grad
        + contract_last(query_low, qw)
        + contract_last(key_low, kw)
        + contract_last(value_low, vw)
    )

    summed_weights = (
        scatter_blocks(grad_query_weight, "dp", "tensor"),
        scatter_blocks(grad_key_weight, "dp", "tensor"),
        scatter_blocks(grad_value_weight, "dp", "tensor"),
        scatter_blocks(grad_output_weight, "tensor", "dp"),
        scatter_blocks(grad_up_weight, "dp", "tensor"),
        scatter_blocks(grad_down_weight, "tensor", "dp"),
    )
    shared = jnp.stack(
        [
            grad_output_bias,
            grad_first_gain,
            grad_first_shift,
            grad_down_bias,
            grad_second_gain,
            grad_second_shift,
        ]
    )
    shared_parts = dp_count * part_count
    shared = shared.reshape(6, shared_parts, -1).transpose(1, 0, 2)
    shared = lax.psum_scatter(shared, ("dp", "tensor"), scatter_dimension=0, tiled=True)[0]
    split = jnp.concatenate(
        [
            grad_query_bias.reshape(part_count, -1),
            grad_value_bias.reshape(part_count, -1),
            grad_up_bias.reshape(part_count, -1),
        ],
        axis=1,
    )
    split = lax.psum(
        lax.psum_scatter(split, "tensor", scatter_dimension=0, tiled=True)[0], "dp"
    )
    return (
        layer_output,
        input_grad,
        summed_weights[0],
        split[:head_width],
        summed_weights[1],
        summed_weights[2],
        split[head_width : 2 * head_width],
        summed_weights[3],
        shared[0],
        shared[1],
        shared[2],
        summed_weights[4],
        split[2 * head_width :],
        summed_weights[5],
        shared[3],
        shared[4],
        shared[5],
    )


def solution(mesh):
    in_specs = (
        P("dp", None),
        P("dp", None),
        P(None, "tensor"),
        P("tensor"),
        P(None, "tensor"),
        P(None, "tensor"),
        P("tensor"),
        P("tensor", None),
        P(),
        P(),
        P(),
        P(None, "tensor"),
        P("tensor"),
        P("tensor", None),
        P(),
        P(),
        P(),
        P("dp", None),
    )
    out_specs = (
        P(("dp", "tensor"), None),
        P(("dp", "tensor"), None),
        P("dp", "tensor"),
        P("tensor"),
        P("dp", "tensor"),
        P("dp", "tensor"),
        P("tensor"),
        P("tensor", "dp"),
        P(("dp", "tensor")),
        P(("dp", "tensor")),
        P(("dp", "tensor")),
        P("dp", "tensor"),
        P("tensor"),
        P("tensor", "dp"),
        P(("dp", "tensor")),
        P(("dp", "tensor")),
        P(("dp", "tensor")),
    )
    return jax.shard_map(
        on_device, mesh=mesh, in_specs=in_specs, out_specs=out_specs, check_vma=False
    )
```

```python
import jax
import jax.numpy as jnp
from jax import lax
from jax.sharding import PartitionSpec as P

HEAD_DIM = 64
GROUP_HEADS = 3

norm_eps = 1e-06


def product(left_side, right_side):
    return jnp.dot(left_side, right_side, preferred_element_type=jnp.float32)


def contract_rows(left_side, right_side):
    return lax.dot_general(
        left_side, right_side, (((0,), (0,)), ((), ())), preferred_element_type=jnp.float32
    )


def contract_last(left_side, right_side):
    return lax.dot_general(
        left_side, right_side, (((1,), (1,)), ((), ())), preferred_element_type=jnp.float32
    )


def normalize(summed, norm_gain, offset):
    centred = summed - jnp.mean(summed, -1, keepdims=True)
    inverse = lax.rsqrt(jnp.mean(centred * centred, -1, keepdims=True) + norm_eps)
    scaled = centred * inverse
    return (scaled * norm_gain + offset, scaled, inverse)


def normalize_back(grad_out, scaled, inverse, norm_gain):
    grad_scaled = grad_out * norm_gain
    mean_grad = jnp.mean(grad_scaled, -1, keepdims=True)
    mean_cross = jnp.mean(grad_scaled * scaled, -1, keepdims=True)
    return inverse * (grad_scaled - mean_grad - scaled * mean_cross)


def gelu_tanh(pre_act):
    return jax.nn.gelu(pre_act, approximate=True)


def score_group(query_group, key_group, segment_row):
    scores = jnp.einsum(
        "qhd,khd->hqk", query_group, key_group, preferred_element_type=jnp.float32
    ) * HEAD_DIM ** (-0.5)
    linked = segment_row[:, None] == segment_row[None, :]
    return jnp.where(linked[None], scores, -1e30)


def split_groups(rows_by_width):
    length, width = rows_by_width.shape
    groups = width // (GROUP_HEADS * HEAD_DIM)
    return rows_by_width.reshape(length, groups, GROUP_HEADS, HEAD_DIM).transpose(1, 0, 2, 3)


def join_groups(grouped):
    groups, length, heads, dim = grouped.shape
    return grouped.transpose(1, 0, 2, 3).reshape(length, groups * heads * dim)


def attend(queries, key_side, value_proj, segment_row):
    def one_group(inputs):
        query_group, key_group, value_group = inputs
        scores = score_group(query_group, key_group, segment_row)
        row_max = jnp.max(scores, -1, keepdims=True)
        exp_scores = jnp.exp(scores - row_max)
        row_total = jnp.sum(exp_scores, -1, keepdims=True)
        prob_low = (exp_scores / row_total).astype(jnp.bfloat16)
        context = jnp.einsum(
            "hqk,khd->qhd", prob_low, value_group, preferred_element_type=jnp.float32
        )
        return (context.astype(jnp.bfloat16), (row_max + jnp.log(row_total))[..., 0])

    context, log_total = lax.map(
        one_group, (split_groups(queries), split_groups(key_side), split_groups(value_proj))
    )
    return (join_groups(context), log_total)


def attend_back(queries, key_side, value_proj, segment_row, log_total, grad_context):
    def one_group(inputs):
        query_group, key_group, value_group, log_group, grad_group = inputs
        scores = score_group(query_group, key_group, segment_row)
        probs_full = jnp.exp(scores - log_group[..., None])
        grad_probs = jnp.einsum(
            "qhd,khd->hqk", grad_group, value_group, preferred_element_type=jnp.float32
        )
        inner_sum = jnp.sum(probs_full * grad_probs, -1, keepdims=True)
        grad_scores = (probs_full * (grad_probs - inner_sum)).astype(jnp.bfloat16)
        grad_query = jnp.einsum(
            "hqk,khd->qhd", grad_scores, key_group, preferred_element_type=jnp.float32
        ) * HEAD_DIM ** (-0.5)
        grad_key = jnp.einsum(
            "hqk,qhd->khd", grad_scores, query_group, preferred_element_type=jnp.float32
        ) * HEAD_DIM ** (-0.5)
        grad_value = jnp.einsum(
            "hqk,qhd->khd",
            probs_full.astype(jnp.bfloat16),
            grad_group,
            preferred_element_type=jnp.float32,
        )
        return (
            grad_query.astype(jnp.bfloat16),
            grad_key.astype(jnp.bfloat16),
            grad_value.astype(jnp.bfloat16),
        )

    grad_query, grad_key, grad_value = lax.map(
        one_group,
        (
            split_groups(queries),
            split_groups(key_side),
            split_groups(value_proj),
            log_total,
            split_groups(grad_context),
        ),
    )
    return (join_groups(grad_query), join_groups(grad_key), join_groups(grad_value))


def gather_shards(first_pieces, second_pieces):
    dp_count = lax.axis_size("dp")
    core = lax.rem(lax.axis_index("dp"), 2)

    def flat(pieces):
        return jnp.concatenate([piece.reshape(-1) for piece in pieces]).reshape(-1, 128)

    first, second = flat(first_pieces), flat(second_pieces)
    mine = jnp.where(core == 0, first, second)
    gathered = lax.all_gather(mine, "tensor", axis=0, tiled=False)
    other = lax.ppermute(gathered, "dp", perm=[(i, i ^ 1) for i in range(dp_count)])
    halves = (jnp.where(core == 0, gathered, other), jnp.where(core == 0, other, gathered))
    shards = []
    for half, pieces in zip(halves, (first_pieces, second_pieces)):
        half = half.reshape(half.shape[0], -1)
        start = 0
        for piece in pieces:
            size = piece.size
            shards.append(half[:, start : start + size].reshape((half.shape[0],) + piece.shape))
            start += size
    return shards


def join_columns(shards):
    count, rows, cols = shards.shape
    return shards.transpose(1, 0, 2).reshape(rows, count * cols)


def join_rows(shards):
    count, rows, cols = shards.shape
    return shards.reshape(count * rows, cols)


def blocked_grad(left_side, right_side, row_axis, col_axis):
    row_parts = lax.axis_size(row_axis)
    col_parts = lax.axis_size(col_axis)
    tokens, rows = left_side.shape
    cols = right_side.shape[1]
    left = left_side.reshape(tokens, row_parts, rows // row_parts)
    right = right_side.reshape(tokens, col_parts, cols // col_parts)
    spec = "nai,nbj->abij" if row_axis == "dp" else "nbi,naj->abij"
    return jnp.einsum(spec, left, right, preferred_element_type=jnp.float32)


def join_grads(blocks):
    parts = blocks[0].shape[0] * blocks[0].shape[1]
    joined = jnp.concatenate([block.reshape(parts, -1, 128) for block in blocks], axis=1)
    return joined.reshape(-1, 128)


def scatter_grads(joined, blocks):
    summed = lax.psum_scatter(joined, ("dp", "tensor"), scatter_dimension=0, tiled=True)
    summed = summed.reshape(-1)
    pieces = []
    start = 0
    for block in blocks:
        size = block[0, 0].size
        pieces.append(summed[start : start + size].reshape(block.shape[2:]))
        start += size
    return pieces


def shared_blocks(vectors):
    parts = lax.axis_size("dp") * lax.axis_size("tensor")
    stacked = jnp.stack(vectors)
    return stacked.reshape(len(vectors), lax.axis_size("dp"), lax.axis_size("tensor"), -1).transpose(
        1, 2, 0, 3
    )


def on_device(
    layer_input,
    segments,
    query_weight,
    query_bias,
    key_weight,
    value_weight,
    value_bias,
    output_weight,
    output_bias,
    first_gain,
    first_shift,
    up_weight,
    up_bias,
    down_weight,
    down_bias,
    second_gain,
    second_shift,
    output_grad,
):
    part_count = lax.axis_size("tensor")
    part_id = lax.axis_index("tensor")
    row_len = segments.shape[1]

    input_rows = lax.dynamic_slice_in_dim(layer_input, part_id * row_len, row_len, 0)
    segment_row = lax.dynamic_index_in_dim(segments, part_id, 0, keepdims=False)
    grad_out = lax.dynamic_slice_in_dim(output_grad, part_id * row_len, row_len, 0).astype(
        jnp.float32
    )

    q_sh, k_sh, v_sh, o_sh = gather_shards(
        [query_weight, key_weight], [value_weight, output_weight]
    )
    u_sh, d_sh = gather_shards([up_weight], [down_weight])
    bias_sh = lax.all_gather(
        jnp.concatenate([query_bias, value_bias, up_bias]), "tensor", axis=0, tiled=False
    )
    qw = join_columns(q_sh)
    kw = join_columns(k_sh)
    vw = join_columns(v_sh)
    ow = join_rows(o_sh)
    uw = join_columns(u_sh)
    dw = join_rows(d_sh)
    head_width = query_bias.shape[0]
    qb = bias_sh[:, :head_width].reshape(-1)
    vb = bias_sh[:, head_width : 2 * head_width].reshape(-1)
    ub = bias_sh[:, 2 * head_width :].reshape(-1)

    input_f32 = input_rows.astype(jnp.float32)
    queries = (product(input_rows, qw) + qb).astype(jnp.bfloat16)
    key_side = product(input_rows, kw).astype(jnp.bfloat16)
    value_proj = (product(input_rows, vw) + vb).astype(jnp.bfloat16)
    context, log_total = attend(queries, key_side, value_proj, segment_row)

    group_width = ow.shape[0] // part_count
    attn_total = input_f32
    for member in range(part_count):
        cols = slice(member * group_width, (member + 1) * group_width)
        attn_total = attn_total + product(context[:, cols], ow[cols]).astype(
            jnp.bfloat16
        ).astype(jnp.float32)
    first_in = attn_total + output_bias
    first_out, first_unit, first_inv = normalize(first_in, first_gain, first_shift)
    first_low = first_out.astype(jnp.bfloat16)
    pre_act = product(first_low, uw) + ub
    gelu_out, pull_gelu = jax.vjp(gelu_tanh, pre_act)
    hidden_low = gelu_out.astype(jnp.bfloat16)
    unit_width = dw.shape[0] // part_count
    second_in = first_out
    for member in range(part_count):
        units = slice(member * unit_width, (member + 1) * unit_width)
        second_in = second_in + product(hidden_low[:, units], dw[units]).astype(
            jnp.bfloat16
        ).astype(jnp.float32)
    second_in = second_in + down_bias
    second_out, second_unit, second_inv = normalize(second_in, second_gain, second_shift)
    layer_output = second_out.astype(jnp.bfloat16)

    grad_second = normalize_back(grad_out, second_unit, second_inv, second_gain)
    grad_second_gain = jnp.sum(grad_out * second_unit, 0)
    grad_second_shift = jnp.sum(grad_out, 0)
    grad_down_bias = jnp.sum(grad_second, 0)
    down_low = grad_second.astype(jnp.bfloat16)
    grad_hidden = contract_last(down_low, dw)
    grad_pre = pull_gelu(grad_hidden)[0].astype(jnp.bfloat16)
    grad_up_bias = jnp.sum(grad_pre, 0, dtype=jnp.float32)
    ffn_blocks = [
        blocked_grad(first_low, grad_pre, "dp", "tensor"),
        blocked_grad(hidden_low, down_low, "tensor", "dp"),
    ]
    first_grad = contract_last(grad_pre, uw) + grad_second
    grad_first_gain = jnp.sum(first_grad * first_unit, 0)
    grad_first_shift = jnp.sum(first_grad, 0)
    attn_grad = normalize_back(first_grad, first_unit, first_inv, first_gain)
    grad_output_bias = jnp.sum(attn_grad, 0)
    attn_grad_low = attn_grad.astype(jnp.bfloat16)
    grad_context = contract_last(attn_grad_low, ow).astype(jnp.bfloat16)
    ffn_blocks.append(blocked_grad(context, attn_grad_low, "tensor", "dp"))
    ffn_joined, grad_context = lax.optimization_barrier((join_grads(ffn_blocks), grad_context))
    ffn_summed = scatter_grads(ffn_joined, ffn_blocks)
    query_low, key_low, value_low = attend_back(
        queries, key_side, value_proj, segment_row, log_total, grad_context
    )
    ffn_summed, query_low, key_low, value_low = lax.optimization_barrier(
        (ffn_summed, query_low, key_low, value_low)
    )
    grad_query_bias = jnp.sum(query_low, 0, dtype=jnp.float32)
    grad_value_bias = jnp.sum(value_low, 0, dtype=jnp.float32)
    attn_blocks = [
        blocked_grad(input_rows, query_low, "dp", "tensor"),
        blocked_grad(input_rows, key_low, "dp", "tensor"),
        blocked_grad(input_rows, value_low, "dp", "tensor"),
    ]
    attn_summed = scatter_grads(join_grads(attn_blocks), attn_blocks)
    input_grad = (
        attn_grad
        + contract_last(query_low, qw)
        + contract_last(key_low, kw)
        + contract_last(value_low, vw)
    )
    small = lax.psum(
        jnp.concatenate(
            [
                grad_query_bias,
                grad_value_bias,
                grad_up_bias,
                grad_output_bias,
                grad_first_gain,
                grad_first_shift,
                grad_down_bias,
                grad_second_gain,
                grad_second_shift,
            ]
        ),
        ("dp", "tensor"),
    )
    split_width = 2 * head_width * part_count + up_bias.shape[0] * part_count
    split = small[:split_width]
    shared = small[split_width:].reshape(6, -1)
    device_id = lax.axis_index("dp") * part_count + part_id
    piece = shared.shape[1] // (lax.axis_size("dp") * part_count)
    shared = lax.dynamic_slice_in_dim(shared, device_id * piece, piece, 1)

    def own_block(vector, offset, width):
        return lax.dynamic_slice_in_dim(vector, offset + part_id * width, width, 0)

    query_bias_grad = own_block(split, 0, head_width)
    value_bias_grad = own_block(split, head_width * part_count, head_width)
    up_bias_grad = own_block(split, 2 * head_width * part_count, up_bias.shape[0])
    return (
        layer_output,
        input_grad,
        attn_summed[0],
        query_bias_grad,
        attn_summed[1],
        attn_summed[2],
        value_bias_grad,
        ffn_summed[2],
        shared[0],
        shared[1],
        shared[2],
        ffn_summed[0],
        up_bias_grad,
        ffn_summed[1],
        shared[3],
        shared[4],
        shared[5],
    )


def solution(mesh):
    in_specs = (
        P("dp", None),
        P("dp", None),
        P(None, "tensor"),
        P("tensor"),
        P(None, "tensor"),
        P(None, "tensor"),
        P("tensor"),
        P("tensor", None),
        P(),
        P(),
        P(),
        P(None, "tensor"),
        P("tensor"),
        P("tensor", None),
        P(),
        P(),
        P(),
        P("dp", None),
    )
    out_specs = (
        P(("dp", "tensor"), None),
        P(("dp", "tensor"), None),
        P("dp", "tensor"),
        P("tensor"),
        P("dp", "tensor"),
        P("dp", "tensor"),
        P("tensor"),
        P("tensor", "dp"),
        P(("dp", "tensor")),
        P(("dp", "tensor")),
        P(("dp", "tensor")),
        P("dp", "tensor"),
        P("tensor"),
        P("tensor", "dp"),
        P(("dp", "tensor")),
        P(("dp", "tensor")),
        P(("dp", "tensor")),
    )
    return jax.shard_map(
        on_device, mesh=mesh, in_specs=in_specs, out_specs=out_specs, check_vma=False
    )
```

```python
import jax
import jax.numpy as jnp
from jax import lax
from jax.sharding import PartitionSpec as P

HEAD_DIM = 64
GROUP_HEADS = 3

norm_eps = 1e-06


def product(left_side, right_side):
    return jnp.dot(left_side, right_side, preferred_element_type=jnp.float32)


def contract_rows(left_side, right_side):
    return lax.dot_general(
        left_side, right_side, (((0,), (0,)), ((), ())), preferred_element_type=jnp.float32
    )


def contract_last(left_side, right_side):
    return lax.dot_general(
        left_side, right_side, (((1,), (1,)), ((), ())), preferred_element_type=jnp.float32
    )


def normalize(summed, norm_gain, offset):
    centred = summed - jnp.mean(summed, -1, keepdims=True)
    inverse = lax.rsqrt(jnp.mean(centred * centred, -1, keepdims=True) + norm_eps)
    scaled = centred * inverse
    return (scaled * norm_gain + offset, scaled, inverse)


def normalize_back(grad_out, scaled, inverse, norm_gain):
    grad_scaled = grad_out * norm_gain
    mean_grad = jnp.mean(grad_scaled, -1, keepdims=True)
    mean_cross = jnp.mean(grad_scaled * scaled, -1, keepdims=True)
    return inverse * (grad_scaled - mean_grad - scaled * mean_cross)


def gelu_tanh(pre_act):
    return jax.nn.gelu(pre_act, approximate=True)


def score_group(query_group, key_group, segment_row):
    scores = jnp.einsum(
        "qhd,khd->hqk", query_group, key_group, preferred_element_type=jnp.float32
    ) * HEAD_DIM ** (-0.5)
    linked = segment_row[:, None] == segment_row[None, :]
    return jnp.where(linked[None], scores, -1e30)


def split_groups(rows_by_width):
    length, width = rows_by_width.shape
    groups = width // (GROUP_HEADS * HEAD_DIM)
    return rows_by_width.reshape(length, groups, GROUP_HEADS, HEAD_DIM).transpose(1, 0, 2, 3)


def join_groups(grouped):
    groups, length, heads, dim = grouped.shape
    return grouped.transpose(1, 0, 2, 3).reshape(length, groups * heads * dim)


def attend(queries, key_side, value_proj, segment_row):
    def one_group(inputs):
        query_group, key_group, value_group = inputs
        scores = score_group(query_group, key_group, segment_row)
        row_max = jnp.max(scores, -1, keepdims=True)
        exp_scores = jnp.exp(scores - row_max)
        row_total = jnp.sum(exp_scores, -1, keepdims=True)
        prob_low = (exp_scores / row_total).astype(jnp.bfloat16)
        context = jnp.einsum(
            "hqk,khd->qhd", prob_low, value_group, preferred_element_type=jnp.float32
        )
        return (context.astype(jnp.bfloat16), (row_max + jnp.log(row_total))[..., 0])

    context, log_total = lax.map(
        one_group, (split_groups(queries), split_groups(key_side), split_groups(value_proj))
    )
    return (join_groups(context), log_total)


def attend_back(queries, key_side, value_proj, segment_row, log_total, grad_context):
    def one_group(inputs):
        query_group, key_group, value_group, log_group, grad_group = inputs
        scores = score_group(query_group, key_group, segment_row)
        probs_full = jnp.exp(scores - log_group[..., None])
        grad_probs = jnp.einsum(
            "qhd,khd->hqk", grad_group, value_group, preferred_element_type=jnp.float32
        )
        inner_sum = jnp.sum(probs_full * grad_probs, -1, keepdims=True)
        grad_scores = (probs_full * (grad_probs - inner_sum)).astype(jnp.bfloat16)
        grad_query = jnp.einsum(
            "hqk,khd->qhd", grad_scores, key_group, preferred_element_type=jnp.float32
        ) * HEAD_DIM ** (-0.5)
        grad_key = jnp.einsum(
            "hqk,qhd->khd", grad_scores, query_group, preferred_element_type=jnp.float32
        ) * HEAD_DIM ** (-0.5)
        grad_value = jnp.einsum(
            "hqk,qhd->khd",
            probs_full.astype(jnp.bfloat16),
            grad_group,
            preferred_element_type=jnp.float32,
        )
        return (
            grad_query.astype(jnp.bfloat16),
            grad_key.astype(jnp.bfloat16),
            grad_value.astype(jnp.bfloat16),
        )

    grad_query, grad_key, grad_value = lax.map(
        one_group,
        (
            split_groups(queries),
            split_groups(key_side),
            split_groups(value_proj),
            log_total,
            split_groups(grad_context),
        ),
    )
    return (join_groups(grad_query), join_groups(grad_key), join_groups(grad_value))


def gather_shards(first_pieces, second_pieces):
    dp_count = lax.axis_size("dp")
    core = lax.rem(lax.axis_index("dp"), 2)

    def flat(pieces):
        return jnp.concatenate([piece.reshape(-1) for piece in pieces]).reshape(-1, 128)

    first, second = flat(first_pieces), flat(second_pieces)
    mine = jnp.where(core == 0, first, second)
    gathered = lax.all_gather(mine, "tensor", axis=0, tiled=False)
    other = lax.ppermute(gathered, "dp", perm=[(i, i ^ 1) for i in range(dp_count)])
    halves = (jnp.where(core == 0, gathered, other), jnp.where(core == 0, other, gathered))
    shards = []
    for half, pieces in zip(halves, (first_pieces, second_pieces)):
        half = half.reshape(half.shape[0], -1)
        start = 0
        for piece in pieces:
            size = piece.size
            shards.append(half[:, start : start + size].reshape((half.shape[0],) + piece.shape))
            start += size
    return shards


def join_columns(shards):
    count, rows, cols = shards.shape
    return shards.transpose(1, 0, 2).reshape(rows, count * cols)


def join_rows(shards):
    count, rows, cols = shards.shape
    return shards.reshape(count * rows, cols)


def blocked_grad(left_side, right_side, row_axis, col_axis):
    row_parts = lax.axis_size(row_axis)
    col_parts = lax.axis_size(col_axis)
    tokens, rows = left_side.shape
    cols = right_side.shape[1]
    left = left_side.reshape(tokens, row_parts, rows // row_parts)
    right = right_side.reshape(tokens, col_parts, cols // col_parts)
    spec = "nai,nbj->abij" if row_axis == "dp" else "nbi,naj->abij"
    return jnp.einsum(spec, left, right, preferred_element_type=jnp.float32)


def join_grads(blocks):
    parts = blocks[0].shape[0] * blocks[0].shape[1]
    joined = jnp.concatenate([block.reshape(parts, -1, 128) for block in blocks], axis=1)
    return joined.reshape(-1, 128).astype(jnp.bfloat16)


def scatter_grads(joined, blocks):
    summed = lax.psum_scatter(joined, ("dp", "tensor"), scatter_dimension=0, tiled=True)
    summed = summed.reshape(-1).astype(jnp.float32)
    pieces = []
    start = 0
    for block in blocks:
        size = block[0, 0].size
        pieces.append(summed[start : start + size].reshape(block.shape[2:]))
        start += size
    return pieces


def shared_blocks(vectors):
    parts = lax.axis_size("dp") * lax.axis_size("tensor")
    stacked = jnp.stack(vectors)
    return stacked.reshape(len(vectors), lax.axis_size("dp"), lax.axis_size("tensor"), -1).transpose(
        1, 2, 0, 3
    )


def on_device(
    layer_input,
    segments,
    query_weight,
    query_bias,
    key_weight,
    value_weight,
    value_bias,
    output_weight,
    output_bias,
    first_gain,
    first_shift,
    up_weight,
    up_bias,
    down_weight,
    down_bias,
    second_gain,
    second_shift,
    output_grad,
):
    part_count = lax.axis_size("tensor")
    part_id = lax.axis_index("tensor")
    row_len = segments.shape[1]

    input_rows = lax.dynamic_slice_in_dim(layer_input, part_id * row_len, row_len, 0)
    segment_row = lax.dynamic_index_in_dim(segments, part_id, 0, keepdims=False)
    grad_out = lax.dynamic_slice_in_dim(output_grad, part_id * row_len, row_len, 0).astype(
        jnp.float32
    )

    q_sh, k_sh, v_sh, o_sh = gather_shards(
        [query_weight, key_weight], [value_weight, output_weight]
    )
    u_sh, d_sh = gather_shards([up_weight], [down_weight])
    bias_sh = lax.all_gather(
        jnp.concatenate([query_bias, value_bias, up_bias]), "tensor", axis=0, tiled=False
    )
    qw = join_columns(q_sh)
    kw = join_columns(k_sh)
    vw = join_columns(v_sh)
    ow = join_rows(o_sh)
    uw = join_columns(u_sh)
    dw = join_rows(d_sh)
    head_width = query_bias.shape[0]
    qb = bias_sh[:, :head_width].reshape(-1)
    vb = bias_sh[:, head_width : 2 * head_width].reshape(-1)
    ub = bias_sh[:, 2 * head_width :].reshape(-1)

    input_f32 = input_rows.astype(jnp.float32)
    queries = (product(input_rows, qw) + qb).astype(jnp.bfloat16)
    key_side = product(input_rows, kw).astype(jnp.bfloat16)
    value_proj = (product(input_rows, vw) + vb).astype(jnp.bfloat16)
    context, log_total = attend(queries, key_side, value_proj, segment_row)

    group_width = ow.shape[0] // part_count
    attn_total = input_f32
    for member in range(part_count):
        cols = slice(member * group_width, (member + 1) * group_width)
        attn_total = attn_total + product(context[:, cols], ow[cols]).astype(
            jnp.bfloat16
        ).astype(jnp.float32)
    first_in = attn_total + output_bias
    first_out, first_unit, first_inv = normalize(first_in, first_gain, first_shift)
    first_low = first_out.astype(jnp.bfloat16)
    pre_act = product(first_low, uw) + ub
    gelu_out, pull_gelu = jax.vjp(gelu_tanh, pre_act)
    hidden_low = gelu_out.astype(jnp.bfloat16)
    unit_width = dw.shape[0] // part_count
    second_in = first_out
    for member in range(part_count):
        units = slice(member * unit_width, (member + 1) * unit_width)
        second_in = second_in + product(hidden_low[:, units], dw[units]).astype(
            jnp.bfloat16
        ).astype(jnp.float32)
    second_in = second_in + down_bias
    second_out, second_unit, second_inv = normalize(second_in, second_gain, second_shift)
    layer_output = second_out.astype(jnp.bfloat16)

    grad_second = normalize_back(grad_out, second_unit, second_inv, second_gain)
    grad_second_gain = jnp.sum(grad_out * second_unit, 0)
    grad_second_shift = jnp.sum(grad_out, 0)
    grad_down_bias = jnp.sum(grad_second, 0)
    down_low = grad_second.astype(jnp.bfloat16)
    grad_hidden = contract_last(down_low, dw)
    grad_pre = pull_gelu(grad_hidden)[0].astype(jnp.bfloat16)
    grad_up_bias = jnp.sum(grad_pre, 0, dtype=jnp.float32)
    ffn_blocks = [
        blocked_grad(first_low, grad_pre, "dp", "tensor"),
        blocked_grad(hidden_low, down_low, "tensor", "dp"),
    ]
    first_grad = contract_last(grad_pre, uw) + grad_second
    grad_first_gain = jnp.sum(first_grad * first_unit, 0)
    grad_first_shift = jnp.sum(first_grad, 0)
    attn_grad = normalize_back(first_grad, first_unit, first_inv, first_gain)
    grad_output_bias = jnp.sum(attn_grad, 0)
    attn_grad_low = attn_grad.astype(jnp.bfloat16)
    grad_context = contract_last(attn_grad_low, ow).astype(jnp.bfloat16)
    ffn_blocks.append(blocked_grad(context, attn_grad_low, "tensor", "dp"))
    ffn_joined, grad_context = lax.optimization_barrier((join_grads(ffn_blocks), grad_context))
    ffn_summed = scatter_grads(ffn_joined, ffn_blocks)
    query_low, key_low, value_low = attend_back(
        queries, key_side, value_proj, segment_row, log_total, grad_context
    )
    ffn_summed, query_low, key_low, value_low = lax.optimization_barrier(
        (ffn_summed, query_low, key_low, value_low)
    )
    grad_query_bias = jnp.sum(query_low, 0, dtype=jnp.float32)
    grad_value_bias = jnp.sum(value_low, 0, dtype=jnp.float32)
    attn_blocks = [
        blocked_grad(input_rows, query_low, "dp", "tensor"),
        blocked_grad(input_rows, key_low, "dp", "tensor"),
        blocked_grad(input_rows, value_low, "dp", "tensor"),
    ]
    attn_summed = scatter_grads(join_grads(attn_blocks), attn_blocks)
    input_grad = (
        attn_grad
        + contract_last(query_low, qw)
        + contract_last(key_low, kw)
        + contract_last(value_low, vw)
    )
    small = lax.psum(
        jnp.concatenate(
            [
                grad_query_bias,
                grad_value_bias,
                grad_up_bias,
                grad_output_bias,
                grad_first_gain,
                grad_first_shift,
                grad_down_bias,
                grad_second_gain,
                grad_second_shift,
            ]
        ),
        ("dp", "tensor"),
    )
    split_width = 2 * head_width * part_count + up_bias.shape[0] * part_count
    split = small[:split_width]
    shared = small[split_width:].reshape(6, -1)
    device_id = lax.axis_index("dp") * part_count + part_id
    piece = shared.shape[1] // (lax.axis_size("dp") * part_count)
    shared = lax.dynamic_slice_in_dim(shared, device_id * piece, piece, 1)

    def own_block(vector, offset, width):
        return lax.dynamic_slice_in_dim(vector, offset + part_id * width, width, 0)

    query_bias_grad = own_block(split, 0, head_width)
    value_bias_grad = own_block(split, head_width * part_count, head_width)
    up_bias_grad = own_block(split, 2 * head_width * part_count, up_bias.shape[0])
    return (
        layer_output,
        input_grad,
        attn_summed[0],
        query_bias_grad,
        attn_summed[1],
        attn_summed[2],
        value_bias_grad,
        ffn_summed[2],
        shared[0],
        shared[1],
        shared[2],
        ffn_summed[0],
        up_bias_grad,
        ffn_summed[1],
        shared[3],
        shared[4],
        shared[5],
    )


def solution(mesh):
    in_specs = (
        P("dp", None),
        P("dp", None),
        P(None, "tensor"),
        P("tensor"),
        P(None, "tensor"),
        P(None, "tensor"),
        P("tensor"),
        P("tensor", None),
        P(),
        P(),
        P(),
        P(None, "tensor"),
        P("tensor"),
        P("tensor", None),
        P(),
        P(),
        P(),
        P("dp", None),
    )
    out_specs = (
        P(("dp", "tensor"), None),
        P(("dp", "tensor"), None),
        P("dp", "tensor"),
        P("tensor"),
        P("dp", "tensor"),
        P("dp", "tensor"),
        P("tensor"),
        P("tensor", "dp"),
        P(("dp", "tensor")),
        P(("dp", "tensor")),
        P(("dp", "tensor")),
        P("dp", "tensor"),
        P("tensor"),
        P("tensor", "dp"),
        P(("dp", "tensor")),
        P(("dp", "tensor")),
        P(("dp", "tensor")),
    )
    return jax.shard_map(
        on_device, mesh=mesh, in_specs=in_specs, out_specs=out_specs, check_vma=False
    )
```

```python
import jax
import jax.numpy as jnp
from jax import lax
from jax.sharding import PartitionSpec as P

HEAD_DIM = 64
GROUP_HEADS = 3

norm_eps = 1e-06


def product(left_side, right_side):
    return jnp.dot(left_side, right_side, preferred_element_type=jnp.float32)


def contract_rows(left_side, right_side):
    return lax.dot_general(
        left_side, right_side, (((0,), (0,)), ((), ())), preferred_element_type=jnp.float32
    )


def contract_last(left_side, right_side):
    return lax.dot_general(
        left_side, right_side, (((1,), (1,)), ((), ())), preferred_element_type=jnp.float32
    )


def normalize(summed, norm_gain, offset):
    centred = summed - jnp.mean(summed, -1, keepdims=True)
    inverse = lax.rsqrt(jnp.mean(centred * centred, -1, keepdims=True) + norm_eps)
    scaled = centred * inverse
    return (scaled * norm_gain + offset, scaled, inverse)


def normalize_back(grad_out, scaled, inverse, norm_gain):
    grad_scaled = grad_out * norm_gain
    mean_grad = jnp.mean(grad_scaled, -1, keepdims=True)
    mean_cross = jnp.mean(grad_scaled * scaled, -1, keepdims=True)
    return inverse * (grad_scaled - mean_grad - scaled * mean_cross)


def gelu_tanh(pre_act):
    return jax.nn.gelu(pre_act, approximate=True)


def score_group(query_group, key_group, segment_row):
    scores = jnp.einsum(
        "qhd,khd->hqk", query_group, key_group, preferred_element_type=jnp.float32
    ) * HEAD_DIM ** (-0.5)
    linked = segment_row[:, None] == segment_row[None, :]
    return jnp.where(linked[None], scores, -1e30)


def split_groups(rows_by_width):
    length, width = rows_by_width.shape
    groups = width // (GROUP_HEADS * HEAD_DIM)
    return rows_by_width.reshape(length, groups, GROUP_HEADS, HEAD_DIM).transpose(1, 0, 2, 3)


def join_groups(grouped):
    groups, length, heads, dim = grouped.shape
    return grouped.transpose(1, 0, 2, 3).reshape(length, groups * heads * dim)


def attend(queries, key_side, value_proj, segment_row):
    def one_group(inputs):
        query_group, key_group, value_group = inputs
        scores = score_group(query_group, key_group, segment_row)
        row_max = jnp.max(scores, -1, keepdims=True)
        exp_scores = jnp.exp(scores - row_max)
        row_total = jnp.sum(exp_scores, -1, keepdims=True)
        prob_low = (exp_scores / row_total).astype(jnp.bfloat16)
        context = jnp.einsum(
            "hqk,khd->qhd", prob_low, value_group, preferred_element_type=jnp.float32
        )
        return (context.astype(jnp.bfloat16), (row_max + jnp.log(row_total))[..., 0])

    context, log_total = lax.map(
        one_group, (split_groups(queries), split_groups(key_side), split_groups(value_proj))
    )
    return (join_groups(context), log_total)


def attend_back(queries, key_side, value_proj, segment_row, log_total, grad_context):
    def one_group(inputs):
        query_group, key_group, value_group, log_group, grad_group = inputs
        scores = score_group(query_group, key_group, segment_row)
        probs_full = jnp.exp(scores - log_group[..., None])
        grad_probs = jnp.einsum(
            "qhd,khd->hqk", grad_group, value_group, preferred_element_type=jnp.float32
        )
        inner_sum = jnp.sum(probs_full * grad_probs, -1, keepdims=True)
        grad_scores = (probs_full * (grad_probs - inner_sum)).astype(jnp.bfloat16)
        grad_query = jnp.einsum(
            "hqk,khd->qhd", grad_scores, key_group, preferred_element_type=jnp.float32
        ) * HEAD_DIM ** (-0.5)
        grad_key = jnp.einsum(
            "hqk,qhd->khd", grad_scores, query_group, preferred_element_type=jnp.float32
        ) * HEAD_DIM ** (-0.5)
        grad_value = jnp.einsum(
            "hqk,qhd->khd",
            probs_full.astype(jnp.bfloat16),
            grad_group,
            preferred_element_type=jnp.float32,
        )
        return (
            grad_query.astype(jnp.bfloat16),
            grad_key.astype(jnp.bfloat16),
            grad_value.astype(jnp.bfloat16),
        )

    grad_query, grad_key, grad_value = lax.map(
        one_group,
        (
            split_groups(queries),
            split_groups(key_side),
            split_groups(value_proj),
            log_total,
            split_groups(grad_context),
        ),
    )
    return (join_groups(grad_query), join_groups(grad_key), join_groups(grad_value))


def gather_shards(first_pieces, second_pieces):
    dp_count = lax.axis_size("dp")
    core = lax.rem(lax.axis_index("dp"), 2)

    def flat(pieces):
        return jnp.concatenate([piece.reshape(-1) for piece in pieces]).reshape(-1, 128)

    first, second = flat(first_pieces), flat(second_pieces)
    mine = jnp.where(core == 0, first, second)
    gathered = lax.all_gather(mine, "tensor", axis=0, tiled=False)
    other = lax.ppermute(gathered, "dp", perm=[(i, i ^ 1) for i in range(dp_count)])
    halves = (jnp.where(core == 0, gathered, other), jnp.where(core == 0, other, gathered))
    shards = []
    for half, pieces in zip(halves, (first_pieces, second_pieces)):
        half = half.reshape(half.shape[0], -1)
        start = 0
        for piece in pieces:
            size = piece.size
            shards.append(half[:, start : start + size].reshape((half.shape[0],) + piece.shape))
            start += size
    return shards


def join_columns(shards):
    count, rows, cols = shards.shape
    return shards.transpose(1, 0, 2).reshape(rows, count * cols)


def join_rows(shards):
    count, rows, cols = shards.shape
    return shards.reshape(count * rows, cols)


def scatter_rows(grads):
    joined = jnp.concatenate(grads, axis=2).astype(jnp.bfloat16)
    rows, parts, width = joined.shape
    summed = lax.psum_scatter(joined.reshape(rows, parts * width), "dp", scatter_dimension=0, tiled=True)
    return summed.reshape(-1, parts, width)


def scatter_parts(partials, grads):
    joined = jnp.concatenate(partials, axis=2)
    summed = lax.psum_scatter(joined, "tensor", scatter_dimension=1, tiled=True)[:, 0]
    pieces = []
    start = 0
    for grad in grads:
        width = grad.shape[2]
        pieces.append(summed[:, start : start + width].astype(jnp.float32))
        start += width
    return pieces


def split_tensor(grad):
    rows, cols = grad.shape
    parts = lax.axis_size("tensor")
    return grad.reshape(rows, parts, cols // parts)


def on_device(
    layer_input,
    segments,
    query_weight,
    query_bias,
    key_weight,
    value_weight,
    value_bias,
    output_weight,
    output_bias,
    first_gain,
    first_shift,
    up_weight,
    up_bias,
    down_weight,
    down_bias,
    second_gain,
    second_shift,
    output_grad,
):
    part_count = lax.axis_size("tensor")
    part_id = lax.axis_index("tensor")
    row_len = segments.shape[1]

    input_rows = lax.dynamic_slice_in_dim(layer_input, part_id * row_len, row_len, 0)
    segment_row = lax.dynamic_index_in_dim(segments, part_id, 0, keepdims=False)
    grad_out = lax.dynamic_slice_in_dim(output_grad, part_id * row_len, row_len, 0).astype(
        jnp.float32
    )

    q_sh, k_sh, v_sh, o_sh = gather_shards(
        [query_weight, key_weight], [value_weight, output_weight]
    )
    u_sh, d_sh = gather_shards([up_weight], [down_weight])
    bias_sh = lax.all_gather(
        jnp.concatenate([query_bias, value_bias, up_bias]), "tensor", axis=0, tiled=False
    )
    qw = join_columns(q_sh)
    kw = join_columns(k_sh)
    vw = join_columns(v_sh)
    ow = join_rows(o_sh)
    uw = join_columns(u_sh)
    dw = join_rows(d_sh)
    head_width = query_bias.shape[0]
    qb = bias_sh[:, :head_width].reshape(-1)
    vb = bias_sh[:, head_width : 2 * head_width].reshape(-1)
    ub = bias_sh[:, 2 * head_width :].reshape(-1)

    input_f32 = input_rows.astype(jnp.float32)
    queries = (product(input_rows, qw) + qb).astype(jnp.bfloat16)
    key_side = product(input_rows, kw).astype(jnp.bfloat16)
    value_proj = (product(input_rows, vw) + vb).astype(jnp.bfloat16)
    context, log_total = attend(queries, key_side, value_proj, segment_row)

    group_width = ow.shape[0] // part_count
    attn_total = input_f32
    for member in range(part_count):
        cols = slice(member * group_width, (member + 1) * group_width)
        attn_total = attn_total + product(context[:, cols], ow[cols]).astype(
            jnp.bfloat16
        ).astype(jnp.float32)
    first_in = attn_total + output_bias
    first_out, first_unit, first_inv = normalize(first_in, first_gain, first_shift)
    first_low = first_out.astype(jnp.bfloat16)
    pre_act = product(first_low, uw) + ub
    gelu_out, pull_gelu = jax.vjp(gelu_tanh, pre_act)
    hidden_low = gelu_out.astype(jnp.bfloat16)
    unit_width = dw.shape[0] // part_count
    second_in = first_out
    for member in range(part_count):
        units = slice(member * unit_width, (member + 1) * unit_width)
        second_in = second_in + product(hidden_low[:, units], dw[units]).astype(
            jnp.bfloat16
        ).astype(jnp.float32)
    second_in = second_in + down_bias
    second_out, second_unit, second_inv = normalize(second_in, second_gain, second_shift)
    layer_output = second_out.astype(jnp.bfloat16)

    grad_second = normalize_back(grad_out, second_unit, second_inv, second_gain)
    grad_second_gain = jnp.sum(grad_out * second_unit, 0)
    grad_second_shift = jnp.sum(grad_out, 0)
    grad_down_bias = jnp.sum(grad_second, 0)
    down_low = grad_second.astype(jnp.bfloat16)
    grad_hidden = contract_last(down_low, dw)
    grad_pre = pull_gelu(grad_hidden)[0].astype(jnp.bfloat16)
    grad_up_bias = jnp.sum(grad_pre, 0, dtype=jnp.float32)
    first_grad = contract_last(grad_pre, uw) + grad_second
    grad_first_gain = jnp.sum(first_grad * first_unit, 0)
    grad_first_shift = jnp.sum(first_grad, 0)
    attn_grad = normalize_back(first_grad, first_unit, first_inv, first_gain)
    grad_output_bias = jnp.sum(attn_grad, 0)
    attn_grad_low = attn_grad.astype(jnp.bfloat16)
    grad_context = contract_last(attn_grad_low, ow).astype(jnp.bfloat16)
    ffn_grads = [
        split_tensor(contract_rows(first_low, grad_pre)),
        split_tensor(contract_rows(down_low, hidden_low)),
        split_tensor(contract_rows(attn_grad_low, context)),
    ]
    ffn_grads, grad_context = lax.optimization_barrier((ffn_grads, grad_context))
    ffn_rows = scatter_rows(ffn_grads)
    query_low, key_low, value_low = attend_back(
        queries, key_side, value_proj, segment_row, log_total, grad_context
    )
    ffn_rows, query_low, key_low, value_low = lax.optimization_barrier(
        (ffn_rows, query_low, key_low, value_low)
    )
    grad_query_bias = jnp.sum(query_low, 0, dtype=jnp.float32)
    grad_value_bias = jnp.sum(value_low, 0, dtype=jnp.float32)
    qkv_low = jnp.stack([query_low, key_low, value_low], axis=1)
    qkv_grads = lax.dot_general(
        input_rows, qkv_low, (((0,), (0,)), ((), ())), preferred_element_type=jnp.float32
    )
    qkv_grads = qkv_grads.reshape(qkv_grads.shape[0], 3, part_count, -1).transpose(0, 2, 1, 3)
    qkv_grads = qkv_grads.reshape(qkv_grads.shape[0], part_count, -1)
    summed = scatter_parts([ffn_rows, scatter_rows([qkv_grads])], ffn_grads + [qkv_grads])
    ffn_summed = summed[:3]
    attn_summed = summed[3].reshape(summed[3].shape[0], 3, -1)
    input_grad = (
        attn_grad
        + contract_last(query_low, qw)
        + contract_last(key_low, kw)
        + contract_last(value_low, vw)
    )
    small = lax.psum(
        jnp.concatenate(
            [
                grad_query_bias,
                grad_value_bias,
                grad_up_bias,
                grad_output_bias,
                grad_first_gain,
                grad_first_shift,
                grad_down_bias,
                grad_second_gain,
                grad_second_shift,
            ]
        ),
        ("dp", "tensor"),
    )
    split_width = 2 * head_width * part_count + up_bias.shape[0] * part_count
    split = small[:split_width]
    shared = small[split_width:].reshape(6, -1)
    device_id = lax.axis_index("dp") * part_count + part_id
    piece = shared.shape[1] // (lax.axis_size("dp") * part_count)
    shared = lax.dynamic_slice_in_dim(shared, device_id * piece, piece, 1)

    def own_block(vector, offset, width):
        return lax.dynamic_slice_in_dim(vector, offset + part_id * width, width, 0)

    query_bias_grad = own_block(split, 0, head_width)
    value_bias_grad = own_block(split, head_width * part_count, head_width)
    up_bias_grad = own_block(split, 2 * head_width * part_count, up_bias.shape[0])
    return (
        layer_output,
        input_grad,
        attn_summed[:, 0],
        query_bias_grad,
        attn_summed[:, 1],
        attn_summed[:, 2],
        value_bias_grad,
        ffn_summed[2].T,
        shared[0],
        shared[1],
        shared[2],
        ffn_summed[0],
        up_bias_grad,
        ffn_summed[1].T,
        shared[3],
        shared[4],
        shared[5],
    )


def solution(mesh):
    in_specs = (
        P("dp", None),
        P("dp", None),
        P(None, "tensor"),
        P("tensor"),
        P(None, "tensor"),
        P(None, "tensor"),
        P("tensor"),
        P("tensor", None),
        P(),
        P(),
        P(),
        P(None, "tensor"),
        P("tensor"),
        P("tensor", None),
        P(),
        P(),
        P(),
        P("dp", None),
    )
    out_specs = (
        P(("dp", "tensor"), None),
        P(("dp", "tensor"), None),
        P("dp", "tensor"),
        P("tensor"),
        P("dp", "tensor"),
        P("dp", "tensor"),
        P("tensor"),
        P("tensor", "dp"),
        P(("dp", "tensor")),
        P(("dp", "tensor")),
        P(("dp", "tensor")),
        P("dp", "tensor"),
        P("tensor"),
        P("tensor", "dp"),
        P(("dp", "tensor")),
        P(("dp", "tensor")),
        P(("dp", "tensor")),
    )
    return jax.shard_map(
        on_device, mesh=mesh, in_specs=in_specs, out_specs=out_specs, check_vma=False
    )
```

```python
import jax
import jax.numpy as jnp
from jax import lax
from jax.sharding import PartitionSpec as P

HEAD_DIM = 64
GROUP_HEADS = 3

norm_eps = 1e-06


def product(left_side, right_side):
    return jnp.dot(left_side, right_side, preferred_element_type=jnp.float32)


def contract_rows(left_side, right_side):
    return lax.dot_general(
        left_side, right_side, (((0,), (0,)), ((), ())), preferred_element_type=jnp.float32
    )


def contract_last(left_side, right_side):
    return lax.dot_general(
        left_side, right_side, (((1,), (1,)), ((), ())), preferred_element_type=jnp.float32
    )


def normalize(summed, norm_gain, offset):
    centred = summed - jnp.mean(summed, -1, keepdims=True)
    inverse = lax.rsqrt(jnp.mean(centred * centred, -1, keepdims=True) + norm_eps)
    scaled = centred * inverse
    return (scaled * norm_gain + offset, scaled, inverse)


def normalize_back(grad_out, scaled, inverse, norm_gain):
    grad_scaled = grad_out * norm_gain
    mean_grad = jnp.mean(grad_scaled, -1, keepdims=True)
    mean_cross = jnp.mean(grad_scaled * scaled, -1, keepdims=True)
    return inverse * (grad_scaled - mean_grad - scaled * mean_cross)


def gelu_tanh(pre_act):
    return jax.nn.gelu(pre_act, approximate=True)


def score_group(query_group, key_group, segment_row):
    scores = jnp.einsum(
        "qhd,khd->hqk", query_group, key_group, preferred_element_type=jnp.float32
    ) * HEAD_DIM ** (-0.5)
    linked = segment_row[:, None] == segment_row[None, :]
    return jnp.where(linked[None], scores, -1e30)


def split_groups(rows_by_width):
    length, width = rows_by_width.shape
    groups = width // (GROUP_HEADS * HEAD_DIM)
    return rows_by_width.reshape(length, groups, GROUP_HEADS, HEAD_DIM).transpose(1, 0, 2, 3)


def join_groups(grouped):
    groups, length, heads, dim = grouped.shape
    return grouped.transpose(1, 0, 2, 3).reshape(length, groups * heads * dim)


def attend(queries, key_side, value_proj, segment_row):
    def one_group(inputs):
        query_group, key_group, value_group = inputs
        scores = score_group(query_group, key_group, segment_row)
        row_max = jnp.max(scores, -1, keepdims=True)
        exp_scores = jnp.exp(scores - row_max)
        row_total = jnp.sum(exp_scores, -1, keepdims=True)
        prob_low = (exp_scores / row_total).astype(jnp.bfloat16)
        context = jnp.einsum(
            "hqk,khd->qhd", prob_low, value_group, preferred_element_type=jnp.float32
        )
        return (context.astype(jnp.bfloat16), (row_max + jnp.log(row_total))[..., 0])

    context, log_total = lax.map(
        one_group, (split_groups(queries), split_groups(key_side), split_groups(value_proj))
    )
    return (join_groups(context), log_total)


def attend_back(queries, key_side, value_proj, segment_row, log_total, grad_context):
    def one_group(inputs):
        query_group, key_group, value_group, log_group, grad_group = inputs
        scores = score_group(query_group, key_group, segment_row)
        probs_full = jnp.exp(scores - log_group[..., None])
        grad_probs = jnp.einsum(
            "qhd,khd->hqk", grad_group, value_group, preferred_element_type=jnp.float32
        )
        inner_sum = jnp.sum(probs_full * grad_probs, -1, keepdims=True)
        grad_scores = (probs_full * (grad_probs - inner_sum)).astype(jnp.bfloat16)
        grad_query = jnp.einsum(
            "hqk,khd->qhd", grad_scores, key_group, preferred_element_type=jnp.float32
        ) * HEAD_DIM ** (-0.5)
        grad_key = jnp.einsum(
            "hqk,qhd->khd", grad_scores, query_group, preferred_element_type=jnp.float32
        ) * HEAD_DIM ** (-0.5)
        grad_value = jnp.einsum(
            "hqk,qhd->khd",
            probs_full.astype(jnp.bfloat16),
            grad_group,
            preferred_element_type=jnp.float32,
        )
        return (
            grad_query.astype(jnp.bfloat16),
            grad_key.astype(jnp.bfloat16),
            grad_value.astype(jnp.bfloat16),
        )

    grad_query, grad_key, grad_value = lax.map(
        one_group,
        (
            split_groups(queries),
            split_groups(key_side),
            split_groups(value_proj),
            log_total,
            split_groups(grad_context),
        ),
    )
    return (join_groups(grad_query), join_groups(grad_key), join_groups(grad_value))


def gather_shards(first_pieces, second_pieces):
    dp_count = lax.axis_size("dp")
    core = lax.rem(lax.axis_index("dp"), 2)
    first, second = jnp.stack(first_pieces), jnp.stack(second_pieces)
    mine = jnp.where(core == 0, first, second)
    gathered = lax.all_gather(mine, "tensor", axis=0, tiled=False)
    other = lax.ppermute(gathered, "dp", perm=[(i, i ^ 1) for i in range(dp_count)])
    halves = (jnp.where(core == 0, gathered, other), jnp.where(core == 0, other, gathered))
    return [half[:, index] for half in halves for index in range(half.shape[1])]


def by_parts(grads):
    parts = lax.axis_size("tensor")
    columns = []
    for part in range(parts):
        used = 0
        for grad in grads:
            width = grad.shape[1] // parts
            columns.append(grad[:, part * width : (part + 1) * width].astype(jnp.bfloat16))
            used += width
        if used % 128:
            columns.append(jnp.zeros((grads[0].shape[0], 128 - used % 128), jnp.bfloat16))
    return jnp.concatenate(columns, axis=1)


def scatter_rows(joined):
    return lax.psum_scatter(joined, "dp", scatter_dimension=0, tiled=True)


def scatter_parts(partials, widths):
    parts = lax.axis_size("tensor")
    joined = jnp.concatenate(
        [partial.reshape(partial.shape[0], parts, -1) for partial in partials], axis=2
    )
    summed = lax.psum_scatter(joined, "tensor", scatter_dimension=1, tiled=True)[:, 0]
    pieces = []
    start = 0
    for partial, group in zip(partials, widths):
        for width in group:
            pieces.append(summed[:, start : start + width].astype(jnp.float32))
            start += width
        start += partial.shape[1] // parts - sum(group)
    return pieces


def on_device(
    layer_input,
    segments,
    query_weight,
    query_bias,
    key_weight,
    value_weight,
    value_bias,
    output_weight,
    output_bias,
    first_gain,
    first_shift,
    up_weight,
    up_bias,
    down_weight,
    down_bias,
    second_gain,
    second_shift,
    output_grad,
):
    part_count = lax.axis_size("tensor")
    part_id = lax.axis_index("tensor")
    row_len = segments.shape[1]

    input_rows = lax.dynamic_slice_in_dim(layer_input, part_id * row_len, row_len, 0)
    segment_row = lax.dynamic_index_in_dim(segments, part_id, 0, keepdims=False)
    grad_out = lax.dynamic_slice_in_dim(output_grad, part_id * row_len, row_len, 0).astype(
        jnp.float32
    )

    qt_sh, kt_sh, vt_sh, o_sh = gather_shards(
        [query_weight.T, key_weight.T], [value_weight.T, output_weight]
    )
    u_sh, d_sh = gather_shards([up_weight], [down_weight])
    bias_sh = lax.all_gather(
        jnp.concatenate([query_bias, value_bias, up_bias]), "tensor", axis=0, tiled=False
    )
    head_width = query_bias.shape[0]
    qb = bias_sh[:, :head_width].reshape(-1)
    vb = bias_sh[:, head_width : 2 * head_width].reshape(-1)
    ub = bias_sh[:, 2 * head_width :]
    width = qt_sh.shape[2]
    qt_full = qt_sh.reshape(-1, width)
    kt_full = kt_sh.reshape(-1, width)
    vt_full = vt_sh.reshape(-1, width)

    input_f32 = input_rows.astype(jnp.float32)
    queries = (contract_last(input_rows, qt_full) + qb).astype(jnp.bfloat16)
    key_side = contract_last(input_rows, kt_full).astype(jnp.bfloat16)
    value_proj = (contract_last(input_rows, vt_full) + vb).astype(jnp.bfloat16)
    context, log_total = attend(queries, key_side, value_proj, segment_row)

    group_width = o_sh.shape[1]
    attn_total = input_f32
    for member in range(part_count):
        cols = slice(member * group_width, (member + 1) * group_width)
        attn_total = attn_total + product(context[:, cols], o_sh[member]).astype(
            jnp.bfloat16
        ).astype(jnp.float32)
    first_in = attn_total + output_bias
    first_out, first_unit, first_inv = normalize(first_in, first_gain, first_shift)
    first_low = first_out.astype(jnp.bfloat16)
    second_in = first_out
    pulls = []
    hidden_parts = []
    for member in range(part_count):
        pre_part = product(first_low, u_sh[member]) + ub[member]
        gelu_out, pull_gelu = jax.vjp(gelu_tanh, pre_part)
        pulls.append(pull_gelu)
        hidden_part = gelu_out.astype(jnp.bfloat16)
        hidden_parts.append(hidden_part)
        second_in = second_in + product(hidden_part, d_sh[member]).astype(
            jnp.bfloat16
        ).astype(jnp.float32)
    second_in = second_in + down_bias
    second_out, second_unit, second_inv = normalize(second_in, second_gain, second_shift)
    layer_output = second_out.astype(jnp.bfloat16)

    grad_second = normalize_back(grad_out, second_unit, second_inv, second_gain)
    grad_second_gain = jnp.sum(grad_out * second_unit, 0)
    grad_second_shift = jnp.sum(grad_out, 0)
    grad_down_bias = jnp.sum(grad_second, 0)
    down_low = grad_second.astype(jnp.bfloat16)
    first_grad = grad_second
    grad_pre_parts = []
    for member in range(part_count):
        grad_hidden = contract_last(down_low, d_sh[member])
        grad_pre = pulls[member](grad_hidden)[0].astype(jnp.bfloat16)
        grad_pre_parts.append(grad_pre)
        first_grad = first_grad + contract_last(grad_pre, u_sh[member])
    grad_pre = jnp.concatenate(grad_pre_parts, axis=1)
    hidden_low = jnp.concatenate(hidden_parts, axis=1)
    grad_up_bias = jnp.sum(grad_pre, 0, dtype=jnp.float32)
    grad_first_gain = jnp.sum(first_grad * first_unit, 0)
    grad_first_shift = jnp.sum(first_grad, 0)
    attn_grad = normalize_back(first_grad, first_unit, first_inv, first_gain)
    grad_output_bias = jnp.sum(attn_grad, 0)
    attn_grad_low = attn_grad.astype(jnp.bfloat16)
    grad_context = contract_last(attn_grad_low, o_sh.reshape(-1, o_sh.shape[2])).astype(
        jnp.bfloat16
    )
    ffn_grads = [
        contract_rows(first_low, grad_pre),
        contract_rows(down_low, hidden_low),
        contract_rows(attn_grad_low, context),
    ]
    ffn_widths = [grad.shape[1] // part_count for grad in ffn_grads]
    ffn_joined, grad_context = lax.optimization_barrier((by_parts(ffn_grads), grad_context))
    ffn_rows = scatter_rows(ffn_joined)
    query_low, key_low, value_low = attend_back(
        queries, key_side, value_proj, segment_row, log_total, grad_context
    )
    ffn_rows, query_low, key_low, value_low = lax.optimization_barrier(
        (ffn_rows, query_low, key_low, value_low)
    )
    grad_query_bias = jnp.sum(query_low, 0, dtype=jnp.float32)
    grad_value_bias = jnp.sum(value_low, 0, dtype=jnp.float32)
    qkv_low = jnp.stack([query_low, key_low, value_low], axis=1)
    qkv_low = qkv_low.reshape(row_len, 3, part_count, -1).transpose(0, 2, 1, 3)
    qkv_grads = contract_rows(input_rows, qkv_low.reshape(row_len, -1)).astype(jnp.bfloat16)
    qkv_widths = [qkv_grads.shape[1] // part_count]
    summed = scatter_parts(
        [ffn_rows, scatter_rows(qkv_grads)], [ffn_widths, qkv_widths]
    )
    ffn_summed = summed[:3]
    attn_summed = summed[3].reshape(summed[3].shape[0], 3, -1)
    input_grad = (
        attn_grad
        + product(query_low, qt_full)
        + product(key_low, kt_full)
        + product(value_low, vt_full)
    )
    small = lax.psum(
        jnp.concatenate(
            [
                grad_query_bias,
                grad_value_bias,
                grad_up_bias,
                grad_output_bias,
                grad_first_gain,
                grad_first_shift,
                grad_down_bias,
                grad_second_gain,
                grad_second_shift,
            ]
        ),
        ("dp", "tensor"),
    )
    split_width = 2 * head_width * part_count + up_bias.shape[0] * part_count
    split = small[:split_width]
    shared = small[split_width:].reshape(6, -1)
    device_id = lax.axis_index("dp") * part_count + part_id
    piece = shared.shape[1] // (lax.axis_size("dp") * part_count)
    shared = lax.dynamic_slice_in_dim(shared, device_id * piece, piece, 1)

    def own_block(vector, offset, width):
        return lax.dynamic_slice_in_dim(vector, offset + part_id * width, width, 0)

    query_bias_grad = own_block(split, 0, head_width)
    value_bias_grad = own_block(split, head_width * part_count, head_width)
    up_bias_grad = own_block(split, 2 * head_width * part_count, up_bias.shape[0])
    return (
        layer_output,
        input_grad,
        attn_summed[:, 0],
        query_bias_grad,
        attn_summed[:, 1],
        attn_summed[:, 2],
        value_bias_grad,
        ffn_summed[2].T,
        shared[0],
        shared[1],
        shared[2],
        ffn_summed[0],
        up_bias_grad,
        ffn_summed[1].T,
        shared[3],
        shared[4],
        shared[5],
    )


def solution(mesh):
    in_specs = (
        P("dp", None),
        P("dp", None),
        P(None, "tensor"),
        P("tensor"),
        P(None, "tensor"),
        P(None, "tensor"),
        P("tensor"),
        P("tensor", None),
        P(),
        P(),
        P(),
        P(None, "tensor"),
        P("tensor"),
        P("tensor", None),
        P(),
        P(),
        P(),
        P("dp", None),
    )
    out_specs = (
        P(("dp", "tensor"), None),
        P(("dp", "tensor"), None),
        P("dp", "tensor"),
        P("tensor"),
        P("dp", "tensor"),
        P("dp", "tensor"),
        P("tensor"),
        P("tensor", "dp"),
        P(("dp", "tensor")),
        P(("dp", "tensor")),
        P(("dp", "tensor")),
        P("dp", "tensor"),
        P("tensor"),
        P("tensor", "dp"),
        P(("dp", "tensor")),
        P(("dp", "tensor")),
        P(("dp", "tensor")),
    )
    return jax.shard_map(
        on_device, mesh=mesh, in_specs=in_specs, out_specs=out_specs, check_vma=False
    )
```

```python
import jax
import jax.numpy as jnp
from jax import lax
from jax.sharding import PartitionSpec as P

HEAD_DIM = 64
GROUP_HEADS = 3

norm_eps = 1e-06


def product(left_side, right_side):
    return jnp.dot(left_side, right_side, preferred_element_type=jnp.float32)


def contract_rows(left_side, right_side):
    return lax.dot_general(
        left_side, right_side, (((0,), (0,)), ((), ())), preferred_element_type=jnp.float32
    )


def contract_last(left_side, right_side):
    return lax.dot_general(
        left_side, right_side, (((1,), (1,)), ((), ())), preferred_element_type=jnp.float32
    )


def normalize(summed, norm_gain, offset):
    centred = summed - jnp.mean(summed, -1, keepdims=True)
    inverse = lax.rsqrt(jnp.mean(centred * centred, -1, keepdims=True) + norm_eps)
    scaled = centred * inverse
    return (scaled * norm_gain + offset, scaled, inverse)


def normalize_back(grad_out, scaled, inverse, norm_gain):
    grad_scaled = grad_out * norm_gain
    mean_grad = jnp.mean(grad_scaled, -1, keepdims=True)
    mean_cross = jnp.mean(grad_scaled * scaled, -1, keepdims=True)
    return inverse * (grad_scaled - mean_grad - scaled * mean_cross)


def gelu_tanh(pre_act):
    return jax.nn.gelu(pre_act, approximate=True)


def score_group(query_group, key_group, segment_row):
    scores = jnp.einsum(
        "qhd,khd->hqk", query_group, key_group, preferred_element_type=jnp.float32
    ) * HEAD_DIM ** (-0.5)
    linked = segment_row[:, None] == segment_row[None, :]
    return jnp.where(linked[None], scores, -1e30)


def split_groups(rows_by_width):
    length, width = rows_by_width.shape
    groups = width // (GROUP_HEADS * HEAD_DIM)
    return rows_by_width.reshape(length, groups, GROUP_HEADS, HEAD_DIM).transpose(1, 0, 2, 3)


def join_groups(grouped):
    groups, length, heads, dim = grouped.shape
    return grouped.transpose(1, 0, 2, 3).reshape(length, groups * heads * dim)


def attend(queries, key_side, value_proj, segment_row):
    def one_group(inputs):
        query_group, key_group, value_group = inputs
        scores = score_group(query_group, key_group, segment_row)
        row_max = jnp.max(scores, -1, keepdims=True)
        exp_scores = jnp.exp(scores - row_max)
        row_total = jnp.sum(exp_scores, -1, keepdims=True)
        prob_low = (exp_scores / row_total).astype(jnp.bfloat16)
        context = jnp.einsum(
            "hqk,khd->qhd", prob_low, value_group, preferred_element_type=jnp.float32
        )
        return (context.astype(jnp.bfloat16), (row_max + jnp.log(row_total))[..., 0])

    context, log_total = lax.map(
        one_group, (split_groups(queries), split_groups(key_side), split_groups(value_proj))
    )
    return (join_groups(context), log_total)


def attend_back(queries, key_side, value_proj, segment_row, log_total, grad_context):
    def one_group(inputs):
        query_group, key_group, value_group, log_group, grad_group = inputs
        scores = score_group(query_group, key_group, segment_row)
        probs_full = jnp.exp(scores - log_group[..., None])
        grad_probs = jnp.einsum(
            "qhd,khd->hqk", grad_group, value_group, preferred_element_type=jnp.float32
        )
        inner_sum = jnp.sum(probs_full * grad_probs, -1, keepdims=True)
        grad_scores = (probs_full * (grad_probs - inner_sum)).astype(jnp.bfloat16)
        grad_query = jnp.einsum(
            "hqk,khd->qhd", grad_scores, key_group, preferred_element_type=jnp.float32
        ) * HEAD_DIM ** (-0.5)
        grad_key = jnp.einsum(
            "hqk,qhd->khd", grad_scores, query_group, preferred_element_type=jnp.float32
        ) * HEAD_DIM ** (-0.5)
        grad_value = jnp.einsum(
            "hqk,qhd->khd",
            probs_full.astype(jnp.bfloat16),
            grad_group,
            preferred_element_type=jnp.float32,
        )
        return (
            grad_query.astype(jnp.bfloat16),
            grad_key.astype(jnp.bfloat16),
            grad_value.astype(jnp.bfloat16),
        )

    grad_query, grad_key, grad_value = lax.map(
        one_group,
        (
            split_groups(queries),
            split_groups(key_side),
            split_groups(value_proj),
            log_total,
            split_groups(grad_context),
        ),
    )
    return (join_groups(grad_query), join_groups(grad_key), join_groups(grad_value))


def gather_shards(first_pieces, second_pieces, after=None):
    dp_count = lax.axis_size("dp")
    core = lax.rem(lax.axis_index("dp"), 2)
    first, second = jnp.stack(first_pieces), jnp.stack(second_pieces)
    mine = jnp.where(core == 0, first, second)
    gathered = lax.all_gather(mine, "tensor", axis=0, tiled=False)
    if after is not None:
        gathered, after = lax.optimization_barrier((gathered, after))
    other = lax.ppermute(gathered, "dp", perm=[(i, i ^ 1) for i in range(dp_count)])
    halves = (jnp.where(core == 0, gathered, other), jnp.where(core == 0, other, gathered))
    return [half[:, index] for half in halves for index in range(half.shape[1])]


def by_parts(grads):
    parts = lax.axis_size("tensor")
    columns = []
    for part in range(parts):
        used = 0
        for grad in grads:
            width = grad.shape[1] // parts
            columns.append(grad[:, part * width : (part + 1) * width].astype(jnp.bfloat16))
            used += width
        if used % 128:
            columns.append(jnp.zeros((grads[0].shape[0], 128 - used % 128), jnp.bfloat16))
    return jnp.concatenate(columns, axis=1)


def scatter_rows(joined):
    return lax.psum_scatter(joined, "dp", scatter_dimension=0, tiled=True)


def scatter_parts(partials, widths):
    parts = lax.axis_size("tensor")
    joined = jnp.concatenate(
        [partial.reshape(partial.shape[0], parts, -1) for partial in partials], axis=2
    )
    summed = lax.psum_scatter(joined, "tensor", scatter_dimension=1, tiled=True)[:, 0]
    pieces = []
    start = 0
    for partial, group in zip(partials, widths):
        for width in group:
            pieces.append(summed[:, start : start + width].astype(jnp.float32))
            start += width
        start += partial.shape[1] // parts - sum(group)
    return pieces


def on_device(
    layer_input,
    segments,
    query_weight,
    query_bias,
    key_weight,
    value_weight,
    value_bias,
    output_weight,
    output_bias,
    first_gain,
    first_shift,
    up_weight,
    up_bias,
    down_weight,
    down_bias,
    second_gain,
    second_shift,
    output_grad,
):
    part_count = lax.axis_size("tensor")
    part_id = lax.axis_index("tensor")
    row_len = segments.shape[1]

    input_rows = lax.dynamic_slice_in_dim(layer_input, part_id * row_len, row_len, 0)
    segment_row = lax.dynamic_index_in_dim(segments, part_id, 0, keepdims=False)
    grad_out = lax.dynamic_slice_in_dim(output_grad, part_id * row_len, row_len, 0).astype(
        jnp.float32
    )

    qt_sh, kt_sh, vt_sh, o_sh = gather_shards(
        [query_weight.T, key_weight.T], [value_weight.T, output_weight]
    )
    bias_sh = lax.all_gather(
        jnp.concatenate([query_bias, value_bias, up_bias]), "tensor", axis=0, tiled=False
    )
    head_width = query_bias.shape[0]
    qb = bias_sh[:, :head_width].reshape(-1)
    vb = bias_sh[:, head_width : 2 * head_width].reshape(-1)
    ub = bias_sh[:, 2 * head_width :]
    width = qt_sh.shape[2]
    qt_full = qt_sh.reshape(-1, width)
    kt_full = kt_sh.reshape(-1, width)
    vt_full = vt_sh.reshape(-1, width)

    input_f32 = input_rows.astype(jnp.float32)
    queries = (contract_last(input_rows, qt_full) + qb).astype(jnp.bfloat16)
    key_side = contract_last(input_rows, kt_full).astype(jnp.bfloat16)
    value_proj = (contract_last(input_rows, vt_full) + vb).astype(jnp.bfloat16)
    context, log_total = attend(queries, key_side, value_proj, segment_row)
    u_sh, d_sh = gather_shards([up_weight], [down_weight], after=context)

    group_width = o_sh.shape[1]
    attn_total = input_f32
    for member in range(part_count):
        cols = slice(member * group_width, (member + 1) * group_width)
        attn_total = attn_total + product(context[:, cols], o_sh[member]).astype(
            jnp.bfloat16
        ).astype(jnp.float32)
    first_in = attn_total + output_bias
    first_out, first_unit, first_inv = normalize(first_in, first_gain, first_shift)
    first_low = first_out.astype(jnp.bfloat16)
    second_in = first_out
    pulls = []
    hidden_parts = []
    for member in range(part_count):
        pre_part = product(first_low, u_sh[member]) + ub[member]
        gelu_out, pull_gelu = jax.vjp(gelu_tanh, pre_part)
        pulls.append(pull_gelu)
        hidden_part = gelu_out.astype(jnp.bfloat16)
        hidden_parts.append(hidden_part)
        second_in = second_in + product(hidden_part, d_sh[member]).astype(
            jnp.bfloat16
        ).astype(jnp.float32)
    second_in = second_in + down_bias
    second_out, second_unit, second_inv = normalize(second_in, second_gain, second_shift)
    layer_output = second_out.astype(jnp.bfloat16)

    grad_second = normalize_back(grad_out, second_unit, second_inv, second_gain)
    grad_second_gain = jnp.sum(grad_out * second_unit, 0)
    grad_second_shift = jnp.sum(grad_out, 0)
    grad_down_bias = jnp.sum(grad_second, 0)
    down_low = grad_second.astype(jnp.bfloat16)
    first_grad = grad_second
    grad_pre_parts = []
    for member in range(part_count):
        grad_hidden = contract_last(down_low, d_sh[member])
        grad_pre = pulls[member](grad_hidden)[0].astype(jnp.bfloat16)
        grad_pre_parts.append(grad_pre)
        first_grad = first_grad + contract_last(grad_pre, u_sh[member])
    grad_pre = jnp.concatenate(grad_pre_parts, axis=1)
    hidden_low = jnp.concatenate(hidden_parts, axis=1)
    grad_up_bias = jnp.sum(grad_pre, 0, dtype=jnp.float32)
    grad_first_gain = jnp.sum(first_grad * first_unit, 0)
    grad_first_shift = jnp.sum(first_grad, 0)
    attn_grad = normalize_back(first_grad, first_unit, first_inv, first_gain)
    grad_output_bias = jnp.sum(attn_grad, 0)
    attn_grad_low = attn_grad.astype(jnp.bfloat16)
    grad_context = contract_last(attn_grad_low, o_sh.reshape(-1, o_sh.shape[2])).astype(
        jnp.bfloat16
    )
    ffn_grads = [
        contract_rows(first_low, grad_pre),
        contract_rows(down_low, hidden_low),
        contract_rows(attn_grad_low, context),
    ]
    ffn_widths = [grad.shape[1] // part_count for grad in ffn_grads]
    ffn_joined, grad_context = lax.optimization_barrier((by_parts(ffn_grads), grad_context))
    ffn_rows = scatter_rows(ffn_joined)
    query_low, key_low, value_low = attend_back(
        queries, key_side, value_proj, segment_row, log_total, grad_context
    )
    ffn_rows, query_low, key_low, value_low = lax.optimization_barrier(
        (ffn_rows, query_low, key_low, value_low)
    )
    grad_query_bias = jnp.sum(query_low, 0, dtype=jnp.float32)
    grad_value_bias = jnp.sum(value_low, 0, dtype=jnp.float32)
    qkv_low = jnp.stack([query_low, key_low, value_low], axis=1)
    qkv_low = qkv_low.reshape(row_len, 3, part_count, -1).transpose(0, 2, 1, 3)
    qkv_grads = contract_rows(input_rows, qkv_low.reshape(row_len, -1)).astype(jnp.bfloat16)
    qkv_widths = [qkv_grads.shape[1] // part_count]
    summed = scatter_parts(
        [ffn_rows, scatter_rows(qkv_grads)], [ffn_widths, qkv_widths]
    )
    ffn_summed = summed[:3]
    attn_summed = summed[3].reshape(summed[3].shape[0], 3, -1)
    input_grad = (
        attn_grad
        + product(query_low, qt_full)
        + product(key_low, kt_full)
        + product(value_low, vt_full)
    )
    small = lax.psum(
        jnp.concatenate(
            [
                grad_query_bias,
                grad_value_bias,
                grad_up_bias,
                grad_output_bias,
                grad_first_gain,
                grad_first_shift,
                grad_down_bias,
                grad_second_gain,
                grad_second_shift,
            ]
        ),
        ("dp", "tensor"),
    )
    split_width = 2 * head_width * part_count + up_bias.shape[0] * part_count
    split = small[:split_width]
    shared = small[split_width:].reshape(6, -1)
    device_id = lax.axis_index("dp") * part_count + part_id
    piece = shared.shape[1] // (lax.axis_size("dp") * part_count)
    shared = lax.dynamic_slice_in_dim(shared, device_id * piece, piece, 1)

    def own_block(vector, offset, width):
        return lax.dynamic_slice_in_dim(vector, offset + part_id * width, width, 0)

    query_bias_grad = own_block(split, 0, head_width)
    value_bias_grad = own_block(split, head_width * part_count, head_width)
    up_bias_grad = own_block(split, 2 * head_width * part_count, up_bias.shape[0])
    return (
        layer_output,
        input_grad,
        attn_summed[:, 0],
        query_bias_grad,
        attn_summed[:, 1],
        attn_summed[:, 2],
        value_bias_grad,
        ffn_summed[2].T,
        shared[0],
        shared[1],
        shared[2],
        ffn_summed[0],
        up_bias_grad,
        ffn_summed[1].T,
        shared[3],
        shared[4],
        shared[5],
    )


def solution(mesh):
    in_specs = (
        P("dp", None),
        P("dp", None),
        P(None, "tensor"),
        P("tensor"),
        P(None, "tensor"),
        P(None, "tensor"),
        P("tensor"),
        P("tensor", None),
        P(),
        P(),
        P(),
        P(None, "tensor"),
        P("tensor"),
        P("tensor", None),
        P(),
        P(),
        P(),
        P("dp", None),
    )
    out_specs = (
        P(("dp", "tensor"), None),
        P(("dp", "tensor"), None),
        P("dp", "tensor"),
        P("tensor"),
        P("dp", "tensor"),
        P("dp", "tensor"),
        P("tensor"),
        P("tensor", "dp"),
        P(("dp", "tensor")),
        P(("dp", "tensor")),
        P(("dp", "tensor")),
        P("dp", "tensor"),
        P("tensor"),
        P("tensor", "dp"),
        P(("dp", "tensor")),
        P(("dp", "tensor")),
        P(("dp", "tensor")),
    )
    return jax.shard_map(
        on_device, mesh=mesh, in_specs=in_specs, out_specs=out_specs, check_vma=False
    )
```

```python
import jax
import jax.numpy as jnp
from jax import lax
from jax.experimental import pallas as pl
from jax.experimental.pallas import tpu as pltpu
from jax.sharding import PartitionSpec as P

HEAD_DIM = 64
GROUP_HEADS = 3

norm_eps = 1e-06


def product(left_side, right_side):
    return jnp.dot(left_side, right_side, preferred_element_type=jnp.float32)


def contract_rows(left_side, right_side):
    return lax.dot_general(
        left_side, right_side, (((0,), (0,)), ((), ())), preferred_element_type=jnp.float32
    )


def contract_last(left_side, right_side):
    return lax.dot_general(
        left_side, right_side, (((1,), (1,)), ((), ())), preferred_element_type=jnp.float32
    )


def normalize(summed, norm_gain, offset):
    centred = summed - jnp.mean(summed, -1, keepdims=True)
    inverse = lax.rsqrt(jnp.mean(centred * centred, -1, keepdims=True) + norm_eps)
    scaled = centred * inverse
    return (scaled * norm_gain + offset, scaled, inverse)


def normalize_back(grad_out, scaled, inverse, norm_gain):
    grad_scaled = grad_out * norm_gain
    mean_grad = jnp.mean(grad_scaled, -1, keepdims=True)
    mean_cross = jnp.mean(grad_scaled * scaled, -1, keepdims=True)
    return inverse * (grad_scaled - mean_grad - scaled * mean_cross)


def gelu_tanh(pre_act):
    return jax.nn.gelu(pre_act, approximate=True)


SCALE = HEAD_DIM ** (-0.5)
STATS = 128


def _scores(q, k, linked):
    s = lax.dot_general(q, k, (((1,), (1,)), ((), ())), preferred_element_type=jnp.float32) * SCALE
    return jnp.where(linked, s, -1e30)


def attn_fwd_kernel(q_ref, k_ref, v_ref, segq_ref, segk_ref, ctx_ref, stats_ref):
    linked = segq_ref[...] == segk_ref[...]
    heads = q_ref.shape[1] // HEAD_DIM
    half = STATS // 2
    for h in range(heads):
        cols = slice(h * HEAD_DIM, (h + 1) * HEAD_DIM)
        s = _scores(q_ref[:, cols], k_ref[:, cols], linked)
        m = jnp.max(s, axis=1, keepdims=True)
        e = jnp.exp(s - m)
        l = jnp.sum(e, axis=1, keepdims=True)
        p = (e / l).astype(jnp.bfloat16)
        ctx = jnp.dot(p, v_ref[:, cols], preferred_element_type=jnp.float32)
        ctx_ref[:, cols] = ctx.astype(ctx_ref.dtype)
        stats_ref[:, h : h + 1] = m
        stats_ref[:, half + h : half + h + 1] = l


def attn_bwd_kernel(q_ref, k_ref, v_ref, dctx_ref, segq_ref, segk_ref, stats_ref,
                    dq_ref, dk_ref, dv_ref, dk_acc, dv_acc):
    step = pl.program_id(0)

    @pl.when(step == 0)
    def _():
        dk_acc[...] = jnp.zeros_like(dk_acc)
        dv_acc[...] = jnp.zeros_like(dv_acc)

    linked = segq_ref[...] == segk_ref[...]
    heads = q_ref.shape[1] // HEAD_DIM
    half = STATS // 2
    for h in range(heads):
        cols = slice(h * HEAD_DIM, (h + 1) * HEAD_DIM)
        q = q_ref[:, cols]
        k = k_ref[:, cols]
        dctx = dctx_ref[:, cols]
        s = _scores(q, k, linked)
        p = jnp.exp(s - stats_ref[:, h : h + 1]) / stats_ref[:, half + h : half + h + 1]
        dp = lax.dot_general(dctx, v_ref[:, cols], (((1,), (1,)), ((), ())), preferred_element_type=jnp.float32)
        inner = jnp.sum(p * dp, axis=1, keepdims=True)
        ds = (p * (dp - inner)).astype(jnp.bfloat16)
        dq = jnp.dot(ds, k, preferred_element_type=jnp.float32) * SCALE
        dq_ref[:, cols] = dq.astype(dq_ref.dtype)
        dk_acc[:, cols] += lax.dot_general(ds, q, (((0,), (0,)), ((), ())), preferred_element_type=jnp.float32)
        dv_acc[:, cols] += lax.dot_general(p.astype(jnp.bfloat16), dctx, (((0,), (0,)), ((), ())), preferred_element_type=jnp.float32)

    @pl.when(step == pl.num_programs(0) - 1)
    def _():
        dk_ref[...] = (dk_acc[...] * SCALE).astype(dk_ref.dtype)
        dv_ref[...] = dv_acc[...].astype(dv_ref.dtype)


def attention_forward(queries, key_side, value_proj, segment_row, block=256):
    length, width = queries.shape
    segq = segment_row.reshape(length, 1)
    segk = segment_row.reshape(1, length)
    full = pl.BlockSpec((length, width), lambda i: (0, 0))
    return pl.pallas_call(
        attn_fwd_kernel,
        out_shape=(jax.ShapeDtypeStruct((length, width), jnp.bfloat16),
                   jax.ShapeDtypeStruct((length, STATS), jnp.float32)),
        grid=(length // block,),
        in_specs=[pl.BlockSpec((block, width), lambda i: (i, 0)), full, full,
                  pl.BlockSpec((block, 1), lambda i: (i, 0)),
                  pl.BlockSpec((1, length), lambda i: (0, 0))],
        out_specs=(pl.BlockSpec((block, width), lambda i: (i, 0)),
                   pl.BlockSpec((block, STATS), lambda i: (i, 0))),
        compiler_params=pltpu.CompilerParams(dimension_semantics=("arbitrary",)),
        cost_estimate=pl.CostEstimate(flops=4 * length * length * width, transcendentals=length * length * width // HEAD_DIM,
                                      bytes_accessed=8 * length * width),
    )(queries, key_side, value_proj, segq, segk)


def attention_backward(queries, key_side, value_proj, segment_row, stats, grad_context, block=256):
    length, width = queries.shape
    segq = segment_row.reshape(length, 1)
    segk = segment_row.reshape(1, length)
    full = pl.BlockSpec((length, width), lambda i: (0, 0))
    rows = pl.BlockSpec((block, width), lambda i: (i, 0))
    return pl.pallas_call(
        attn_bwd_kernel,
        out_shape=tuple(jax.ShapeDtypeStruct((length, width), jnp.bfloat16) for _ in range(3)),
        grid=(length // block,),
        in_specs=[rows, full, full, rows,
                  pl.BlockSpec((block, 1), lambda i: (i, 0)),
                  pl.BlockSpec((1, length), lambda i: (0, 0)),
                  pl.BlockSpec((block, STATS), lambda i: (i, 0))],
        out_specs=(rows, full, full),
        scratch_shapes=[pltpu.VMEM((length, width), jnp.float32), pltpu.VMEM((length, width), jnp.float32)],
        compiler_params=pltpu.CompilerParams(dimension_semantics=("arbitrary",)),
        cost_estimate=pl.CostEstimate(flops=10 * length * length * width, transcendentals=length * length * width // HEAD_DIM,
                                      bytes_accessed=14 * length * width),
    )(queries, key_side, value_proj, grad_context, segq, segk, stats)


def gather_shards(first_pieces, second_pieces, after=None):
    dp_count = lax.axis_size("dp")
    core = lax.rem(lax.axis_index("dp"), 2)
    first, second = jnp.stack(first_pieces), jnp.stack(second_pieces)
    mine = jnp.where(core == 0, first, second)
    gathered = lax.all_gather(mine, "tensor", axis=0, tiled=False)
    if after is not None:
        gathered, after = lax.optimization_barrier((gathered, after))
    other = lax.ppermute(gathered, "dp", perm=[(i, i ^ 1) for i in range(dp_count)])
    halves = (jnp.where(core == 0, gathered, other), jnp.where(core == 0, other, gathered))
    return [half[:, index] for half in halves for index in range(half.shape[1])]


def by_parts(grads):
    parts = lax.axis_size("tensor")
    columns = []
    for part in range(parts):
        used = 0
        for grad in grads:
            width = grad.shape[1] // parts
            columns.append(grad[:, part * width : (part + 1) * width].astype(jnp.bfloat16))
            used += width
        if used % 128:
            columns.append(jnp.zeros((grads[0].shape[0], 128 - used % 128), jnp.bfloat16))
    return jnp.concatenate(columns, axis=1)


def scatter_rows(joined):
    return lax.psum_scatter(joined, "dp", scatter_dimension=0, tiled=True)


def scatter_parts(partials, widths):
    parts = lax.axis_size("tensor")
    joined = jnp.concatenate(
        [partial.reshape(partial.shape[0], parts, -1) for partial in partials], axis=2
    )
    summed = lax.psum_scatter(joined, "tensor", scatter_dimension=1, tiled=True)[:, 0]
    pieces = []
    start = 0
    for partial, group in zip(partials, widths):
        for width in group:
            pieces.append(summed[:, start : start + width].astype(jnp.float32))
            start += width
        start += partial.shape[1] // parts - sum(group)
    return pieces


def on_device(
    layer_input,
    segments,
    query_weight,
    query_bias,
    key_weight,
    value_weight,
    value_bias,
    output_weight,
    output_bias,
    first_gain,
    first_shift,
    up_weight,
    up_bias,
    down_weight,
    down_bias,
    second_gain,
    second_shift,
    output_grad,
):
    part_count = lax.axis_size("tensor")
    part_id = lax.axis_index("tensor")
    row_len = segments.shape[1]

    input_rows = lax.dynamic_slice_in_dim(layer_input, part_id * row_len, row_len, 0)
    segment_row = lax.dynamic_index_in_dim(segments, part_id, 0, keepdims=False)
    grad_out = lax.dynamic_slice_in_dim(output_grad, part_id * row_len, row_len, 0).astype(
        jnp.float32
    )

    qt_sh, kt_sh, vt_sh, o_sh = gather_shards(
        [query_weight.T, key_weight.T], [value_weight.T, output_weight]
    )
    bias_sh = lax.all_gather(
        jnp.concatenate([query_bias, value_bias, up_bias]), "tensor", axis=0, tiled=False
    )
    head_width = query_bias.shape[0]
    qb = bias_sh[:, :head_width].reshape(-1)
    vb = bias_sh[:, head_width : 2 * head_width].reshape(-1)
    ub = bias_sh[:, 2 * head_width :]
    width = qt_sh.shape[2]
    qt_full = qt_sh.reshape(-1, width)
    kt_full = kt_sh.reshape(-1, width)
    vt_full = vt_sh.reshape(-1, width)

    input_f32 = input_rows.astype(jnp.float32)
    queries = (contract_last(input_rows, qt_full) + qb).astype(jnp.bfloat16)
    key_side = contract_last(input_rows, kt_full).astype(jnp.bfloat16)
    value_proj = (contract_last(input_rows, vt_full) + vb).astype(jnp.bfloat16)
    context, softmax_stats = attention_forward(queries, key_side, value_proj, segment_row)
    u_sh, d_sh = gather_shards([up_weight], [down_weight], after=context)

    group_width = o_sh.shape[1]
    attn_total = input_f32
    for member in range(part_count):
        cols = slice(member * group_width, (member + 1) * group_width)
        attn_total = attn_total + product(context[:, cols], o_sh[member]).astype(
            jnp.bfloat16
        ).astype(jnp.float32)
    first_in = attn_total + output_bias
    first_out, first_unit, first_inv = normalize(first_in, first_gain, first_shift)
    first_low = first_out.astype(jnp.bfloat16)
    second_in = first_out
    pulls = []
    hidden_parts = []
    for member in range(part_count):
        pre_part = product(first_low, u_sh[member]) + ub[member]
        gelu_out, pull_gelu = jax.vjp(gelu_tanh, pre_part)
        pulls.append(pull_gelu)
        hidden_part = gelu_out.astype(jnp.bfloat16)
        hidden_parts.append(hidden_part)
        second_in = second_in + product(hidden_part, d_sh[member]).astype(
            jnp.bfloat16
        ).astype(jnp.float32)
    second_in = second_in + down_bias
    second_out, second_unit, second_inv = normalize(second_in, second_gain, second_shift)
    layer_output = second_out.astype(jnp.bfloat16)

    grad_second = normalize_back(grad_out, second_unit, second_inv, second_gain)
    grad_second_gain = jnp.sum(grad_out * second_unit, 0)
    grad_second_shift = jnp.sum(grad_out, 0)
    grad_down_bias = jnp.sum(grad_second, 0)
    down_low = grad_second.astype(jnp.bfloat16)
    first_grad = grad_second
    grad_pre_parts = []
    for member in range(part_count):
        grad_hidden = contract_last(down_low, d_sh[member])
        grad_pre = pulls[member](grad_hidden)[0].astype(jnp.bfloat16)
        grad_pre_parts.append(grad_pre)
        first_grad = first_grad + contract_last(grad_pre, u_sh[member])
    grad_pre = jnp.concatenate(grad_pre_parts, axis=1)
    hidden_low = jnp.concatenate(hidden_parts, axis=1)
    grad_up_bias = jnp.sum(grad_pre, 0, dtype=jnp.float32)
    grad_first_gain = jnp.sum(first_grad * first_unit, 0)
    grad_first_shift = jnp.sum(first_grad, 0)
    attn_grad = normalize_back(first_grad, first_unit, first_inv, first_gain)
    grad_output_bias = jnp.sum(attn_grad, 0)
    attn_grad_low = attn_grad.astype(jnp.bfloat16)
    grad_context = contract_last(attn_grad_low, o_sh.reshape(-1, o_sh.shape[2])).astype(
        jnp.bfloat16
    )
    ffn_grads = [
        contract_rows(first_low, grad_pre),
        contract_rows(down_low, hidden_low),
        contract_rows(attn_grad_low, context),
    ]
    ffn_widths = [grad.shape[1] // part_count for grad in ffn_grads]
    ffn_joined, grad_context = lax.optimization_barrier((by_parts(ffn_grads), grad_context))
    ffn_rows = scatter_rows(ffn_joined)
    query_low, key_low, value_low = attention_backward(
        queries, key_side, value_proj, segment_row, softmax_stats, grad_context
    )
    ffn_rows, query_low, key_low, value_low = lax.optimization_barrier(
        (ffn_rows, query_low, key_low, value_low)
    )
    grad_query_bias = jnp.sum(query_low, 0, dtype=jnp.float32)
    grad_value_bias = jnp.sum(value_low, 0, dtype=jnp.float32)
    qkv_low = jnp.stack([query_low, key_low, value_low], axis=1)
    qkv_low = qkv_low.reshape(row_len, 3, part_count, -1).transpose(0, 2, 1, 3)
    qkv_grads = contract_rows(input_rows, qkv_low.reshape(row_len, -1)).astype(jnp.bfloat16)
    qkv_widths = [qkv_grads.shape[1] // part_count]
    summed = scatter_parts(
        [ffn_rows, scatter_rows(qkv_grads)], [ffn_widths, qkv_widths]
    )
    ffn_summed = summed[:3]
    attn_summed = summed[3].reshape(summed[3].shape[0], 3, -1)
    input_grad = (
        attn_grad
        + product(query_low, qt_full)
        + product(key_low, kt_full)
        + product(value_low, vt_full)
    )
    small = lax.psum(
        jnp.concatenate(
            [
                grad_query_bias,
                grad_value_bias,
                grad_up_bias,
                grad_output_bias,
                grad_first_gain,
                grad_first_shift,
                grad_down_bias,
                grad_second_gain,
                grad_second_shift,
            ]
        ),
        ("dp", "tensor"),
    )
    split_width = 2 * head_width * part_count + up_bias.shape[0] * part_count
    split = small[:split_width]
    shared = small[split_width:].reshape(6, -1)
    device_id = lax.axis_index("dp") * part_count + part_id
    piece = shared.shape[1] // (lax.axis_size("dp") * part_count)
    shared = lax.dynamic_slice_in_dim(shared, device_id * piece, piece, 1)

    def own_block(vector, offset, width):
        return lax.dynamic_slice_in_dim(vector, offset + part_id * width, width, 0)

    query_bias_grad = own_block(split, 0, head_width)
    value_bias_grad = own_block(split, head_width * part_count, head_width)
    up_bias_grad = own_block(split, 2 * head_width * part_count, up_bias.shape[0])
    return (
        layer_output,
        input_grad,
        attn_summed[:, 0],
        query_bias_grad,
        attn_summed[:, 1],
        attn_summed[:, 2],
        value_bias_grad,
        ffn_summed[2].T,
        shared[0],
        shared[1],
        shared[2],
        ffn_summed[0],
        up_bias_grad,
        ffn_summed[1].T,
        shared[3],
        shared[4],
        shared[5],
    )


def solution(mesh):
    in_specs = (
        P("dp", None),
        P("dp", None),
        P(None, "tensor"),
        P("tensor"),
        P(None, "tensor"),
        P(None, "tensor"),
        P("tensor"),
        P("tensor", None),
        P(),
        P(),
        P(),
        P(None, "tensor"),
        P("tensor"),
        P("tensor", None),
        P(),
        P(),
        P(),
        P("dp", None),
    )
    out_specs = (
        P(("dp", "tensor"), None),
        P(("dp", "tensor"), None),
        P("dp", "tensor"),
        P("tensor"),
        P("dp", "tensor"),
        P("dp", "tensor"),
        P("tensor"),
        P("tensor", "dp"),
        P(("dp", "tensor")),
        P(("dp", "tensor")),
        P(("dp", "tensor")),
        P("dp", "tensor"),
        P("tensor"),
        P("tensor", "dp"),
        P(("dp", "tensor")),
        P(("dp", "tensor")),
        P(("dp", "tensor")),
    )
    return jax.shard_map(
        on_device, mesh=mesh, in_specs=in_specs, out_specs=out_specs, check_vma=False
    )
```

```python
import jax
import jax.numpy as jnp
from jax import lax
from jax.experimental import pallas as pl
from jax.experimental.pallas import tpu as pltpu
from jax.sharding import PartitionSpec as P

HEAD_DIM = 64
GROUP_HEADS = 3

norm_eps = 1e-06


def product(left_side, right_side):
    return jnp.dot(left_side, right_side, preferred_element_type=jnp.float32)


def contract_rows(left_side, right_side):
    return lax.dot_general(
        left_side, right_side, (((0,), (0,)), ((), ())), preferred_element_type=jnp.float32
    )


def contract_last(left_side, right_side):
    return lax.dot_general(
        left_side, right_side, (((1,), (1,)), ((), ())), preferred_element_type=jnp.float32
    )


def normalize(summed, norm_gain, offset):
    centred = summed - jnp.mean(summed, -1, keepdims=True)
    inverse = lax.rsqrt(jnp.mean(centred * centred, -1, keepdims=True) + norm_eps)
    scaled = centred * inverse
    return (scaled * norm_gain + offset, scaled, inverse)


def normalize_back(grad_out, scaled, inverse, norm_gain):
    grad_scaled = grad_out * norm_gain
    mean_grad = jnp.mean(grad_scaled, -1, keepdims=True)
    mean_cross = jnp.mean(grad_scaled * scaled, -1, keepdims=True)
    return inverse * (grad_scaled - mean_grad - scaled * mean_cross)


def gelu_tanh(pre_act):
    return jax.nn.gelu(pre_act, approximate=True)


SCALE = HEAD_DIM ** (-0.5)
STATS = 128


def _scores(q, k, linked):
    s = lax.dot_general(q, k, (((1,), (1,)), ((), ())), preferred_element_type=jnp.float32) * SCALE
    return jnp.where(linked, s, -1e30)


def attn_fwd_kernel(q_ref, k_ref, v_ref, segq_ref, segk_ref, ctx_ref, stats_ref):
    linked = segq_ref[...] == segk_ref[...]
    heads = q_ref.shape[1] // HEAD_DIM
    half = STATS // 2
    for h in range(heads):
        cols = slice(h * HEAD_DIM, (h + 1) * HEAD_DIM)
        s = _scores(q_ref[:, cols], k_ref[:, cols], linked)
        m = jnp.max(s, axis=1, keepdims=True)
        e = jnp.exp(s - m)
        l = jnp.sum(e, axis=1, keepdims=True)
        p = (e / l).astype(jnp.bfloat16)
        ctx = jnp.dot(p, v_ref[:, cols], preferred_element_type=jnp.float32)
        ctx_ref[:, cols] = ctx.astype(ctx_ref.dtype)
        stats_ref[:, h : h + 1] = m
        stats_ref[:, half + h : half + h + 1] = l


def attn_bwd_kernel(q_ref, k_ref, v_ref, dctx_ref, segq_ref, segk_ref, stats_ref,
                    dq_ref, dk_ref, dv_ref, dk_acc, dv_acc):
    step = pl.program_id(0)

    @pl.when(step == 0)
    def _():
        dk_acc[...] = jnp.zeros_like(dk_acc)
        dv_acc[...] = jnp.zeros_like(dv_acc)

    linked = segq_ref[...] == segk_ref[...]
    heads = q_ref.shape[1] // HEAD_DIM
    half = STATS // 2
    for h in range(heads):
        cols = slice(h * HEAD_DIM, (h + 1) * HEAD_DIM)
        q = q_ref[:, cols]
        k = k_ref[:, cols]
        dctx = dctx_ref[:, cols]
        s = _scores(q, k, linked)
        p = jnp.exp(s - stats_ref[:, h : h + 1]) / stats_ref[:, half + h : half + h + 1]
        dp = lax.dot_general(dctx, v_ref[:, cols], (((1,), (1,)), ((), ())), preferred_element_type=jnp.float32)
        inner = jnp.sum(p * dp, axis=1, keepdims=True)
        ds = (p * (dp - inner)).astype(jnp.bfloat16)
        dq = jnp.dot(ds, k, preferred_element_type=jnp.float32) * SCALE
        dq_ref[:, cols] = dq.astype(dq_ref.dtype)
        dk_acc[:, cols] += lax.dot_general(ds, q, (((0,), (0,)), ((), ())), preferred_element_type=jnp.float32)
        dv_acc[:, cols] += lax.dot_general(p.astype(jnp.bfloat16), dctx, (((0,), (0,)), ((), ())), preferred_element_type=jnp.float32)

    @pl.when(step == pl.num_programs(0) - 1)
    def _():
        dk_ref[...] = (dk_acc[...] * SCALE).astype(dk_ref.dtype)
        dv_ref[...] = dv_acc[...].astype(dv_ref.dtype)


def attention_forward(queries, key_side, value_proj, segment_row, block=256):
    length, width = queries.shape
    segq = segment_row.reshape(length, 1)
    segk = segment_row.reshape(1, length)
    full = pl.BlockSpec((length, width), lambda i: (0, 0))
    return pl.pallas_call(
        attn_fwd_kernel,
        out_shape=(jax.ShapeDtypeStruct((length, width), jnp.bfloat16),
                   jax.ShapeDtypeStruct((length, STATS), jnp.float32)),
        grid=(length // block,),
        in_specs=[pl.BlockSpec((block, width), lambda i: (i, 0)), full, full,
                  pl.BlockSpec((block, 1), lambda i: (i, 0)),
                  pl.BlockSpec((1, length), lambda i: (0, 0))],
        out_specs=(pl.BlockSpec((block, width), lambda i: (i, 0)),
                   pl.BlockSpec((block, STATS), lambda i: (i, 0))),
        compiler_params=pltpu.CompilerParams(dimension_semantics=("arbitrary",)),
        cost_estimate=pl.CostEstimate(flops=4 * length * length * width, transcendentals=length * length * width // HEAD_DIM,
                                      bytes_accessed=8 * length * width),
    )(queries, key_side, value_proj, segq, segk)


def attention_backward(queries, key_side, value_proj, segment_row, stats, grad_context, block=256):
    length, width = queries.shape
    segq = segment_row.reshape(length, 1)
    segk = segment_row.reshape(1, length)
    full = pl.BlockSpec((length, width), lambda i: (0, 0))
    rows = pl.BlockSpec((block, width), lambda i: (i, 0))
    return pl.pallas_call(
        attn_bwd_kernel,
        out_shape=tuple(jax.ShapeDtypeStruct((length, width), jnp.bfloat16) for _ in range(3)),
        grid=(length // block,),
        in_specs=[rows, full, full, rows,
                  pl.BlockSpec((block, 1), lambda i: (i, 0)),
                  pl.BlockSpec((1, length), lambda i: (0, 0)),
                  pl.BlockSpec((block, STATS), lambda i: (i, 0))],
        out_specs=(rows, full, full),
        scratch_shapes=[pltpu.VMEM((length, width), jnp.float32), pltpu.VMEM((length, width), jnp.float32)],
        compiler_params=pltpu.CompilerParams(dimension_semantics=("arbitrary",)),
        cost_estimate=pl.CostEstimate(flops=10 * length * length * width, transcendentals=length * length * width // HEAD_DIM,
                                      bytes_accessed=14 * length * width),
    )(queries, key_side, value_proj, grad_context, segq, segk, stats)


def gather_shards(first_pieces, second_pieces, after=None):
    dp_count = lax.axis_size("dp")
    core = lax.rem(lax.axis_index("dp"), 2)
    first, second = jnp.stack(first_pieces), jnp.stack(second_pieces)
    mine = jnp.where(core == 0, first, second)
    gathered = lax.all_gather(mine, "tensor", axis=0, tiled=False)
    if after is not None:
        gathered, after = lax.optimization_barrier((gathered, after))
    other = lax.ppermute(gathered, "dp", perm=[(i, i ^ 1) for i in range(dp_count)])
    halves = (jnp.where(core == 0, gathered, other), jnp.where(core == 0, other, gathered))
    return [half[:, index] for half in halves for index in range(half.shape[1])]


def scatter_rows(grads):
    joined = jnp.concatenate([grad.astype(jnp.bfloat16) for grad in grads], axis=1)
    return lax.psum_scatter(joined, "dp", scatter_dimension=0, tiled=True)


def scatter_parts(partials, counts):
    parts = lax.axis_size("tensor")
    flat = []
    for partial, count in zip(partials, counts):
        rows, width = partial.shape
        split = partial.reshape(rows, count, parts, width // (count * parts)).transpose(2, 1, 0, 3)
        flat.append(split.reshape(parts, -1))
    joined = jnp.concatenate(flat, axis=1).reshape(-1, 128)
    summed = lax.psum_scatter(joined, "tensor", scatter_dimension=0, tiled=True).reshape(-1)
    pieces = []
    start = 0
    for partial, count in zip(partials, counts):
        rows, width = partial.shape
        size = rows * width // parts
        block = summed[start : start + size].reshape(count, rows, -1).astype(jnp.float32)
        pieces.extend(block[index] for index in range(count))
        start += size
    return pieces


def on_device(
    layer_input,
    segments,
    query_weight,
    query_bias,
    key_weight,
    value_weight,
    value_bias,
    output_weight,
    output_bias,
    first_gain,
    first_shift,
    up_weight,
    up_bias,
    down_weight,
    down_bias,
    second_gain,
    second_shift,
    output_grad,
):
    part_count = lax.axis_size("tensor")
    part_id = lax.axis_index("tensor")
    row_len = segments.shape[1]

    input_rows = lax.dynamic_slice_in_dim(layer_input, part_id * row_len, row_len, 0)
    segment_row = lax.dynamic_index_in_dim(segments, part_id, 0, keepdims=False)
    grad_out = lax.dynamic_slice_in_dim(output_grad, part_id * row_len, row_len, 0).astype(
        jnp.float32
    )

    qt_sh, kt_sh, vt_sh, o_sh = gather_shards(
        [query_weight.T, key_weight.T], [value_weight.T, output_weight]
    )
    bias_sh = lax.all_gather(
        jnp.concatenate([query_bias, value_bias, up_bias]), "tensor", axis=0, tiled=False
    )
    head_width = query_bias.shape[0]
    qb = bias_sh[:, :head_width].reshape(-1)
    vb = bias_sh[:, head_width : 2 * head_width].reshape(-1)
    ub = bias_sh[:, 2 * head_width :]
    width = qt_sh.shape[2]
    qt_full = qt_sh.reshape(-1, width)
    kt_full = kt_sh.reshape(-1, width)
    vt_full = vt_sh.reshape(-1, width)

    input_f32 = input_rows.astype(jnp.float32)
    queries = (contract_last(input_rows, qt_full) + qb).astype(jnp.bfloat16)
    key_side = contract_last(input_rows, kt_full).astype(jnp.bfloat16)
    value_proj = (contract_last(input_rows, vt_full) + vb).astype(jnp.bfloat16)
    context, softmax_stats = attention_forward(queries, key_side, value_proj, segment_row)
    u_sh, d_sh = gather_shards([up_weight], [down_weight], after=context)

    group_width = o_sh.shape[1]
    attn_total = input_f32
    for member in range(part_count):
        cols = slice(member * group_width, (member + 1) * group_width)
        attn_total = attn_total + product(context[:, cols], o_sh[member]).astype(
            jnp.bfloat16
        ).astype(jnp.float32)
    first_in = attn_total + output_bias
    first_out, first_unit, first_inv = normalize(first_in, first_gain, first_shift)
    first_low = first_out.astype(jnp.bfloat16)
    second_in = first_out
    pulls = []
    hidden_parts = []
    for member in range(part_count):
        pre_part = product(first_low, u_sh[member]) + ub[member]
        gelu_out, pull_gelu = jax.vjp(gelu_tanh, pre_part)
        pulls.append(pull_gelu)
        hidden_part = gelu_out.astype(jnp.bfloat16)
        hidden_parts.append(hidden_part)
        second_in = second_in + product(hidden_part, d_sh[member]).astype(
            jnp.bfloat16
        ).astype(jnp.float32)
    second_in = second_in + down_bias
    second_out, second_unit, second_inv = normalize(second_in, second_gain, second_shift)
    layer_output = second_out.astype(jnp.bfloat16)

    grad_second = normalize_back(grad_out, second_unit, second_inv, second_gain)
    grad_second_gain = jnp.sum(grad_out * second_unit, 0)
    grad_second_shift = jnp.sum(grad_out, 0)
    grad_down_bias = jnp.sum(grad_second, 0)
    down_low = grad_second.astype(jnp.bfloat16)
    first_grad = grad_second
    grad_pre_parts = []
    for member in range(part_count):
        grad_hidden = contract_last(down_low, d_sh[member])
        grad_pre = pulls[member](grad_hidden)[0].astype(jnp.bfloat16)
        grad_pre_parts.append(grad_pre)
        first_grad = first_grad + contract_last(grad_pre, u_sh[member])
    grad_pre = jnp.concatenate(grad_pre_parts, axis=1)
    hidden_low = jnp.concatenate(hidden_parts, axis=1)
    grad_up_bias = jnp.sum(grad_pre, 0, dtype=jnp.float32)
    ffn_grads = [contract_rows(first_low, grad_pre), contract_rows(down_low, hidden_low)]
    ffn_joined, first_grad = lax.optimization_barrier(
        (jnp.concatenate([grad.astype(jnp.bfloat16) for grad in ffn_grads], axis=1), first_grad)
    )
    ffn_rows = scatter_rows([ffn_joined])
    grad_first_gain = jnp.sum(first_grad * first_unit, 0)
    grad_first_shift = jnp.sum(first_grad, 0)
    attn_grad = normalize_back(first_grad, first_unit, first_inv, first_gain)
    grad_output_bias = jnp.sum(attn_grad, 0)
    attn_grad_low = attn_grad.astype(jnp.bfloat16)
    grad_context = contract_last(attn_grad_low, o_sh.reshape(-1, o_sh.shape[2])).astype(
        jnp.bfloat16
    )
    output_grad_t = contract_rows(attn_grad_low, context)
    query_low, key_low, value_low = attention_backward(
        queries, key_side, value_proj, segment_row, softmax_stats, grad_context
    )
    ffn_rows, query_low, key_low, value_low = lax.optimization_barrier(
        (ffn_rows, query_low, key_low, value_low)
    )
    grad_query_bias = jnp.sum(query_low, 0, dtype=jnp.float32)
    grad_value_bias = jnp.sum(value_low, 0, dtype=jnp.float32)
    attn_rows = scatter_rows(
        [
            contract_rows(input_rows, query_low),
            contract_rows(input_rows, key_low),
            contract_rows(input_rows, value_low),
            output_grad_t,
        ]
    )
    summed = scatter_parts([ffn_rows, attn_rows], [2, 4])
    input_grad = (
        attn_grad
        + product(query_low, qt_full)
        + product(key_low, kt_full)
        + product(value_low, vt_full)
    )
    small = lax.psum(
        jnp.concatenate(
            [
                grad_query_bias,
                grad_value_bias,
                grad_up_bias,
                grad_output_bias,
                grad_first_gain,
                grad_first_shift,
                grad_down_bias,
                grad_second_gain,
                grad_second_shift,
            ]
        ),
        ("dp", "tensor"),
    )
    split_width = 2 * head_width * part_count + up_bias.shape[0] * part_count
    split = small[:split_width]
    shared = small[split_width:].reshape(6, -1)
    device_id = lax.axis_index("dp") * part_count + part_id
    piece = shared.shape[1] // (lax.axis_size("dp") * part_count)
    shared = lax.dynamic_slice_in_dim(shared, device_id * piece, piece, 1)

    def own_block(vector, offset, width):
        return lax.dynamic_slice_in_dim(vector, offset + part_id * width, width, 0)

    query_bias_grad = own_block(split, 0, head_width)
    value_bias_grad = own_block(split, head_width * part_count, head_width)
    up_bias_grad = own_block(split, 2 * head_width * part_count, up_bias.shape[0])
    return (
        layer_output,
        input_grad,
        summed[2],
        query_bias_grad,
        summed[3],
        summed[4],
        value_bias_grad,
        summed[5].T,
        shared[0],
        shared[1],
        shared[2],
        summed[0],
        up_bias_grad,
        summed[1].T,
        shared[3],
        shared[4],
        shared[5],
    )


def solution(mesh):
    in_specs = (
        P("dp", None),
        P("dp", None),
        P(None, "tensor"),
        P("tensor"),
        P(None, "tensor"),
        P(None, "tensor"),
        P("tensor"),
        P("tensor", None),
        P(),
        P(),
        P(),
        P(None, "tensor"),
        P("tensor"),
        P("tensor", None),
        P(),
        P(),
        P(),
        P("dp", None),
    )
    out_specs = (
        P(("dp", "tensor"), None),
        P(("dp", "tensor"), None),
        P("dp", "tensor"),
        P("tensor"),
        P("dp", "tensor"),
        P("dp", "tensor"),
        P("tensor"),
        P("tensor", "dp"),
        P(("dp", "tensor")),
        P(("dp", "tensor")),
        P(("dp", "tensor")),
        P("dp", "tensor"),
        P("tensor"),
        P("tensor", "dp"),
        P(("dp", "tensor")),
        P(("dp", "tensor")),
        P(("dp", "tensor")),
    )
    return jax.shard_map(
        on_device, mesh=mesh, in_specs=in_specs, out_specs=out_specs, check_vma=False
    )
```

```python
import jax
import jax.numpy as jnp
from jax import lax
from jax.experimental import pallas as pl
from jax.experimental.pallas import tpu as pltpu
from jax.sharding import PartitionSpec as P

HEAD_DIM = 64
GROUP_HEADS = 3

norm_eps = 1e-06


def product(left_side, right_side):
    return jnp.dot(left_side, right_side, preferred_element_type=jnp.float32)


def contract_rows(left_side, right_side):
    return lax.dot_general(
        left_side, right_side, (((0,), (0,)), ((), ())), preferred_element_type=jnp.float32
    )


def contract_last(left_side, right_side):
    return lax.dot_general(
        left_side, right_side, (((1,), (1,)), ((), ())), preferred_element_type=jnp.float32
    )


def normalize(summed, norm_gain, offset):
    centred = summed - jnp.mean(summed, -1, keepdims=True)
    inverse = lax.rsqrt(jnp.mean(centred * centred, -1, keepdims=True) + norm_eps)
    scaled = centred * inverse
    return (scaled * norm_gain + offset, scaled, inverse)


def normalize_back(grad_out, scaled, inverse, norm_gain):
    grad_scaled = grad_out * norm_gain
    mean_grad = jnp.mean(grad_scaled, -1, keepdims=True)
    mean_cross = jnp.mean(grad_scaled * scaled, -1, keepdims=True)
    return inverse * (grad_scaled - mean_grad - scaled * mean_cross)


def gelu_tanh(pre_act):
    return jax.nn.gelu(pre_act, approximate=True)


SCALE = HEAD_DIM ** (-0.5)
STATS = 128


def _scores(q, k, linked):
    s = lax.dot_general(q, k, (((1,), (1,)), ((), ())), preferred_element_type=jnp.float32) * SCALE
    return jnp.where(linked, s, -1e30)


def attn_fwd_kernel(q_ref, k_ref, v_ref, segq_ref, segk_ref, ctx_ref, stats_ref):
    linked = segq_ref[...] == segk_ref[...]
    heads = q_ref.shape[1] // HEAD_DIM
    half = STATS // 2
    for h in range(heads):
        cols = slice(h * HEAD_DIM, (h + 1) * HEAD_DIM)
        s = _scores(q_ref[:, cols], k_ref[:, cols], linked)
        m = jnp.max(s, axis=1, keepdims=True)
        e = jnp.exp(s - m)
        l = jnp.sum(e, axis=1, keepdims=True)
        p = (e / l).astype(jnp.bfloat16)
        ctx = jnp.dot(p, v_ref[:, cols], preferred_element_type=jnp.float32)
        ctx_ref[:, cols] = ctx.astype(ctx_ref.dtype)
        stats_ref[:, h : h + 1] = m
        stats_ref[:, half + h : half + h + 1] = l


def attn_bwd_kernel(q_ref, k_ref, v_ref, dctx_ref, segq_ref, segk_ref, stats_ref, x_ref, xall_ref,
                    out_t_ref, dq_ref, dk_ref, dv_ref, wgrad_ref, bias_ref, dk_acc, dv_acc, dwq_acc):
    step = pl.program_id(0)

    @pl.when(step == 0)
    def _():
        dk_acc[...] = jnp.zeros_like(dk_acc)
        dv_acc[...] = jnp.zeros_like(dv_acc)
        dwq_acc[...] = jnp.zeros_like(dwq_acc)
        bias_ref[...] = jnp.zeros_like(bias_ref)

    linked = segq_ref[...] == segk_ref[...]
    heads = q_ref.shape[1] // HEAD_DIM
    half = STATS // 2
    dq_parts = []
    for h in range(heads):
        cols = slice(h * HEAD_DIM, (h + 1) * HEAD_DIM)
        q = q_ref[:, cols]
        k = k_ref[:, cols]
        dctx = dctx_ref[:, cols]
        s = _scores(q, k, linked)
        p = jnp.exp(s - stats_ref[:, h : h + 1]) / stats_ref[:, half + h : half + h + 1]
        dp = lax.dot_general(dctx, v_ref[:, cols], (((1,), (1,)), ((), ())), preferred_element_type=jnp.float32)
        inner = jnp.sum(p * dp, axis=1, keepdims=True)
        ds = (p * (dp - inner)).astype(jnp.bfloat16)
        dq = (jnp.dot(ds, k, preferred_element_type=jnp.float32) * SCALE).astype(dq_ref.dtype)
        dq_ref[:, cols] = dq
        dq_parts.append(dq)
        dk_acc[:, cols] += lax.dot_general(ds, q, (((0,), (0,)), ((), ())), preferred_element_type=jnp.float32)
        dv_acc[:, cols] += lax.dot_general(p.astype(jnp.bfloat16), dctx, (((0,), (0,)), ((), ())), preferred_element_type=jnp.float32)
    dq_block = jnp.concatenate(dq_parts, axis=1)
    dwq_acc[...] += lax.dot_general(x_ref[...], dq_block, (((0,), (0,)), ((), ())), preferred_element_type=jnp.float32)
    bias_ref[0:1, :] += jnp.sum(dq_block.astype(jnp.float32), axis=0, keepdims=True)

    @pl.when(step == pl.num_programs(0) - 1)
    def _():
        width = dk_ref.shape[1]
        dk = (dk_acc[...] * SCALE).astype(dk_ref.dtype)
        dv = dv_acc[...].astype(dv_ref.dtype)
        dk_ref[...] = dk
        dv_ref[...] = dv
        bias_ref[1:2, :] = jnp.sum(dv.astype(jnp.float32), axis=0, keepdims=True)
        xall = xall_ref[...]
        wgrad_ref[:, 0:width] = dwq_acc[...].astype(wgrad_ref.dtype)
        wgrad_ref[:, width : 2 * width] = lax.dot_general(
            xall, dk, (((0,), (0,)), ((), ())), preferred_element_type=jnp.float32).astype(wgrad_ref.dtype)
        wgrad_ref[:, 2 * width : 3 * width] = lax.dot_general(
            xall, dv, (((0,), (0,)), ((), ())), preferred_element_type=jnp.float32).astype(wgrad_ref.dtype)
        wgrad_ref[:, 3 * width : 4 * width] = out_t_ref[...]


def attention_forward(queries, key_side, value_proj, segment_row, block=256):
    length, width = queries.shape
    segq = segment_row.reshape(length, 1)
    segk = segment_row.reshape(1, length)
    full = pl.BlockSpec((length, width), lambda i: (0, 0))
    return pl.pallas_call(
        attn_fwd_kernel,
        out_shape=(jax.ShapeDtypeStruct((length, width), jnp.bfloat16),
                   jax.ShapeDtypeStruct((length, STATS), jnp.float32)),
        grid=(length // block,),
        in_specs=[pl.BlockSpec((block, width), lambda i: (i, 0)), full, full,
                  pl.BlockSpec((block, 1), lambda i: (i, 0)),
                  pl.BlockSpec((1, length), lambda i: (0, 0))],
        out_specs=(pl.BlockSpec((block, width), lambda i: (i, 0)),
                   pl.BlockSpec((block, STATS), lambda i: (i, 0))),
        compiler_params=pltpu.CompilerParams(dimension_semantics=("arbitrary",)),
        cost_estimate=pl.CostEstimate(flops=4 * length * length * width, transcendentals=length * length * width // HEAD_DIM,
                                      bytes_accessed=8 * length * width),
    )(queries, key_side, value_proj, segq, segk)


def attention_backward(queries, key_side, value_proj, segment_row, stats, grad_context, inputs, out_t, block=256):
    length, width = queries.shape
    features = inputs.shape[1]
    segq = segment_row.reshape(length, 1)
    segk = segment_row.reshape(1, length)
    full = pl.BlockSpec((length, width), lambda i: (0, 0))
    rows = pl.BlockSpec((block, width), lambda i: (i, 0))
    return pl.pallas_call(
        attn_bwd_kernel,
        out_shape=tuple(jax.ShapeDtypeStruct((length, width), jnp.bfloat16) for _ in range(3))
        + (jax.ShapeDtypeStruct((features, 4 * width), jnp.bfloat16),
           jax.ShapeDtypeStruct((8, width), jnp.float32)),
        grid=(length // block,),
        in_specs=[rows, full, full, rows,
                  pl.BlockSpec((block, 1), lambda i: (i, 0)),
                  pl.BlockSpec((1, length), lambda i: (0, 0)),
                  pl.BlockSpec((block, STATS), lambda i: (i, 0)),
                  pl.BlockSpec((block, features), lambda i: (i, 0)),
                  pl.BlockSpec((length, features), lambda i: (0, 0)),
                  pl.BlockSpec((features, width), lambda i: (0, 0))],
        out_specs=(rows, full, full,
                   pl.BlockSpec((features, 4 * width), lambda i: (0, 0)),
                   pl.BlockSpec((8, width), lambda i: (0, 0))),
        scratch_shapes=[pltpu.VMEM((length, width), jnp.float32), pltpu.VMEM((length, width), jnp.float32),
                        pltpu.VMEM((features, width), jnp.float32)],
        compiler_params=pltpu.CompilerParams(dimension_semantics=("arbitrary",), vmem_limit_bytes=60 * 1024 * 1024),
        cost_estimate=pl.CostEstimate(flops=10 * length * length * width + 6 * length * features * width,
                                      transcendentals=length * length * width // HEAD_DIM,
                                      bytes_accessed=14 * length * width + 10 * features * width),
    )(queries, key_side, value_proj, grad_context, segq, segk, stats, inputs, inputs, out_t)


def gather_shards(first_pieces, second_pieces, after=None):
    dp_count = lax.axis_size("dp")
    core = lax.rem(lax.axis_index("dp"), 2)
    first, second = jnp.stack(first_pieces), jnp.stack(second_pieces)
    mine = jnp.where(core == 0, first, second)
    gathered = lax.all_gather(mine, "tensor", axis=0, tiled=False)
    if after is not None:
        gathered, after = lax.optimization_barrier((gathered, after))
    other = lax.ppermute(gathered, "dp", perm=[(i, i ^ 1) for i in range(dp_count)])
    halves = (jnp.where(core == 0, gathered, other), jnp.where(core == 0, other, gathered))
    return [half[:, index] for half in halves for index in range(half.shape[1])]


def scatter_rows(grads):
    joined = jnp.concatenate([grad.astype(jnp.bfloat16) for grad in grads], axis=1)
    return lax.psum_scatter(joined, "dp", scatter_dimension=0, tiled=True)


def scatter_parts(partials, counts):
    parts = lax.axis_size("tensor")
    flat = []
    for partial, count in zip(partials, counts):
        rows, width = partial.shape
        split = partial.reshape(rows, count, parts, width // (count * parts)).transpose(2, 1, 0, 3)
        flat.append(split.reshape(parts, -1))
    joined = jnp.concatenate(flat, axis=1).reshape(-1, 128)
    summed = lax.psum_scatter(joined, "tensor", scatter_dimension=0, tiled=True).reshape(-1)
    pieces = []
    start = 0
    for partial, count in zip(partials, counts):
        rows, width = partial.shape
        size = rows * width // parts
        block = summed[start : start + size].reshape(count, rows, -1).astype(jnp.float32)
        pieces.extend(block[index] for index in range(count))
        start += size
    return pieces


def on_device(
    layer_input,
    segments,
    query_weight,
    query_bias,
    key_weight,
    value_weight,
    value_bias,
    output_weight,
    output_bias,
    first_gain,
    first_shift,
    up_weight,
    up_bias,
    down_weight,
    down_bias,
    second_gain,
    second_shift,
    output_grad,
):
    part_count = lax.axis_size("tensor")
    part_id = lax.axis_index("tensor")
    row_len = segments.shape[1]

    input_rows = lax.dynamic_slice_in_dim(layer_input, part_id * row_len, row_len, 0)
    segment_row = lax.dynamic_index_in_dim(segments, part_id, 0, keepdims=False)
    grad_out = lax.dynamic_slice_in_dim(output_grad, part_id * row_len, row_len, 0).astype(
        jnp.float32
    )

    qt_sh, kt_sh, vt_sh, o_sh = gather_shards(
        [query_weight.T, key_weight.T], [value_weight.T, output_weight]
    )
    bias_sh = lax.all_gather(
        jnp.concatenate([query_bias, value_bias, up_bias]), "tensor", axis=0, tiled=False
    )
    head_width = query_bias.shape[0]
    qb = bias_sh[:, :head_width].reshape(-1)
    vb = bias_sh[:, head_width : 2 * head_width].reshape(-1)
    ub = bias_sh[:, 2 * head_width :]
    width = qt_sh.shape[2]
    qt_full = qt_sh.reshape(-1, width)
    kt_full = kt_sh.reshape(-1, width)
    vt_full = vt_sh.reshape(-1, width)

    input_f32 = input_rows.astype(jnp.float32)
    queries = (contract_last(input_rows, qt_full) + qb).astype(jnp.bfloat16)
    key_side = contract_last(input_rows, kt_full).astype(jnp.bfloat16)
    value_proj = (contract_last(input_rows, vt_full) + vb).astype(jnp.bfloat16)
    context, softmax_stats = attention_forward(queries, key_side, value_proj, segment_row)
    u_sh, d_sh = gather_shards([up_weight], [down_weight], after=context)

    group_width = o_sh.shape[1]
    attn_total = input_f32
    for member in range(part_count):
        cols = slice(member * group_width, (member + 1) * group_width)
        attn_total = attn_total + product(context[:, cols], o_sh[member]).astype(
            jnp.bfloat16
        ).astype(jnp.float32)
    first_in = attn_total + output_bias
    first_out, first_unit, first_inv = normalize(first_in, first_gain, first_shift)
    first_low = first_out.astype(jnp.bfloat16)
    second_in = first_out
    pulls = []
    hidden_parts = []
    for member in range(part_count):
        pre_part = product(first_low, u_sh[member]) + ub[member]
        gelu_out, pull_gelu = jax.vjp(gelu_tanh, pre_part)
        pulls.append(pull_gelu)
        hidden_part = gelu_out.astype(jnp.bfloat16)
        hidden_parts.append(hidden_part)
        second_in = second_in + product(hidden_part, d_sh[member]).astype(
            jnp.bfloat16
        ).astype(jnp.float32)
    second_in = second_in + down_bias
    second_out, second_unit, second_inv = normalize(second_in, second_gain, second_shift)
    layer_output = second_out.astype(jnp.bfloat16)

    grad_second = normalize_back(grad_out, second_unit, second_inv, second_gain)
    grad_second_gain = jnp.sum(grad_out * second_unit, 0)
    grad_second_shift = jnp.sum(grad_out, 0)
    grad_down_bias = jnp.sum(grad_second, 0)
    down_low = grad_second.astype(jnp.bfloat16)
    first_grad = grad_second
    grad_pre_parts = []
    for member in range(part_count):
        grad_hidden = contract_last(down_low, d_sh[member])
        grad_pre = pulls[member](grad_hidden)[0].astype(jnp.bfloat16)
        grad_pre_parts.append(grad_pre)
        first_grad = first_grad + contract_last(grad_pre, u_sh[member])
    grad_pre = jnp.concatenate(grad_pre_parts, axis=1)
    hidden_low = jnp.concatenate(hidden_parts, axis=1)
    grad_up_bias = jnp.sum(grad_pre, 0, dtype=jnp.float32)
    ffn_grads = [contract_rows(first_low, grad_pre), contract_rows(down_low, hidden_low)]
    ffn_joined, first_grad = lax.optimization_barrier(
        (jnp.concatenate([grad.astype(jnp.bfloat16) for grad in ffn_grads], axis=1), first_grad)
    )
    ffn_rows = scatter_rows([ffn_joined])
    grad_first_gain = jnp.sum(first_grad * first_unit, 0)
    grad_first_shift = jnp.sum(first_grad, 0)
    attn_grad = normalize_back(first_grad, first_unit, first_inv, first_gain)
    grad_output_bias = jnp.sum(attn_grad, 0)
    attn_grad_low = attn_grad.astype(jnp.bfloat16)
    grad_context = contract_last(attn_grad_low, o_sh.reshape(-1, o_sh.shape[2])).astype(
        jnp.bfloat16
    )
    output_grad_t = contract_rows(attn_grad_low, context).astype(jnp.bfloat16)
    query_low, key_low, value_low, attn_joined, qv_bias = attention_backward(
        queries, key_side, value_proj, segment_row, softmax_stats, grad_context, input_rows,
        output_grad_t,
    )
    ffn_rows, attn_joined, qv_bias = lax.optimization_barrier((ffn_rows, attn_joined, qv_bias))
    grad_query_bias = qv_bias[0]
    grad_value_bias = qv_bias[1]
    attn_rows = scatter_rows([attn_joined])
    small = lax.psum(
        jnp.concatenate(
            [
                grad_query_bias,
                grad_value_bias,
                grad_up_bias,
                grad_output_bias,
                grad_first_gain,
                grad_first_shift,
                grad_down_bias,
                grad_second_gain,
                grad_second_shift,
            ]
        ),
        ("dp", "tensor"),
    )
    input_grad = (
        attn_grad
        + product(query_low, qt_full)
        + product(key_low, kt_full)
        + product(value_low, vt_full)
    )
    attn_rows, small, input_grad = lax.optimization_barrier((attn_rows, small, input_grad))
    summed = scatter_parts([ffn_rows, attn_rows], [2, 4])
    split_width = 2 * head_width * part_count + up_bias.shape[0] * part_count
    split = small[:split_width]
    shared = small[split_width:].reshape(6, -1)
    device_id = lax.axis_index("dp") * part_count + part_id
    piece = shared.shape[1] // (lax.axis_size("dp") * part_count)
    shared = lax.dynamic_slice_in_dim(shared, device_id * piece, piece, 1)

    def own_block(vector, offset, width):
        return lax.dynamic_slice_in_dim(vector, offset + part_id * width, width, 0)

    query_bias_grad = own_block(split, 0, head_width)
    value_bias_grad = own_block(split, head_width * part_count, head_width)
    up_bias_grad = own_block(split, 2 * head_width * part_count, up_bias.shape[0])
    return (
        layer_output,
        input_grad,
        summed[2],
        query_bias_grad,
        summed[3],
        summed[4],
        value_bias_grad,
        summed[5].T,
        shared[0],
        shared[1],
        shared[2],
        summed[0],
        up_bias_grad,
        summed[1].T,
        shared[3],
        shared[4],
        shared[5],
    )


def solution(mesh):
    in_specs = (
        P("dp", None),
        P("dp", None),
        P(None, "tensor"),
        P("tensor"),
        P(None, "tensor"),
        P(None, "tensor"),
        P("tensor"),
        P("tensor", None),
        P(),
        P(),
        P(),
        P(None, "tensor"),
        P("tensor"),
        P("tensor", None),
        P(),
        P(),
        P(),
        P("dp", None),
    )
    out_specs = (
        P(("dp", "tensor"), None),
        P(("dp", "tensor"), None),
        P("dp", "tensor"),
        P("tensor"),
        P("dp", "tensor"),
        P("dp", "tensor"),
        P("tensor"),
        P("tensor", "dp"),
        P(("dp", "tensor")),
        P(("dp", "tensor")),
        P(("dp", "tensor")),
        P("dp", "tensor"),
        P("tensor"),
        P("tensor", "dp"),
        P(("dp", "tensor")),
        P(("dp", "tensor")),
        P(("dp", "tensor")),
    )
    return jax.shard_map(
        on_device, mesh=mesh, in_specs=in_specs, out_specs=out_specs, check_vma=False
    )
```

```python
import functools

import jax
import jax.numpy as jnp
from jax import lax
from jax.experimental import pallas as pl
from jax.experimental.pallas import tpu as pltpu
from jax.sharding import PartitionSpec as P

HEAD_DIM = 64
GROUP_HEADS = 3

norm_eps = 1e-06


def product(left_side, right_side):
    return jnp.dot(left_side, right_side, preferred_element_type=jnp.float32)


def contract_rows(left_side, right_side):
    return lax.dot_general(
        left_side, right_side, (((0,), (0,)), ((), ())), preferred_element_type=jnp.float32
    )


def contract_last(left_side, right_side):
    return lax.dot_general(
        left_side, right_side, (((1,), (1,)), ((), ())), preferred_element_type=jnp.float32
    )


def normalize(summed, norm_gain, offset):
    centred = summed - jnp.mean(summed, -1, keepdims=True)
    inverse = lax.rsqrt(jnp.mean(centred * centred, -1, keepdims=True) + norm_eps)
    scaled = centred * inverse
    return (scaled * norm_gain + offset, scaled, inverse)


def normalize_back(grad_out, scaled, inverse, norm_gain):
    grad_scaled = grad_out * norm_gain
    mean_grad = jnp.mean(grad_scaled, -1, keepdims=True)
    mean_cross = jnp.mean(grad_scaled * scaled, -1, keepdims=True)
    return inverse * (grad_scaled - mean_grad - scaled * mean_cross)


def gelu_tanh(pre_act):
    return jax.nn.gelu(pre_act, approximate=True)


SCALE = HEAD_DIM ** (-0.5)
STATS = 128


def _scores(q, k, linked):
    s = lax.dot_general(q, k, (((1,), (1,)), ((), ())), preferred_element_type=jnp.float32) * SCALE
    return jnp.where(linked, s, -1e30)


def attn_fwd_kernel(q_ref, k_ref, v_ref, segq_ref, segk_ref, ctx_ref, stats_ref):
    linked = segq_ref[...] == segk_ref[...]
    heads = q_ref.shape[1] // HEAD_DIM
    half = STATS // 2
    for h in range(heads):
        cols = slice(h * HEAD_DIM, (h + 1) * HEAD_DIM)
        s = _scores(q_ref[:, cols], k_ref[:, cols], linked)
        m = jnp.max(s, axis=1, keepdims=True)
        e = jnp.exp(s - m)
        l = jnp.sum(e, axis=1, keepdims=True)
        p = (e / l).astype(jnp.bfloat16)
        ctx = jnp.dot(p, v_ref[:, cols], preferred_element_type=jnp.float32)
        ctx_ref[:, cols] = ctx.astype(ctx_ref.dtype)
        stats_ref[:, h : h + 1] = m
        stats_ref[:, half + h : half + h + 1] = l


def attn_bwd_kernel(parts, q_ref, k_ref, v_ref, dctx_ref, segq_ref, segk_ref, stats_ref, x_ref, xall_ref,
                    out_t_ref, dq_ref, dk_ref, dv_ref, wgrad_ref, bias_ref, dk_acc, dv_acc, dwq_acc):
    step = pl.program_id(0)

    @pl.when(step == 0)
    def _():
        dk_acc[...] = jnp.zeros_like(dk_acc)
        dv_acc[...] = jnp.zeros_like(dv_acc)
        dwq_acc[...] = jnp.zeros_like(dwq_acc)
        bias_ref[...] = jnp.zeros_like(bias_ref)

    linked = segq_ref[...] == segk_ref[...]
    heads = q_ref.shape[1] // HEAD_DIM
    half = STATS // 2
    dq_parts = []
    for h in range(heads):
        cols = slice(h * HEAD_DIM, (h + 1) * HEAD_DIM)
        q = q_ref[:, cols]
        k = k_ref[:, cols]
        dctx = dctx_ref[:, cols]
        s = _scores(q, k, linked)
        p = jnp.exp(s - stats_ref[:, h : h + 1]) / stats_ref[:, half + h : half + h + 1]
        dp = lax.dot_general(dctx, v_ref[:, cols], (((1,), (1,)), ((), ())), preferred_element_type=jnp.float32)
        inner = jnp.sum(p * dp, axis=1, keepdims=True)
        ds = (p * (dp - inner)).astype(jnp.bfloat16)
        dq = (jnp.dot(ds, k, preferred_element_type=jnp.float32) * SCALE).astype(dq_ref.dtype)
        dq_ref[:, cols] = dq
        dq_parts.append(dq)
        dk_acc[:, cols] += lax.dot_general(ds, q, (((0,), (0,)), ((), ())), preferred_element_type=jnp.float32)
        dv_acc[:, cols] += lax.dot_general(p.astype(jnp.bfloat16), dctx, (((0,), (0,)), ((), ())), preferred_element_type=jnp.float32)
    dq_block = jnp.concatenate(dq_parts, axis=1)
    dwq_acc[...] += lax.dot_general(x_ref[...], dq_block, (((0,), (0,)), ((), ())), preferred_element_type=jnp.float32)
    bias_ref[0:1, :] += jnp.sum(dq_block.astype(jnp.float32), axis=0, keepdims=True)

    @pl.when(step == pl.num_programs(0) - 1)
    def _():
        width = dk_ref.shape[1]
        dk = (dk_acc[...] * SCALE).astype(dk_ref.dtype)
        dv = dv_acc[...].astype(dv_ref.dtype)
        dk_ref[...] = dk
        dv_ref[...] = dv
        bias_ref[1:2, :] = jnp.sum(dv.astype(jnp.float32), axis=0, keepdims=True)
        xall = xall_ref[...]
        grads = (
            dwq_acc[...].astype(wgrad_ref.dtype),
            lax.dot_general(xall, dk, (((0,), (0,)), ((), ())),
                            preferred_element_type=jnp.float32).astype(wgrad_ref.dtype),
            lax.dot_general(xall, dv, (((0,), (0,)), ((), ())),
                            preferred_element_type=jnp.float32).astype(wgrad_ref.dtype),
            out_t_ref[...],
        )
        piece = width // parts
        for part in range(parts):
            for index, grad in enumerate(grads):
                start = (part * len(grads) + index) * piece
                wgrad_ref[:, start : start + piece] = grad[:, part * piece : (part + 1) * piece]


def attention_forward(queries, key_side, value_proj, segment_row, block=256):
    length, width = queries.shape
    segq = segment_row.reshape(length, 1)
    segk = segment_row.reshape(1, length)
    full = pl.BlockSpec((length, width), lambda i: (0, 0))
    return pl.pallas_call(
        attn_fwd_kernel,
        out_shape=(jax.ShapeDtypeStruct((length, width), jnp.bfloat16),
                   jax.ShapeDtypeStruct((length, STATS), jnp.float32)),
        grid=(length // block,),
        in_specs=[pl.BlockSpec((block, width), lambda i: (i, 0)), full, full,
                  pl.BlockSpec((block, 1), lambda i: (i, 0)),
                  pl.BlockSpec((1, length), lambda i: (0, 0))],
        out_specs=(pl.BlockSpec((block, width), lambda i: (i, 0)),
                   pl.BlockSpec((block, STATS), lambda i: (i, 0))),
        compiler_params=pltpu.CompilerParams(dimension_semantics=("arbitrary",)),
        cost_estimate=pl.CostEstimate(flops=4 * length * length * width, transcendentals=length * length * width // HEAD_DIM,
                                      bytes_accessed=8 * length * width),
    )(queries, key_side, value_proj, segq, segk)


def attention_backward(queries, key_side, value_proj, segment_row, stats, grad_context, inputs, out_t, parts,
                       block=256):
    length, width = queries.shape
    features = inputs.shape[1]
    segq = segment_row.reshape(length, 1)
    segk = segment_row.reshape(1, length)
    full = pl.BlockSpec((length, width), lambda i: (0, 0))
    rows = pl.BlockSpec((block, width), lambda i: (i, 0))
    return pl.pallas_call(
        functools.partial(attn_bwd_kernel, parts),
        out_shape=tuple(jax.ShapeDtypeStruct((length, width), jnp.bfloat16) for _ in range(3))
        + (jax.ShapeDtypeStruct((features, 4 * width), jnp.bfloat16),
           jax.ShapeDtypeStruct((8, width), jnp.float32)),
        grid=(length // block,),
        in_specs=[rows, full, full, rows,
                  pl.BlockSpec((block, 1), lambda i: (i, 0)),
                  pl.BlockSpec((1, length), lambda i: (0, 0)),
                  pl.BlockSpec((block, STATS), lambda i: (i, 0)),
                  pl.BlockSpec((block, features), lambda i: (i, 0)),
                  pl.BlockSpec((length, features), lambda i: (0, 0)),
                  pl.BlockSpec((features, width), lambda i: (0, 0))],
        out_specs=(rows, full, full,
                   pl.BlockSpec((features, 4 * width), lambda i: (0, 0)),
                   pl.BlockSpec((8, width), lambda i: (0, 0))),
        scratch_shapes=[pltpu.VMEM((length, width), jnp.float32), pltpu.VMEM((length, width), jnp.float32),
                        pltpu.VMEM((features, width), jnp.float32)],
        compiler_params=pltpu.CompilerParams(dimension_semantics=("arbitrary",), vmem_limit_bytes=60 * 1024 * 1024),
        cost_estimate=pl.CostEstimate(flops=10 * length * length * width + 6 * length * features * width,
                                      transcendentals=length * length * width // HEAD_DIM,
                                      bytes_accessed=14 * length * width + 10 * features * width),
    )(queries, key_side, value_proj, grad_context, segq, segk, stats, inputs, inputs, out_t)


def gather_shards(first_pieces, second_pieces, after=None):
    dp_count = lax.axis_size("dp")
    core = lax.rem(lax.axis_index("dp"), 2)
    first, second = jnp.stack(first_pieces), jnp.stack(second_pieces)
    mine = jnp.where(core == 0, first, second)
    gathered = lax.all_gather(mine, "tensor", axis=0, tiled=False)
    if after is not None:
        gathered, after = lax.optimization_barrier((gathered, after))
    other = lax.ppermute(gathered, "dp", perm=[(i, i ^ 1) for i in range(dp_count)])
    halves = (jnp.where(core == 0, gathered, other), jnp.where(core == 0, other, gathered))
    return [half[:, index] for half in halves for index in range(half.shape[1])]


def scatter_rows(grads):
    joined = jnp.concatenate([grad.astype(jnp.bfloat16) for grad in grads], axis=1)
    return lax.psum_scatter(joined, "dp", scatter_dimension=0, tiled=True)


def part_major(grads):
    parts = lax.axis_size("tensor")
    columns = []
    for part in range(parts):
        for grad in grads:
            width = grad.shape[1] // parts
            columns.append(grad[:, part * width : (part + 1) * width].astype(jnp.bfloat16))
    return jnp.concatenate(columns, axis=1)


def scatter_parts(partials, widths):
    parts = lax.axis_size("tensor")
    joined = jnp.concatenate(
        [partial.reshape(partial.shape[0], parts, -1) for partial in partials], axis=2
    )
    summed = lax.psum_scatter(joined, "tensor", scatter_dimension=1, tiled=True)[:, 0]
    pieces = []
    start = 0
    for group in widths:
        for width in group:
            pieces.append(summed[:, start : start + width].astype(jnp.float32))
            start += width
    return pieces


def on_device(
    layer_input,
    segments,
    query_weight,
    query_bias,
    key_weight,
    value_weight,
    value_bias,
    output_weight,
    output_bias,
    first_gain,
    first_shift,
    up_weight,
    up_bias,
    down_weight,
    down_bias,
    second_gain,
    second_shift,
    output_grad,
):
    part_count = lax.axis_size("tensor")
    part_id = lax.axis_index("tensor")
    row_len = segments.shape[1]

    input_rows = lax.dynamic_slice_in_dim(layer_input, part_id * row_len, row_len, 0)
    segment_row = lax.dynamic_index_in_dim(segments, part_id, 0, keepdims=False)
    grad_out = lax.dynamic_slice_in_dim(output_grad, part_id * row_len, row_len, 0).astype(
        jnp.float32
    )

    qt_sh, kt_sh, vt_sh, o_sh = gather_shards(
        [query_weight.T, key_weight.T], [value_weight.T, output_weight]
    )
    bias_sh = lax.all_gather(
        jnp.concatenate([query_bias, value_bias, up_bias]), "tensor", axis=0, tiled=False
    )
    head_width = query_bias.shape[0]
    qb = bias_sh[:, :head_width].reshape(-1)
    vb = bias_sh[:, head_width : 2 * head_width].reshape(-1)
    ub = bias_sh[:, 2 * head_width :]
    width = qt_sh.shape[2]
    qt_full = qt_sh.reshape(-1, width)
    kt_full = kt_sh.reshape(-1, width)
    vt_full = vt_sh.reshape(-1, width)

    input_f32 = input_rows.astype(jnp.float32)
    queries = (contract_last(input_rows, qt_full) + qb).astype(jnp.bfloat16)
    key_side = contract_last(input_rows, kt_full).astype(jnp.bfloat16)
    value_proj = (contract_last(input_rows, vt_full) + vb).astype(jnp.bfloat16)
    context, softmax_stats = attention_forward(queries, key_side, value_proj, segment_row)
    u_sh, d_sh = gather_shards([up_weight], [down_weight], after=context)

    group_width = o_sh.shape[1]
    attn_total = input_f32
    for member in range(part_count):
        cols = slice(member * group_width, (member + 1) * group_width)
        attn_total = attn_total + product(context[:, cols], o_sh[member]).astype(
            jnp.bfloat16
        ).astype(jnp.float32)
    first_in = attn_total + output_bias
    first_out, first_unit, first_inv = normalize(first_in, first_gain, first_shift)
    first_low = first_out.astype(jnp.bfloat16)
    second_in = first_out
    pulls = []
    hidden_parts = []
    for member in range(part_count):
        pre_part = product(first_low, u_sh[member]) + ub[member]
        gelu_out, pull_gelu = jax.vjp(gelu_tanh, pre_part)
        pulls.append(pull_gelu)
        hidden_part = gelu_out.astype(jnp.bfloat16)
        hidden_parts.append(hidden_part)
        second_in = second_in + product(hidden_part, d_sh[member]).astype(
            jnp.bfloat16
        ).astype(jnp.float32)
    second_in = second_in + down_bias
    second_out, second_unit, second_inv = normalize(second_in, second_gain, second_shift)
    layer_output = second_out.astype(jnp.bfloat16)

    grad_second = normalize_back(grad_out, second_unit, second_inv, second_gain)
    grad_second_gain = jnp.sum(grad_out * second_unit, 0)
    grad_second_shift = jnp.sum(grad_out, 0)
    grad_down_bias = jnp.sum(grad_second, 0)
    down_low = grad_second.astype(jnp.bfloat16)
    first_grad = grad_second
    grad_pre_parts = []
    for member in range(part_count):
        grad_hidden = contract_last(down_low, d_sh[member])
        grad_pre = pulls[member](grad_hidden)[0].astype(jnp.bfloat16)
        grad_pre_parts.append(grad_pre)
        first_grad = first_grad + contract_last(grad_pre, u_sh[member])
    grad_pre = jnp.concatenate(grad_pre_parts, axis=1)
    hidden_low = jnp.concatenate(hidden_parts, axis=1)
    grad_up_bias = jnp.sum(grad_pre, 0, dtype=jnp.float32)
    ffn_grads = [contract_rows(first_low, grad_pre), contract_rows(down_low, hidden_low)]
    ffn_joined, first_grad = lax.optimization_barrier((part_major(ffn_grads), first_grad))
    ffn_rows = scatter_rows([ffn_joined])
    grad_first_gain = jnp.sum(first_grad * first_unit, 0)
    grad_first_shift = jnp.sum(first_grad, 0)
    attn_grad = normalize_back(first_grad, first_unit, first_inv, first_gain)
    grad_output_bias = jnp.sum(attn_grad, 0)
    attn_grad_low = attn_grad.astype(jnp.bfloat16)
    grad_context = contract_last(attn_grad_low, o_sh.reshape(-1, o_sh.shape[2])).astype(
        jnp.bfloat16
    )
    output_grad_t = contract_rows(attn_grad_low, context).astype(jnp.bfloat16)
    query_low, key_low, value_low, attn_joined, qv_bias = attention_backward(
        queries, key_side, value_proj, segment_row, softmax_stats, grad_context, input_rows,
        output_grad_t, part_count,
    )
    ffn_rows, attn_joined, qv_bias = lax.optimization_barrier((ffn_rows, attn_joined, qv_bias))
    grad_query_bias = qv_bias[0]
    grad_value_bias = qv_bias[1]
    attn_rows = scatter_rows([attn_joined])
    small = lax.psum(
        jnp.concatenate(
            [
                grad_query_bias,
                grad_value_bias,
                grad_up_bias,
                grad_output_bias,
                grad_first_gain,
                grad_first_shift,
                grad_down_bias,
                grad_second_gain,
                grad_second_shift,
            ]
        ),
        ("dp", "tensor"),
    )
    input_grad = (
        attn_grad
        + product(query_low, qt_full)
        + product(key_low, kt_full)
        + product(value_low, vt_full)
    )
    attn_rows, small, input_grad = lax.optimization_barrier((attn_rows, small, input_grad))
    ffn_width = up_weight.shape[1]
    summed = scatter_parts([ffn_rows, attn_rows], [[ffn_width] * 2, [head_width] * 4])
    split_width = 2 * head_width * part_count + up_bias.shape[0] * part_count
    split = small[:split_width]
    shared = small[split_width:].reshape(6, -1)
    device_id = lax.axis_index("dp") * part_count + part_id
    piece = shared.shape[1] // (lax.axis_size("dp") * part_count)
    shared = lax.dynamic_slice_in_dim(shared, device_id * piece, piece, 1)

    def own_block(vector, offset, width):
        return lax.dynamic_slice_in_dim(vector, offset + part_id * width, width, 0)

    query_bias_grad = own_block(split, 0, head_width)
    value_bias_grad = own_block(split, head_width * part_count, head_width)
    up_bias_grad = own_block(split, 2 * head_width * part_count, up_bias.shape[0])
    return (
        layer_output,
        input_grad,
        summed[2],
        query_bias_grad,
        summed[3],
        summed[4],
        value_bias_grad,
        summed[5].T,
        shared[0],
        shared[1],
        shared[2],
        summed[0],
        up_bias_grad,
        summed[1].T,
        shared[3],
        shared[4],
        shared[5],
    )


def solution(mesh):
    in_specs = (
        P("dp", None),
        P("dp", None),
        P(None, "tensor"),
        P("tensor"),
        P(None, "tensor"),
        P(None, "tensor"),
        P("tensor"),
        P("tensor", None),
        P(),
        P(),
        P(),
        P(None, "tensor"),
        P("tensor"),
        P("tensor", None),
        P(),
        P(),
        P(),
        P("dp", None),
    )
    out_specs = (
        P(("dp", "tensor"), None),
        P(("dp", "tensor"), None),
        P("dp", "tensor"),
        P("tensor"),
        P("dp", "tensor"),
        P("dp", "tensor"),
        P("tensor"),
        P("tensor", "dp"),
        P(("dp", "tensor")),
        P(("dp", "tensor")),
        P(("dp", "tensor")),
        P("dp", "tensor"),
        P("tensor"),
        P("tensor", "dp"),
        P(("dp", "tensor")),
        P(("dp", "tensor")),
        P(("dp", "tensor")),
    )
    return jax.shard_map(
        on_device, mesh=mesh, in_specs=in_specs, out_specs=out_specs, check_vma=False
    )
```

```python
import functools

import jax
import jax.numpy as jnp
from jax import lax
from jax.experimental import pallas as pl
from jax.experimental.pallas import tpu as pltpu
from jax.sharding import PartitionSpec as P

HEAD_DIM = 64
GROUP_HEADS = 3

norm_eps = 1e-06


def product(left_side, right_side):
    return jnp.dot(left_side, right_side, preferred_element_type=jnp.float32)


def contract_rows(left_side, right_side):
    return lax.dot_general(
        left_side, right_side, (((0,), (0,)), ((), ())), preferred_element_type=jnp.float32
    )


def contract_last(left_side, right_side):
    return lax.dot_general(
        left_side, right_side, (((1,), (1,)), ((), ())), preferred_element_type=jnp.float32
    )


def normalize(summed, norm_gain, offset):
    centred = summed - jnp.mean(summed, -1, keepdims=True)
    inverse = lax.rsqrt(jnp.mean(centred * centred, -1, keepdims=True) + norm_eps)
    scaled = centred * inverse
    return (scaled * norm_gain + offset, scaled, inverse)


def normalize_back(grad_out, scaled, inverse, norm_gain):
    grad_scaled = grad_out * norm_gain
    mean_grad = jnp.mean(grad_scaled, -1, keepdims=True)
    mean_cross = jnp.mean(grad_scaled * scaled, -1, keepdims=True)
    return inverse * (grad_scaled - mean_grad - scaled * mean_cross)


def gelu_tanh(pre_act):
    return jax.nn.gelu(pre_act, approximate=True)


SCALE = HEAD_DIM ** (-0.5)
STATS = 128


def _scores(q, k, linked):
    s = lax.dot_general(q, k, (((1,), (1,)), ((), ())), preferred_element_type=jnp.float32) * SCALE
    return jnp.where(linked, s, -1e30)


def attn_fwd_kernel(q_ref, k_ref, v_ref, segq_ref, segk_ref, ctx_ref, stats_ref):
    linked = segq_ref[...] == segk_ref[...]
    heads = q_ref.shape[1] // HEAD_DIM
    half = STATS // 2
    for h in range(heads):
        cols = slice(h * HEAD_DIM, (h + 1) * HEAD_DIM)
        s = _scores(q_ref[:, cols], k_ref[:, cols], linked)
        m = jnp.max(s, axis=1, keepdims=True)
        e = jnp.exp(s - m)
        l = jnp.sum(e, axis=1, keepdims=True)
        p = (e / l).astype(jnp.bfloat16)
        ctx = jnp.dot(p, v_ref[:, cols], preferred_element_type=jnp.float32)
        ctx_ref[:, cols] = ctx.astype(ctx_ref.dtype)
        stats_ref[:, h : h + 1] = m
        stats_ref[:, half + h : half + h + 1] = l


def attn_bwd_kernel(parts, q_ref, k_ref, v_ref, dctx_ref, segq_ref, segk_ref, stats_ref, x_ref, xall_ref,
                    out_t_ref, dq_ref, dk_ref, dv_ref, wgrad_ref, bias_ref, dk_acc, dv_acc, dwq_acc):
    step = pl.program_id(0)

    @pl.when(step == 0)
    def _():
        dk_acc[...] = jnp.zeros_like(dk_acc)
        dv_acc[...] = jnp.zeros_like(dv_acc)
        dwq_acc[...] = jnp.zeros_like(dwq_acc)
        bias_ref[...] = jnp.zeros_like(bias_ref)

    linked = segq_ref[...] == segk_ref[...]
    heads = q_ref.shape[1] // HEAD_DIM
    half = STATS // 2
    dq_parts = []
    for h in range(heads):
        cols = slice(h * HEAD_DIM, (h + 1) * HEAD_DIM)
        q = q_ref[:, cols]
        k = k_ref[:, cols]
        dctx = dctx_ref[:, cols]
        s = _scores(q, k, linked)
        p = jnp.exp(s - stats_ref[:, h : h + 1]) / stats_ref[:, half + h : half + h + 1]
        dp = lax.dot_general(dctx, v_ref[:, cols], (((1,), (1,)), ((), ())), preferred_element_type=jnp.float32)
        inner = jnp.sum(p * dp, axis=1, keepdims=True)
        ds = (p * (dp - inner)).astype(jnp.bfloat16)
        dq = (jnp.dot(ds, k, preferred_element_type=jnp.float32) * SCALE).astype(dq_ref.dtype)
        dq_ref[:, cols] = dq
        dq_parts.append(dq)
        dk_acc[:, cols] += lax.dot_general(ds, q, (((0,), (0,)), ((), ())), preferred_element_type=jnp.float32)
        dv_acc[:, cols] += lax.dot_general(p.astype(jnp.bfloat16), dctx, (((0,), (0,)), ((), ())), preferred_element_type=jnp.float32)
    dq_block = jnp.concatenate(dq_parts, axis=1)
    dwq_acc[...] += lax.dot_general(x_ref[...], dq_block, (((0,), (0,)), ((), ())), preferred_element_type=jnp.float32)
    bias_ref[0:1, :] += jnp.sum(dq_block.astype(jnp.float32), axis=0, keepdims=True)

    @pl.when(step == pl.num_programs(0) - 1)
    def _():
        width = dk_ref.shape[1]
        dk = (dk_acc[...] * SCALE).astype(dk_ref.dtype)
        dv = dv_acc[...].astype(dv_ref.dtype)
        dk_ref[...] = dk
        dv_ref[...] = dv
        bias_ref[1:2, :] = jnp.sum(dv.astype(jnp.float32), axis=0, keepdims=True)
        xall = xall_ref[...]
        grads = (
            dwq_acc[...].astype(wgrad_ref.dtype),
            lax.dot_general(xall, dk, (((0,), (0,)), ((), ())),
                            preferred_element_type=jnp.float32).astype(wgrad_ref.dtype),
            lax.dot_general(xall, dv, (((0,), (0,)), ((), ())),
                            preferred_element_type=jnp.float32).astype(wgrad_ref.dtype),
            out_t_ref[...],
        )
        piece = width // parts
        for part in range(parts):
            for index, grad in enumerate(grads):
                start = (part * len(grads) + index) * piece
                wgrad_ref[:, start : start + piece] = grad[:, part * piece : (part + 1) * piece]


def attention_forward(queries, key_side, value_proj, segment_row, block=256):
    length, width = queries.shape
    segq = segment_row.reshape(length, 1)
    segk = segment_row.reshape(1, length)
    full = pl.BlockSpec((length, width), lambda i: (0, 0))
    return pl.pallas_call(
        attn_fwd_kernel,
        out_shape=(jax.ShapeDtypeStruct((length, width), jnp.bfloat16),
                   jax.ShapeDtypeStruct((length, STATS), jnp.float32)),
        grid=(length // block,),
        in_specs=[pl.BlockSpec((block, width), lambda i: (i, 0)), full, full,
                  pl.BlockSpec((block, 1), lambda i: (i, 0)),
                  pl.BlockSpec((1, length), lambda i: (0, 0))],
        out_specs=(pl.BlockSpec((block, width), lambda i: (i, 0)),
                   pl.BlockSpec((block, STATS), lambda i: (i, 0))),
        compiler_params=pltpu.CompilerParams(dimension_semantics=("arbitrary",)),
        cost_estimate=pl.CostEstimate(flops=4 * length * length * width, transcendentals=length * length * width // HEAD_DIM,
                                      bytes_accessed=8 * length * width),
    )(queries, key_side, value_proj, segq, segk)


def attention_backward(queries, key_side, value_proj, segment_row, stats, grad_context, inputs, out_t, parts,
                       block=256):
    length, width = queries.shape
    features = inputs.shape[1]
    segq = segment_row.reshape(length, 1)
    segk = segment_row.reshape(1, length)
    full = pl.BlockSpec((length, width), lambda i: (0, 0))
    rows = pl.BlockSpec((block, width), lambda i: (i, 0))
    return pl.pallas_call(
        functools.partial(attn_bwd_kernel, parts),
        out_shape=tuple(jax.ShapeDtypeStruct((length, width), jnp.bfloat16) for _ in range(3))
        + (jax.ShapeDtypeStruct((features, 4 * width), jnp.bfloat16),
           jax.ShapeDtypeStruct((8, width), jnp.float32)),
        grid=(length // block,),
        in_specs=[rows, full, full, rows,
                  pl.BlockSpec((block, 1), lambda i: (i, 0)),
                  pl.BlockSpec((1, length), lambda i: (0, 0)),
                  pl.BlockSpec((block, STATS), lambda i: (i, 0)),
                  pl.BlockSpec((block, features), lambda i: (i, 0)),
                  pl.BlockSpec((length, features), lambda i: (0, 0)),
                  pl.BlockSpec((features, width), lambda i: (0, 0))],
        out_specs=(rows, full, full,
                   pl.BlockSpec((features, 4 * width), lambda i: (0, 0)),
                   pl.BlockSpec((8, width), lambda i: (0, 0))),
        scratch_shapes=[pltpu.VMEM((length, width), jnp.float32), pltpu.VMEM((length, width), jnp.float32),
                        pltpu.VMEM((features, width), jnp.float32)],
        compiler_params=pltpu.CompilerParams(dimension_semantics=("arbitrary",), vmem_limit_bytes=60 * 1024 * 1024),
        cost_estimate=pl.CostEstimate(flops=10 * length * length * width + 6 * length * features * width,
                                      transcendentals=length * length * width // HEAD_DIM,
                                      bytes_accessed=14 * length * width + 10 * features * width),
    )(queries, key_side, value_proj, grad_context, segq, segk, stats, inputs, inputs, out_t)


def gather_shards(first_pieces, second_pieces, after=None):
    dp_count = lax.axis_size("dp")
    core = lax.rem(lax.axis_index("dp"), 2)
    first, second = jnp.stack(first_pieces), jnp.stack(second_pieces)
    mine = jnp.where(core == 0, first, second)
    gathered = lax.all_gather(mine, "tensor", axis=0, tiled=False)
    if after is not None:
        gathered, after = lax.optimization_barrier((gathered, after))
    other = lax.ppermute(gathered, "dp", perm=[(i, i ^ 1) for i in range(dp_count)])
    halves = (jnp.where(core == 0, gathered, other), jnp.where(core == 0, other, gathered))
    return [half[:, index] for half in halves for index in range(half.shape[1])]


def gather_pieces(pieces, after):
    dp_count = lax.axis_size("dp")
    part_count = lax.axis_size("tensor")
    rows = pieces[0].shape[0] // dp_count
    own = lax.dynamic_slice_in_dim(jnp.stack(pieces), lax.axis_index("dp") * rows, rows, 1)
    gathered = lax.all_gather(own, ("dp", "tensor"), axis=0, tiled=False)
    gathered, after = lax.optimization_barrier((gathered, after))
    gathered = gathered.reshape((dp_count, part_count) + own.shape)
    stacks = gathered.transpose(2, 1, 0, 3, 4).reshape(
        (len(pieces), part_count, dp_count * rows) + own.shape[2:]
    )
    return [stacks[index] for index in range(len(pieces))]


def scatter_rows(grads):
    joined = jnp.concatenate([grad.astype(jnp.bfloat16) for grad in grads], axis=1)
    return lax.psum_scatter(joined, "dp", scatter_dimension=0, tiled=True)


def part_major(grads):
    parts = lax.axis_size("tensor")
    columns = []
    for part in range(parts):
        for grad in grads:
            width = grad.shape[1] // parts
            columns.append(grad[:, part * width : (part + 1) * width].astype(jnp.bfloat16))
    return jnp.concatenate(columns, axis=1)


def scatter_parts(partials, widths):
    parts = lax.axis_size("tensor")
    joined = jnp.concatenate(
        [partial.reshape(partial.shape[0], parts, -1) for partial in partials], axis=2
    )
    summed = lax.psum_scatter(joined, "tensor", scatter_dimension=1, tiled=True)[:, 0]
    pieces = []
    start = 0
    for group in widths:
        for width in group:
            pieces.append(summed[:, start : start + width].astype(jnp.float32))
            start += width
    return pieces


def on_device(
    layer_input,
    segments,
    query_weight,
    query_bias,
    key_weight,
    value_weight,
    value_bias,
    output_weight,
    output_bias,
    first_gain,
    first_shift,
    up_weight,
    up_bias,
    down_weight,
    down_bias,
    second_gain,
    second_shift,
    output_grad,
):
    part_count = lax.axis_size("tensor")
    part_id = lax.axis_index("tensor")
    row_len = segments.shape[1]

    input_rows = lax.dynamic_slice_in_dim(layer_input, part_id * row_len, row_len, 0)
    segment_row = lax.dynamic_index_in_dim(segments, part_id, 0, keepdims=False)
    grad_out = lax.dynamic_slice_in_dim(output_grad, part_id * row_len, row_len, 0).astype(
        jnp.float32
    )

    qt_sh, kt_sh, vt_sh, o_sh = gather_shards(
        [query_weight.T, key_weight.T], [value_weight.T, output_weight]
    )
    bias_sh = lax.all_gather(
        jnp.concatenate([query_bias, value_bias, up_bias]), "tensor", axis=0, tiled=False
    )
    head_width = query_bias.shape[0]
    qb = bias_sh[:, :head_width].reshape(-1)
    vb = bias_sh[:, head_width : 2 * head_width].reshape(-1)
    ub = bias_sh[:, 2 * head_width :]
    width = qt_sh.shape[2]
    qt_full = qt_sh.reshape(-1, width)
    kt_full = kt_sh.reshape(-1, width)
    vt_full = vt_sh.reshape(-1, width)

    input_f32 = input_rows.astype(jnp.float32)
    queries = (contract_last(input_rows, qt_full) + qb).astype(jnp.bfloat16)
    key_side = contract_last(input_rows, kt_full).astype(jnp.bfloat16)
    value_proj = (contract_last(input_rows, vt_full) + vb).astype(jnp.bfloat16)
    context, softmax_stats = attention_forward(queries, key_side, value_proj, segment_row)
    u_sh, d_sh = gather_pieces([up_weight, down_weight], context)

    group_width = o_sh.shape[1]
    attn_total = input_f32
    for member in range(part_count):
        cols = slice(member * group_width, (member + 1) * group_width)
        attn_total = attn_total + product(context[:, cols], o_sh[member]).astype(
            jnp.bfloat16
        ).astype(jnp.float32)
    first_in = attn_total + output_bias
    first_out, first_unit, first_inv = normalize(first_in, first_gain, first_shift)
    first_low = first_out.astype(jnp.bfloat16)
    second_in = first_out
    pulls = []
    hidden_parts = []
    for member in range(part_count):
        pre_part = product(first_low, u_sh[member]) + ub[member]
        gelu_out, pull_gelu = jax.vjp(gelu_tanh, pre_part)
        pulls.append(pull_gelu)
        hidden_part = gelu_out.astype(jnp.bfloat16)
        hidden_parts.append(hidden_part)
        second_in = second_in + product(hidden_part, d_sh[member]).astype(
            jnp.bfloat16
        ).astype(jnp.float32)
    second_in = second_in + down_bias
    second_out, second_unit, second_inv = normalize(second_in, second_gain, second_shift)
    layer_output = second_out.astype(jnp.bfloat16)

    grad_second = normalize_back(grad_out, second_unit, second_inv, second_gain)
    grad_second_gain = jnp.sum(grad_out * second_unit, 0)
    grad_second_shift = jnp.sum(grad_out, 0)
    grad_down_bias = jnp.sum(grad_second, 0)
    down_low = grad_second.astype(jnp.bfloat16)
    first_grad = grad_second
    grad_pre_parts = []
    for member in range(part_count):
        grad_hidden = contract_last(down_low, d_sh[member])
        grad_pre = pulls[member](grad_hidden)[0].astype(jnp.bfloat16)
        grad_pre_parts.append(grad_pre)
        first_grad = first_grad + contract_last(grad_pre, u_sh[member])
    grad_pre = jnp.concatenate(grad_pre_parts, axis=1)
    hidden_low = jnp.concatenate(hidden_parts, axis=1)
    grad_up_bias = jnp.sum(grad_pre, 0, dtype=jnp.float32)
    ffn_grads = [contract_rows(first_low, grad_pre), contract_rows(down_low, hidden_low)]
    ffn_joined, first_grad = lax.optimization_barrier((part_major(ffn_grads), first_grad))
    ffn_rows = scatter_rows([ffn_joined])
    grad_first_gain = jnp.sum(first_grad * first_unit, 0)
    grad_first_shift = jnp.sum(first_grad, 0)
    attn_grad = normalize_back(first_grad, first_unit, first_inv, first_gain)
    grad_output_bias = jnp.sum(attn_grad, 0)
    attn_grad_low = attn_grad.astype(jnp.bfloat16)
    grad_context = contract_last(attn_grad_low, o_sh.reshape(-1, o_sh.shape[2])).astype(
        jnp.bfloat16
    )
    output_grad_t = contract_rows(attn_grad_low, context).astype(jnp.bfloat16)
    query_low, key_low, value_low, attn_joined, qv_bias = attention_backward(
        queries, key_side, value_proj, segment_row, softmax_stats, grad_context, input_rows,
        output_grad_t, part_count,
    )
    ffn_rows, attn_joined, qv_bias = lax.optimization_barrier((ffn_rows, attn_joined, qv_bias))
    grad_query_bias = qv_bias[0]
    grad_value_bias = qv_bias[1]
    attn_rows = scatter_rows([attn_joined])
    small = lax.psum(
        jnp.concatenate(
            [
                grad_query_bias,
                grad_value_bias,
                grad_up_bias,
                grad_output_bias,
                grad_first_gain,
                grad_first_shift,
                grad_down_bias,
                grad_second_gain,
                grad_second_shift,
            ]
        ),
        ("dp", "tensor"),
    )
    input_grad = (
        attn_grad
        + product(query_low, qt_full)
        + product(key_low, kt_full)
        + product(value_low, vt_full)
    )
    attn_rows, small, input_grad = lax.optimization_barrier((attn_rows, small, input_grad))
    ffn_width = up_weight.shape[1]
    summed = scatter_parts([ffn_rows, attn_rows], [[ffn_width] * 2, [head_width] * 4])
    split_width = 2 * head_width * part_count + up_bias.shape[0] * part_count
    split = small[:split_width]
    shared = small[split_width:].reshape(6, -1)
    device_id = lax.axis_index("dp") * part_count + part_id
    piece = shared.shape[1] // (lax.axis_size("dp") * part_count)
    shared = lax.dynamic_slice_in_dim(shared, device_id * piece, piece, 1)

    def own_block(vector, offset, width):
        return lax.dynamic_slice_in_dim(vector, offset + part_id * width, width, 0)

    query_bias_grad = own_block(split, 0, head_width)
    value_bias_grad = own_block(split, head_width * part_count, head_width)
    up_bias_grad = own_block(split, 2 * head_width * part_count, up_bias.shape[0])
    return (
        layer_output,
        input_grad,
        summed[2],
        query_bias_grad,
        summed[3],
        summed[4],
        value_bias_grad,
        summed[5].T,
        shared[0],
        shared[1],
        shared[2],
        summed[0],
        up_bias_grad,
        summed[1].T,
        shared[3],
        shared[4],
        shared[5],
    )


def solution(mesh):
    in_specs = (
        P("dp", None),
        P("dp", None),
        P(None, "tensor"),
        P("tensor"),
        P(None, "tensor"),
        P(None, "tensor"),
        P("tensor"),
        P("tensor", None),
        P(),
        P(),
        P(),
        P(None, "tensor"),
        P("tensor"),
        P("tensor", None),
        P(),
        P(),
        P(),
        P("dp", None),
    )
    out_specs = (
        P(("dp", "tensor"), None),
        P(("dp", "tensor"), None),
        P("dp", "tensor"),
        P("tensor"),
        P("dp", "tensor"),
        P("dp", "tensor"),
        P("tensor"),
        P("tensor", "dp"),
        P(("dp", "tensor")),
        P(("dp", "tensor")),
        P(("dp", "tensor")),
        P("dp", "tensor"),
        P("tensor"),
        P("tensor", "dp"),
        P(("dp", "tensor")),
        P(("dp", "tensor")),
        P(("dp", "tensor")),
    )
    return jax.shard_map(
        on_device, mesh=mesh, in_specs=in_specs, out_specs=out_specs, check_vma=False
    )
```

```python
import functools

import jax
import jax.numpy as jnp
from jax import lax
from jax.experimental import pallas as pl
from jax.experimental.pallas import tpu as pltpu
from jax.sharding import PartitionSpec as P

HEAD_DIM = 64
GROUP_HEADS = 3

norm_eps = 1e-06


def product(left_side, right_side):
    return jnp.dot(left_side, right_side, preferred_element_type=jnp.float32)


def contract_rows(left_side, right_side):
    return lax.dot_general(
        left_side, right_side, (((0,), (0,)), ((), ())), preferred_element_type=jnp.float32
    )


def contract_last(left_side, right_side):
    return lax.dot_general(
        left_side, right_side, (((1,), (1,)), ((), ())), preferred_element_type=jnp.float32
    )


def normalize(summed, norm_gain, offset):
    centred = summed - jnp.mean(summed, -1, keepdims=True)
    inverse = lax.rsqrt(jnp.mean(centred * centred, -1, keepdims=True) + norm_eps)
    scaled = centred * inverse
    return (scaled * norm_gain + offset, scaled, inverse)


def normalize_back(grad_out, scaled, inverse, norm_gain):
    grad_scaled = grad_out * norm_gain
    mean_grad = jnp.mean(grad_scaled, -1, keepdims=True)
    mean_cross = jnp.mean(grad_scaled * scaled, -1, keepdims=True)
    return inverse * (grad_scaled - mean_grad - scaled * mean_cross)


def gelu_tanh(pre_act):
    return jax.nn.gelu(pre_act, approximate=True)


SCALE = HEAD_DIM ** (-0.5)
STATS = 128


def _scores(q, k, linked):
    s = lax.dot_general(q, k, (((1,), (1,)), ((), ())), preferred_element_type=jnp.float32) * SCALE
    return jnp.where(linked, s, -1e30)


def attn_fwd_kernel(q_ref, k_ref, v_ref, segq_ref, segk_ref, ctx_ref, stats_ref):
    linked = segq_ref[...] == segk_ref[...]
    heads = q_ref.shape[1] // HEAD_DIM
    half = STATS // 2
    for h in range(heads):
        cols = slice(h * HEAD_DIM, (h + 1) * HEAD_DIM)
        s = _scores(q_ref[:, cols], k_ref[:, cols], linked)
        m = jnp.max(s, axis=1, keepdims=True)
        e = jnp.exp(s - m)
        l = jnp.sum(e, axis=1, keepdims=True)
        p = (e / l).astype(jnp.bfloat16)
        ctx = jnp.dot(p, v_ref[:, cols], preferred_element_type=jnp.float32)
        ctx_ref[:, cols] = ctx.astype(ctx_ref.dtype)
        stats_ref[:, h : h + 1] = m
        stats_ref[:, half + h : half + h + 1] = l


def attn_bwd_kernel(parts, q_ref, k_ref, v_ref, dctx_ref, segq_ref, segk_ref, stats_ref, x_ref, xall_ref,
                    out_t_ref, dq_ref, dk_ref, dv_ref, wgrad_ref, bias_ref, dk_acc, dv_acc, dwq_acc):
    step = pl.program_id(0)

    @pl.when(step == 0)
    def _():
        dk_acc[...] = jnp.zeros_like(dk_acc)
        dv_acc[...] = jnp.zeros_like(dv_acc)
        dwq_acc[...] = jnp.zeros_like(dwq_acc)
        bias_ref[...] = jnp.zeros_like(bias_ref)

    linked = segq_ref[...] == segk_ref[...]
    heads = q_ref.shape[1] // HEAD_DIM
    half = STATS // 2
    dq_parts = []
    for h in range(heads):
        cols = slice(h * HEAD_DIM, (h + 1) * HEAD_DIM)
        q = q_ref[:, cols]
        k = k_ref[:, cols]
        dctx = dctx_ref[:, cols]
        s = _scores(q, k, linked)
        p = jnp.exp(s - stats_ref[:, h : h + 1]) / stats_ref[:, half + h : half + h + 1]
        dp = lax.dot_general(dctx, v_ref[:, cols], (((1,), (1,)), ((), ())), preferred_element_type=jnp.float32)
        inner = jnp.sum(p * dp, axis=1, keepdims=True)
        ds = (p * (dp - inner)).astype(jnp.bfloat16)
        dq = (jnp.dot(ds, k, preferred_element_type=jnp.float32) * SCALE).astype(dq_ref.dtype)
        dq_ref[:, cols] = dq
        dq_parts.append(dq)
        dk_acc[:, cols] += lax.dot_general(ds, q, (((0,), (0,)), ((), ())), preferred_element_type=jnp.float32)
        dv_acc[:, cols] += lax.dot_general(p.astype(jnp.bfloat16), dctx, (((0,), (0,)), ((), ())), preferred_element_type=jnp.float32)
    dq_block = jnp.concatenate(dq_parts, axis=1)
    dwq_acc[...] += lax.dot_general(x_ref[...], dq_block, (((0,), (0,)), ((), ())), preferred_element_type=jnp.float32)
    bias_ref[0:1, :] += jnp.sum(dq_block.astype(jnp.float32), axis=0, keepdims=True)

    @pl.when(step == pl.num_programs(0) - 1)
    def _():
        width = dk_ref.shape[1]
        dk = (dk_acc[...] * SCALE).astype(dk_ref.dtype)
        dv = dv_acc[...].astype(dv_ref.dtype)
        dk_ref[...] = dk
        dv_ref[...] = dv
        bias_ref[1:2, :] = jnp.sum(dv.astype(jnp.float32), axis=0, keepdims=True)
        xall = xall_ref[...]
        grads = (
            dwq_acc[...].astype(wgrad_ref.dtype),
            lax.dot_general(xall, dk, (((0,), (0,)), ((), ())),
                            preferred_element_type=jnp.float32).astype(wgrad_ref.dtype),
            lax.dot_general(xall, dv, (((0,), (0,)), ((), ())),
                            preferred_element_type=jnp.float32).astype(wgrad_ref.dtype),
            out_t_ref[...],
        )
        piece = width // parts
        for part in range(parts):
            for index, grad in enumerate(grads):
                start = (part * len(grads) + index) * piece
                wgrad_ref[:, start : start + piece] = grad[:, part * piece : (part + 1) * piece]


def attention_forward(queries, key_side, value_proj, segment_row, block=256):
    length, width = queries.shape
    segq = segment_row.reshape(length, 1)
    segk = segment_row.reshape(1, length)
    full = pl.BlockSpec((length, width), lambda i: (0, 0))
    return pl.pallas_call(
        attn_fwd_kernel,
        out_shape=(jax.ShapeDtypeStruct((length, width), jnp.bfloat16),
                   jax.ShapeDtypeStruct((length, STATS), jnp.float32)),
        grid=(length // block,),
        in_specs=[pl.BlockSpec((block, width), lambda i: (i, 0)), full, full,
                  pl.BlockSpec((block, 1), lambda i: (i, 0)),
                  pl.BlockSpec((1, length), lambda i: (0, 0))],
        out_specs=(pl.BlockSpec((block, width), lambda i: (i, 0)),
                   pl.BlockSpec((block, STATS), lambda i: (i, 0))),
        compiler_params=pltpu.CompilerParams(dimension_semantics=("arbitrary",)),
        cost_estimate=pl.CostEstimate(flops=4 * length * length * width, transcendentals=length * length * width // HEAD_DIM,
                                      bytes_accessed=8 * length * width),
    )(queries, key_side, value_proj, segq, segk)


def attention_backward(queries, key_side, value_proj, segment_row, stats, grad_context, inputs, out_t, parts,
                       block=256):
    length, width = queries.shape
    features = inputs.shape[1]
    segq = segment_row.reshape(length, 1)
    segk = segment_row.reshape(1, length)
    full = pl.BlockSpec((length, width), lambda i: (0, 0))
    rows = pl.BlockSpec((block, width), lambda i: (i, 0))
    return pl.pallas_call(
        functools.partial(attn_bwd_kernel, parts),
        out_shape=tuple(jax.ShapeDtypeStruct((length, width), jnp.bfloat16) for _ in range(3))
        + (jax.ShapeDtypeStruct((features, 4 * width), jnp.bfloat16),
           jax.ShapeDtypeStruct((8, width), jnp.float32)),
        grid=(length // block,),
        in_specs=[rows, full, full, rows,
                  pl.BlockSpec((block, 1), lambda i: (i, 0)),
                  pl.BlockSpec((1, length), lambda i: (0, 0)),
                  pl.BlockSpec((block, STATS), lambda i: (i, 0)),
                  pl.BlockSpec((block, features), lambda i: (i, 0)),
                  pl.BlockSpec((length, features), lambda i: (0, 0)),
                  pl.BlockSpec((features, width), lambda i: (0, 0))],
        out_specs=(rows, full, full,
                   pl.BlockSpec((features, 4 * width), lambda i: (0, 0)),
                   pl.BlockSpec((8, width), lambda i: (0, 0))),
        scratch_shapes=[pltpu.VMEM((length, width), jnp.float32), pltpu.VMEM((length, width), jnp.float32),
                        pltpu.VMEM((features, width), jnp.float32)],
        compiler_params=pltpu.CompilerParams(dimension_semantics=("arbitrary",), vmem_limit_bytes=60 * 1024 * 1024),
        cost_estimate=pl.CostEstimate(flops=10 * length * length * width + 6 * length * features * width,
                                      transcendentals=length * length * width // HEAD_DIM,
                                      bytes_accessed=14 * length * width + 10 * features * width),
    )(queries, key_side, value_proj, grad_context, segq, segk, stats, inputs, inputs, out_t)


def gather_shards(first_pieces, second_pieces, extra):
    dp_count = lax.axis_size("dp")
    part_count = lax.axis_size("tensor")
    part_id = lax.axis_index("tensor")
    core = lax.rem(lax.axis_index("dp"), 2)
    first, second = jnp.stack(first_pieces), jnp.stack(second_pieces)
    mine = jnp.where(core == 0, first, second)

    def around(value):
        received = [value]
        for shift in range(1, part_count):
            perm = [(i, (i + shift) % part_count) for i in range(part_count)]
            received.append(lax.ppermute(value, "tensor", perm=perm))
        order = lax.rem(part_id - jnp.arange(part_count) + part_count, part_count)
        return jnp.take(jnp.stack(received), order, axis=0)

    gathered = around(mine)
    extras = around(extra)
    other = lax.ppermute(gathered, "dp", perm=[(i, i ^ 1) for i in range(dp_count)])
    halves = (jnp.where(core == 0, gathered, other), jnp.where(core == 0, other, gathered))
    return [half[:, index] for half in halves for index in range(half.shape[1])], extras


def gather_pieces(pieces, after):
    dp_count = lax.axis_size("dp")
    part_count = lax.axis_size("tensor")
    rows = pieces[0].shape[0] // dp_count
    own = lax.dynamic_slice_in_dim(jnp.stack(pieces), lax.axis_index("dp") * rows, rows, 1)
    gathered = lax.all_gather(own, ("dp", "tensor"), axis=0, tiled=False)
    gathered, after = lax.optimization_barrier((gathered, after))
    gathered = gathered.reshape((dp_count, part_count) + own.shape)
    stacks = gathered.transpose(2, 1, 0, 3, 4).reshape(
        (len(pieces), part_count, dp_count * rows) + own.shape[2:]
    )
    return [stacks[index] for index in range(len(pieces))]


def scatter_rows(grads):
    joined = jnp.concatenate([grad.astype(jnp.bfloat16) for grad in grads], axis=1)
    return lax.psum_scatter(joined, "dp", scatter_dimension=0, tiled=True)


def part_major(grads):
    parts = lax.axis_size("tensor")
    columns = []
    for part in range(parts):
        for grad in grads:
            width = grad.shape[1] // parts
            columns.append(grad[:, part * width : (part + 1) * width].astype(jnp.bfloat16))
    return jnp.concatenate(columns, axis=1)


def scatter_parts(partials, widths):
    parts = lax.axis_size("tensor")
    joined = jnp.concatenate(
        [partial.reshape(partial.shape[0], parts, -1) for partial in partials], axis=2
    )
    summed = lax.psum_scatter(joined, "tensor", scatter_dimension=1, tiled=True)[:, 0]
    pieces = []
    start = 0
    for group in widths:
        for width in group:
            pieces.append(summed[:, start : start + width].astype(jnp.float32))
            start += width
    return pieces


def on_device(
    layer_input,
    segments,
    query_weight,
    query_bias,
    key_weight,
    value_weight,
    value_bias,
    output_weight,
    output_bias,
    first_gain,
    first_shift,
    up_weight,
    up_bias,
    down_weight,
    down_bias,
    second_gain,
    second_shift,
    output_grad,
):
    part_count = lax.axis_size("tensor")
    part_id = lax.axis_index("tensor")
    row_len = segments.shape[1]

    input_rows = lax.dynamic_slice_in_dim(layer_input, part_id * row_len, row_len, 0)
    segment_row = lax.dynamic_index_in_dim(segments, part_id, 0, keepdims=False)
    grad_out = lax.dynamic_slice_in_dim(output_grad, part_id * row_len, row_len, 0).astype(
        jnp.float32
    )

    (qt_sh, kt_sh, vt_sh, o_sh), bias_sh = gather_shards(
        [query_weight.T, key_weight.T],
        [value_weight.T, output_weight],
        jnp.concatenate([query_bias, value_bias, up_bias]),
    )
    head_width = query_bias.shape[0]
    qb = bias_sh[:, :head_width].reshape(-1)
    vb = bias_sh[:, head_width : 2 * head_width].reshape(-1)
    ub = bias_sh[:, 2 * head_width :]
    width = qt_sh.shape[2]
    qt_full = qt_sh.reshape(-1, width)
    kt_full = kt_sh.reshape(-1, width)
    vt_full = vt_sh.reshape(-1, width)

    input_f32 = input_rows.astype(jnp.float32)
    queries = (contract_last(input_rows, qt_full) + qb).astype(jnp.bfloat16)
    key_side = contract_last(input_rows, kt_full).astype(jnp.bfloat16)
    value_proj = (contract_last(input_rows, vt_full) + vb).astype(jnp.bfloat16)
    context, softmax_stats = attention_forward(queries, key_side, value_proj, segment_row)
    u_sh, d_sh = gather_pieces([up_weight, down_weight], context)

    group_width = o_sh.shape[1]
    attn_total = input_f32
    for member in range(part_count):
        cols = slice(member * group_width, (member + 1) * group_width)
        attn_total = attn_total + product(context[:, cols], o_sh[member]).astype(
            jnp.bfloat16
        ).astype(jnp.float32)
    first_in = attn_total + output_bias
    first_out, first_unit, first_inv = normalize(first_in, first_gain, first_shift)
    first_low = first_out.astype(jnp.bfloat16)
    second_in = first_out
    pulls = []
    hidden_parts = []
    for member in range(part_count):
        pre_part = product(first_low, u_sh[member]) + ub[member]
        gelu_out, pull_gelu = jax.vjp(gelu_tanh, pre_part)
        pulls.append(pull_gelu)
        hidden_part = gelu_out.astype(jnp.bfloat16)
        hidden_parts.append(hidden_part)
        second_in = second_in + product(hidden_part, d_sh[member]).astype(
            jnp.bfloat16
        ).astype(jnp.float32)
    second_in = second_in + down_bias
    second_out, second_unit, second_inv = normalize(second_in, second_gain, second_shift)
    layer_output = second_out.astype(jnp.bfloat16)

    grad_second = normalize_back(grad_out, second_unit, second_inv, second_gain)
    grad_second_gain = jnp.sum(grad_out * second_unit, 0)
    grad_second_shift = jnp.sum(grad_out, 0)
    grad_down_bias = jnp.sum(grad_second, 0)
    down_low = grad_second.astype(jnp.bfloat16)
    first_grad = grad_second
    grad_pre_parts = []
    for member in range(part_count):
        grad_hidden = contract_last(down_low, d_sh[member])
        grad_pre = pulls[member](grad_hidden)[0].astype(jnp.bfloat16)
        grad_pre_parts.append(grad_pre)
        first_grad = first_grad + contract_last(grad_pre, u_sh[member])
    grad_pre = jnp.concatenate(grad_pre_parts, axis=1)
    hidden_low = jnp.concatenate(hidden_parts, axis=1)
    grad_up_bias = jnp.sum(grad_pre, 0, dtype=jnp.float32)
    ffn_grads = [contract_rows(first_low, grad_pre), contract_rows(down_low, hidden_low)]
    ffn_joined, first_grad = lax.optimization_barrier((part_major(ffn_grads), first_grad))
    ffn_rows = scatter_rows([ffn_joined])
    grad_first_gain = jnp.sum(first_grad * first_unit, 0)
    grad_first_shift = jnp.sum(first_grad, 0)
    attn_grad = normalize_back(first_grad, first_unit, first_inv, first_gain)
    grad_output_bias = jnp.sum(attn_grad, 0)
    attn_grad_low = attn_grad.astype(jnp.bfloat16)
    grad_context = contract_last(attn_grad_low, o_sh.reshape(-1, o_sh.shape[2])).astype(
        jnp.bfloat16
    )
    output_grad_t = contract_rows(attn_grad_low, context).astype(jnp.bfloat16)
    query_low, key_low, value_low, attn_joined, qv_bias = attention_backward(
        queries, key_side, value_proj, segment_row, softmax_stats, grad_context, input_rows,
        output_grad_t, part_count,
    )
    ffn_rows, attn_joined, qv_bias = lax.optimization_barrier((ffn_rows, attn_joined, qv_bias))
    grad_query_bias = qv_bias[0]
    grad_value_bias = qv_bias[1]
    attn_rows = scatter_rows([attn_joined])
    small = lax.psum(
        jnp.concatenate(
            [
                grad_query_bias,
                grad_value_bias,
                grad_up_bias,
                grad_output_bias,
                grad_first_gain,
                grad_first_shift,
                grad_down_bias,
                grad_second_gain,
                grad_second_shift,
            ]
        ),
        ("dp", "tensor"),
    )
    input_grad = (
        attn_grad
        + product(query_low, qt_full)
        + product(key_low, kt_full)
        + product(value_low, vt_full)
    )
    attn_rows, small, input_grad = lax.optimization_barrier((attn_rows, small, input_grad))
    ffn_width = up_weight.shape[1]
    summed = scatter_parts([ffn_rows, attn_rows], [[ffn_width] * 2, [head_width] * 4])
    split_width = 2 * head_width * part_count + up_bias.shape[0] * part_count
    split = small[:split_width]
    shared = small[split_width:].reshape(6, -1)
    device_id = lax.axis_index("dp") * part_count + part_id
    piece = shared.shape[1] // (lax.axis_size("dp") * part_count)
    shared = lax.dynamic_slice_in_dim(shared, device_id * piece, piece, 1)

    def own_block(vector, offset, width):
        return lax.dynamic_slice_in_dim(vector, offset + part_id * width, width, 0)

    query_bias_grad = own_block(split, 0, head_width)
    value_bias_grad = own_block(split, head_width * part_count, head_width)
    up_bias_grad = own_block(split, 2 * head_width * part_count, up_bias.shape[0])
    return (
        layer_output,
        input_grad,
        summed[2],
        query_bias_grad,
        summed[3],
        summed[4],
        value_bias_grad,
        summed[5].T,
        shared[0],
        shared[1],
        shared[2],
        summed[0],
        up_bias_grad,
        summed[1].T,
        shared[3],
        shared[4],
        shared[5],
    )


def solution(mesh):
    in_specs = (
        P("dp", None),
        P("dp", None),
        P(None, "tensor"),
        P("tensor"),
        P(None, "tensor"),
        P(None, "tensor"),
        P("tensor"),
        P("tensor", None),
        P(),
        P(),
        P(),
        P(None, "tensor"),
        P("tensor"),
        P("tensor", None),
        P(),
        P(),
        P(),
        P("dp", None),
    )
    out_specs = (
        P(("dp", "tensor"), None),
        P(("dp", "tensor"), None),
        P("dp", "tensor"),
        P("tensor"),
        P("dp", "tensor"),
        P("dp", "tensor"),
        P("tensor"),
        P("tensor", "dp"),
        P(("dp", "tensor")),
        P(("dp", "tensor")),
        P(("dp", "tensor")),
        P("dp", "tensor"),
        P("tensor"),
        P("tensor", "dp"),
        P(("dp", "tensor")),
        P(("dp", "tensor")),
        P(("dp", "tensor")),
    )
    return jax.shard_map(
        on_device, mesh=mesh, in_specs=in_specs, out_specs=out_specs, check_vma=False
    )
```

```python
import functools

import jax
import jax.numpy as jnp
from jax import lax
from jax.experimental import pallas as pl
from jax.experimental.pallas import tpu as pltpu
from jax.sharding import PartitionSpec as P

HEAD_DIM = 64
GROUP_HEADS = 3

norm_eps = 1e-06


def product(left_side, right_side):
    return jnp.dot(left_side, right_side, preferred_element_type=jnp.float32)


def contract_rows(left_side, right_side):
    return lax.dot_general(
        left_side, right_side, (((0,), (0,)), ((), ())), preferred_element_type=jnp.float32
    )


def contract_last(left_side, right_side):
    return lax.dot_general(
        left_side, right_side, (((1,), (1,)), ((), ())), preferred_element_type=jnp.float32
    )


def normalize(summed, norm_gain, offset):
    centred = summed - jnp.mean(summed, -1, keepdims=True)
    inverse = lax.rsqrt(jnp.mean(centred * centred, -1, keepdims=True) + norm_eps)
    scaled = centred * inverse
    return (scaled * norm_gain + offset, scaled, inverse)


def normalize_back(grad_out, scaled, inverse, norm_gain):
    grad_scaled = grad_out * norm_gain
    mean_grad = jnp.mean(grad_scaled, -1, keepdims=True)
    mean_cross = jnp.mean(grad_scaled * scaled, -1, keepdims=True)
    return inverse * (grad_scaled - mean_grad - scaled * mean_cross)


def gelu_tanh(pre_act):
    return jax.nn.gelu(pre_act, approximate=True)


SCALE = HEAD_DIM ** (-0.5)
STATS = 128


def _scores(q, k, linked):
    s = lax.dot_general(q, k, (((1,), (1,)), ((), ())), preferred_element_type=jnp.float32) * SCALE
    return jnp.where(linked, s, -1e30)


def attn_fwd_kernel(q_ref, k_ref, v_ref, segq_ref, segk_ref, ctx_ref, stats_ref):
    linked = segq_ref[...] == segk_ref[...]
    heads = q_ref.shape[1] // HEAD_DIM
    half = STATS // 2
    for h in range(heads):
        cols = slice(h * HEAD_DIM, (h + 1) * HEAD_DIM)
        s = _scores(q_ref[:, cols], k_ref[:, cols], linked)
        m = jnp.max(s, axis=1, keepdims=True)
        e = jnp.exp(s - m)
        l = jnp.sum(e, axis=1, keepdims=True)
        p = (e / l).astype(jnp.bfloat16)
        ctx = jnp.dot(p, v_ref[:, cols], preferred_element_type=jnp.float32)
        ctx_ref[:, cols] = ctx.astype(ctx_ref.dtype)
        stats_ref[:, h : h + 1] = m
        stats_ref[:, half + h : half + h + 1] = l


def attn_bwd_kernel(parts, q_ref, k_ref, v_ref, dctx_ref, segq_ref, segk_ref, stats_ref, x_ref, xall_ref,
                    out_t_ref, dq_ref, dk_ref, dv_ref, wgrad_ref, bias_ref, dk_acc, dv_acc, dwq_acc):
    step = pl.program_id(0)

    @pl.when(step == 0)
    def _():
        dk_acc[...] = jnp.zeros_like(dk_acc)
        dv_acc[...] = jnp.zeros_like(dv_acc)
        dwq_acc[...] = jnp.zeros_like(dwq_acc)
        bias_ref[...] = jnp.zeros_like(bias_ref)

    linked = segq_ref[...] == segk_ref[...]
    heads = q_ref.shape[1] // HEAD_DIM
    half = STATS // 2
    dq_parts = []
    for h in range(heads):
        cols = slice(h * HEAD_DIM, (h + 1) * HEAD_DIM)
        q = q_ref[:, cols]
        k = k_ref[:, cols]
        dctx = dctx_ref[:, cols]
        s = _scores(q, k, linked)
        p = jnp.exp(s - stats_ref[:, h : h + 1]) / stats_ref[:, half + h : half + h + 1]
        dp = lax.dot_general(dctx, v_ref[:, cols], (((1,), (1,)), ((), ())), preferred_element_type=jnp.float32)
        inner = jnp.sum(p * dp, axis=1, keepdims=True)
        ds = (p * (dp - inner)).astype(jnp.bfloat16)
        dq = (jnp.dot(ds, k, preferred_element_type=jnp.float32) * SCALE).astype(dq_ref.dtype)
        dq_ref[:, cols] = dq
        dq_parts.append(dq)
        dk_acc[:, cols] += lax.dot_general(ds, q, (((0,), (0,)), ((), ())), preferred_element_type=jnp.float32)
        dv_acc[:, cols] += lax.dot_general(p.astype(jnp.bfloat16), dctx, (((0,), (0,)), ((), ())), preferred_element_type=jnp.float32)
    dq_block = jnp.concatenate(dq_parts, axis=1)
    dwq_acc[...] += lax.dot_general(x_ref[...], dq_block, (((0,), (0,)), ((), ())), preferred_element_type=jnp.float32)
    bias_ref[0:1, :] += jnp.sum(dq_block.astype(jnp.float32), axis=0, keepdims=True)

    @pl.when(step == pl.num_programs(0) - 1)
    def _():
        width = dk_ref.shape[1]
        dk = (dk_acc[...] * SCALE).astype(dk_ref.dtype)
        dv = dv_acc[...].astype(dv_ref.dtype)
        dk_ref[...] = dk
        dv_ref[...] = dv
        bias_ref[1:2, :] = jnp.sum(dv.astype(jnp.float32), axis=0, keepdims=True)
        xall = xall_ref[...]
        grads = (
            dwq_acc[...].astype(wgrad_ref.dtype),
            lax.dot_general(xall, dk, (((0,), (0,)), ((), ())),
                            preferred_element_type=jnp.float32).astype(wgrad_ref.dtype),
            lax.dot_general(xall, dv, (((0,), (0,)), ((), ())),
                            preferred_element_type=jnp.float32).astype(wgrad_ref.dtype),
            out_t_ref[...],
        )
        piece = width // parts
        for part in range(parts):
            for index, grad in enumerate(grads):
                start = (part * len(grads) + index) * piece
                wgrad_ref[:, start : start + piece] = grad[:, part * piece : (part + 1) * piece]


def attention_forward(queries, key_side, value_proj, segment_row, block=256):
    length, width = queries.shape
    segq = segment_row.reshape(length, 1)
    segk = segment_row.reshape(1, length)
    full = pl.BlockSpec((length, width), lambda i: (0, 0))
    return pl.pallas_call(
        attn_fwd_kernel,
        out_shape=(jax.ShapeDtypeStruct((length, width), jnp.bfloat16),
                   jax.ShapeDtypeStruct((length, STATS), jnp.float32)),
        grid=(length // block,),
        in_specs=[pl.BlockSpec((block, width), lambda i: (i, 0)), full, full,
                  pl.BlockSpec((block, 1), lambda i: (i, 0)),
                  pl.BlockSpec((1, length), lambda i: (0, 0))],
        out_specs=(pl.BlockSpec((block, width), lambda i: (i, 0)),
                   pl.BlockSpec((block, STATS), lambda i: (i, 0))),
        compiler_params=pltpu.CompilerParams(dimension_semantics=("arbitrary",)),
        cost_estimate=pl.CostEstimate(flops=4 * length * length * width, transcendentals=length * length * width // HEAD_DIM,
                                      bytes_accessed=8 * length * width),
    )(queries, key_side, value_proj, segq, segk)


def attention_backward(queries, key_side, value_proj, segment_row, stats, grad_context, inputs, out_t, parts,
                       block=256):
    length, width = queries.shape
    features = inputs.shape[1]
    segq = segment_row.reshape(length, 1)
    segk = segment_row.reshape(1, length)
    full = pl.BlockSpec((length, width), lambda i: (0, 0))
    rows = pl.BlockSpec((block, width), lambda i: (i, 0))
    return pl.pallas_call(
        functools.partial(attn_bwd_kernel, parts),
        out_shape=tuple(jax.ShapeDtypeStruct((length, width), jnp.bfloat16) for _ in range(3))
        + (jax.ShapeDtypeStruct((features, 4 * width), jnp.bfloat16),
           jax.ShapeDtypeStruct((8, width), jnp.float32)),
        grid=(length // block,),
        in_specs=[rows, full, full, rows,
                  pl.BlockSpec((block, 1), lambda i: (i, 0)),
                  pl.BlockSpec((1, length), lambda i: (0, 0)),
                  pl.BlockSpec((block, STATS), lambda i: (i, 0)),
                  pl.BlockSpec((block, features), lambda i: (i, 0)),
                  pl.BlockSpec((length, features), lambda i: (0, 0)),
                  pl.BlockSpec((features, width), lambda i: (0, 0))],
        out_specs=(rows, full, full,
                   pl.BlockSpec((features, 4 * width), lambda i: (0, 0)),
                   pl.BlockSpec((8, width), lambda i: (0, 0))),
        scratch_shapes=[pltpu.VMEM((length, width), jnp.float32), pltpu.VMEM((length, width), jnp.float32),
                        pltpu.VMEM((features, width), jnp.float32)],
        compiler_params=pltpu.CompilerParams(dimension_semantics=("arbitrary",), vmem_limit_bytes=60 * 1024 * 1024),
        cost_estimate=pl.CostEstimate(flops=10 * length * length * width + 6 * length * features * width,
                                      transcendentals=length * length * width // HEAD_DIM,
                                      bytes_accessed=14 * length * width + 10 * features * width),
    )(queries, key_side, value_proj, grad_context, segq, segk, stats, inputs, inputs, out_t)


def gather_shards(first_pieces, second_pieces, after=None):
    dp_count = lax.axis_size("dp")
    core = lax.rem(lax.axis_index("dp"), 2)
    first, second = jnp.stack(first_pieces), jnp.stack(second_pieces)
    mine = jnp.where(core == 0, first, second)
    gathered = lax.all_gather(mine, "tensor", axis=0, tiled=False)
    if after is not None:
        gathered, after = lax.optimization_barrier((gathered, after))
    other = lax.ppermute(gathered, "dp", perm=[(i, i ^ 1) for i in range(dp_count)])
    halves = (jnp.where(core == 0, gathered, other), jnp.where(core == 0, other, gathered))
    return [half[:, index] for half in halves for index in range(half.shape[1])]


def gather_pieces(pieces, after):
    dp_count = lax.axis_size("dp")
    part_count = lax.axis_size("tensor")
    rows = pieces[0].shape[0] // dp_count
    own = lax.dynamic_slice_in_dim(jnp.stack(pieces), lax.axis_index("dp") * rows, rows, 1)
    gathered = lax.all_gather(own, ("dp", "tensor"), axis=0, tiled=False)
    gathered, after = lax.optimization_barrier((gathered, after))
    gathered = gathered.reshape((dp_count, part_count) + own.shape)
    stacks = gathered.transpose(2, 1, 0, 3, 4).reshape(
        (len(pieces), part_count, dp_count * rows) + own.shape[2:]
    )
    return [stacks[index] for index in range(len(pieces))]


def scatter_rows(grads):
    joined = jnp.concatenate([grad.astype(jnp.bfloat16) for grad in grads], axis=1)
    return lax.psum_scatter(joined, "dp", scatter_dimension=0, tiled=True)


def part_major(grads):
    parts = lax.axis_size("tensor")
    columns = []
    for part in range(parts):
        for grad in grads:
            width = grad.shape[1] // parts
            columns.append(grad[:, part * width : (part + 1) * width].astype(jnp.bfloat16))
    return jnp.concatenate(columns, axis=1)


def scatter_parts(partials, widths):
    parts = lax.axis_size("tensor")
    joined = jnp.concatenate(
        [partial.reshape(partial.shape[0], parts, -1) for partial in partials], axis=2
    )
    summed = lax.psum_scatter(joined, "tensor", scatter_dimension=1, tiled=True)[:, 0]
    pieces = []
    start = 0
    for group in widths:
        for width in group:
            pieces.append(summed[:, start : start + width].astype(jnp.float32))
            start += width
    return pieces


def on_device(
    layer_input,
    segments,
    query_weight,
    query_bias,
    key_weight,
    value_weight,
    value_bias,
    output_weight,
    output_bias,
    first_gain,
    first_shift,
    up_weight,
    up_bias,
    down_weight,
    down_bias,
    second_gain,
    second_shift,
    output_grad,
):
    part_count = lax.axis_size("tensor")
    part_id = lax.axis_index("tensor")
    row_len = segments.shape[1]

    input_rows = lax.dynamic_slice_in_dim(layer_input, part_id * row_len, row_len, 0)
    segment_row = lax.dynamic_index_in_dim(segments, part_id, 0, keepdims=False)
    grad_out = lax.dynamic_slice_in_dim(output_grad, part_id * row_len, row_len, 0).astype(
        jnp.float32
    )

    qt_sh, kt_sh, vt_sh, o_sh = gather_shards(
        [query_weight.T, key_weight.T], [value_weight.T, output_weight]
    )
    bias_sh = lax.all_gather(
        jnp.concatenate([query_bias, value_bias, up_bias]), "tensor", axis=0, tiled=False
    )
    head_width = query_bias.shape[0]
    qb = bias_sh[:, :head_width].reshape(-1)
    vb = bias_sh[:, head_width : 2 * head_width].reshape(-1)
    ub = bias_sh[:, 2 * head_width :]
    width = qt_sh.shape[2]
    qt_full = qt_sh.reshape(-1, width)
    kt_full = kt_sh.reshape(-1, width)
    vt_full = vt_sh.reshape(-1, width)

    input_f32 = input_rows.astype(jnp.float32)
    queries = (contract_last(input_rows, qt_full) + qb).astype(jnp.bfloat16)
    key_side = contract_last(input_rows, kt_full).astype(jnp.bfloat16)
    value_proj = (contract_last(input_rows, vt_full) + vb).astype(jnp.bfloat16)
    context, softmax_stats = attention_forward(queries, key_side, value_proj, segment_row)
    u_sh, d_sh = gather_pieces([up_weight, down_weight], context)

    group_width = o_sh.shape[1]
    attn_total = input_f32
    for member in range(part_count):
        cols = slice(member * group_width, (member + 1) * group_width)
        attn_total = attn_total + product(context[:, cols], o_sh[member]).astype(
            jnp.bfloat16
        ).astype(jnp.float32)
    first_in = attn_total + output_bias
    first_out, first_unit, first_inv = normalize(first_in, first_gain, first_shift)
    first_low = first_out.astype(jnp.bfloat16)
    second_in = first_out
    pulls = []
    hidden_parts = []
    for member in range(part_count):
        pre_part = product(first_low, u_sh[member]) + ub[member]
        gelu_out, pull_gelu = jax.vjp(gelu_tanh, pre_part)
        pulls.append(pull_gelu)
        hidden_part = gelu_out.astype(jnp.bfloat16)
        hidden_parts.append(hidden_part)
        second_in = second_in + product(hidden_part, d_sh[member]).astype(
            jnp.bfloat16
        ).astype(jnp.float32)
    second_in = second_in + down_bias
    second_out, second_unit, second_inv = normalize(second_in, second_gain, second_shift)
    layer_output = second_out.astype(jnp.bfloat16)

    grad_second = normalize_back(grad_out, second_unit, second_inv, second_gain)
    grad_second_gain = jnp.sum(grad_out * second_unit, 0)
    grad_second_shift = jnp.sum(grad_out, 0)
    grad_down_bias = jnp.sum(grad_second, 0)
    down_low = grad_second.astype(jnp.bfloat16)
    first_grad = grad_second
    grad_pre_parts = []
    for member in range(part_count):
        grad_hidden = contract_last(down_low, d_sh[member])
        grad_pre = pulls[member](grad_hidden)[0].astype(jnp.bfloat16)
        grad_pre_parts.append(grad_pre)
        first_grad = first_grad + contract_last(grad_pre, u_sh[member])
    grad_pre = jnp.concatenate(grad_pre_parts, axis=1)
    hidden_low = jnp.concatenate(hidden_parts, axis=1)
    grad_up_bias = jnp.sum(grad_pre, 0, dtype=jnp.float32)
    ffn_grads = [contract_rows(first_low, grad_pre), contract_rows(down_low, hidden_low)]
    ffn_joined, first_grad = lax.optimization_barrier((part_major(ffn_grads), first_grad))
    ffn_rows = scatter_rows([ffn_joined])
    grad_first_gain = jnp.sum(first_grad * first_unit, 0)
    grad_first_shift = jnp.sum(first_grad, 0)
    attn_grad = normalize_back(first_grad, first_unit, first_inv, first_gain)
    grad_output_bias = jnp.sum(attn_grad, 0)
    attn_grad_low = attn_grad.astype(jnp.bfloat16)
    grad_context = contract_last(attn_grad_low, o_sh.reshape(-1, o_sh.shape[2])).astype(
        jnp.bfloat16
    )
    output_grad_t = contract_rows(attn_grad_low, context).astype(jnp.bfloat16)
    query_low, key_low, value_low, attn_joined, qv_bias = attention_backward(
        queries, key_side, value_proj, segment_row, softmax_stats, grad_context, input_rows,
        output_grad_t, part_count,
    )
    ffn_rows, attn_joined, qv_bias = lax.optimization_barrier((ffn_rows, attn_joined, qv_bias))
    grad_query_bias = qv_bias[0]
    grad_value_bias = qv_bias[1]
    attn_rows = scatter_rows([attn_joined])
    small = lax.psum(
        jnp.concatenate(
            [
                grad_query_bias,
                grad_value_bias,
                grad_up_bias,
                grad_output_bias,
                grad_first_gain,
                grad_first_shift,
                grad_down_bias,
                grad_second_gain,
                grad_second_shift,
            ]
        ),
        ("dp", "tensor"),
    )
    small, query_low, key_low, value_low = lax.optimization_barrier(
        (small, query_low, key_low, value_low)
    )
    input_grad = (
        attn_grad
        + product(query_low, qt_full)
        + product(key_low, kt_full)
        + product(value_low, vt_full)
    )
    attn_rows, small, input_grad = lax.optimization_barrier((attn_rows, small, input_grad))
    ffn_width = up_weight.shape[1]
    summed = scatter_parts([ffn_rows, attn_rows], [[ffn_width] * 2, [head_width] * 4])
    split_width = 2 * head_width * part_count + up_bias.shape[0] * part_count
    split = small[:split_width]
    shared = small[split_width:].reshape(6, -1)
    device_id = lax.axis_index("dp") * part_count + part_id
    piece = shared.shape[1] // (lax.axis_size("dp") * part_count)
    shared = lax.dynamic_slice_in_dim(shared, device_id * piece, piece, 1)

    def own_block(vector, offset, width):
        return lax.dynamic_slice_in_dim(vector, offset + part_id * width, width, 0)

    query_bias_grad = own_block(split, 0, head_width)
    value_bias_grad = own_block(split, head_width * part_count, head_width)
    up_bias_grad = own_block(split, 2 * head_width * part_count, up_bias.shape[0])
    return (
        layer_output,
        input_grad,
        summed[2],
        query_bias_grad,
        summed[3],
        summed[4],
        value_bias_grad,
        summed[5].T,
        shared[0],
        shared[1],
        shared[2],
        summed[0],
        up_bias_grad,
        summed[1].T,
        shared[3],
        shared[4],
        shared[5],
    )


def solution(mesh):
    in_specs = (
        P("dp", None),
        P("dp", None),
        P(None, "tensor"),
        P("tensor"),
        P(None, "tensor"),
        P(None, "tensor"),
        P("tensor"),
        P("tensor", None),
        P(),
        P(),
        P(),
        P(None, "tensor"),
        P("tensor"),
        P("tensor", None),
        P(),
        P(),
        P(),
        P("dp", None),
    )
    out_specs = (
        P(("dp", "tensor"), None),
        P(("dp", "tensor"), None),
        P("dp", "tensor"),
        P("tensor"),
        P("dp", "tensor"),
        P("dp", "tensor"),
        P("tensor"),
        P("tensor", "dp"),
        P(("dp", "tensor")),
        P(("dp", "tensor")),
        P(("dp", "tensor")),
        P("dp", "tensor"),
        P("tensor"),
        P("tensor", "dp"),
        P(("dp", "tensor")),
        P(("dp", "tensor")),
        P(("dp", "tensor")),
    )
    return jax.shard_map(
        on_device, mesh=mesh, in_specs=in_specs, out_specs=out_specs, check_vma=False
    )
```

```python
import functools

import jax
import jax.numpy as jnp
from jax import lax
from jax.experimental import pallas as pl
from jax.experimental.pallas import tpu as pltpu
from jax.sharding import PartitionSpec as P

HEAD_DIM = 64
GROUP_HEADS = 3

norm_eps = 1e-06


def product(left_side, right_side):
    return jnp.dot(left_side, right_side, preferred_element_type=jnp.float32)


def contract_rows(left_side, right_side):
    return lax.dot_general(
        left_side, right_side, (((0,), (0,)), ((), ())), preferred_element_type=jnp.float32
    )


def contract_last(left_side, right_side):
    return lax.dot_general(
        left_side, right_side, (((1,), (1,)), ((), ())), preferred_element_type=jnp.float32
    )


def normalize(summed, norm_gain, offset):
    centred = summed - jnp.mean(summed, -1, keepdims=True)
    inverse = lax.rsqrt(jnp.mean(centred * centred, -1, keepdims=True) + norm_eps)
    scaled = centred * inverse
    return (scaled * norm_gain + offset, scaled, inverse)


def normalize_back(grad_out, scaled, inverse, norm_gain):
    grad_scaled = grad_out * norm_gain
    mean_grad = jnp.mean(grad_scaled, -1, keepdims=True)
    mean_cross = jnp.mean(grad_scaled * scaled, -1, keepdims=True)
    return inverse * (grad_scaled - mean_grad - scaled * mean_cross)


def gelu_tanh(pre_act):
    return jax.nn.gelu(pre_act, approximate=True)


SCALE = HEAD_DIM ** (-0.5)
STATS = 128


def _scores(q, k, linked):
    s = lax.dot_general(q, k, (((1,), (1,)), ((), ())), preferred_element_type=jnp.float32) * SCALE
    return jnp.where(linked, s, -1e30)


def attn_fwd_kernel(q_ref, k_ref, v_ref, segq_ref, segk_ref, ctx_ref, stats_ref):
    linked = segq_ref[...] == segk_ref[...]
    heads = q_ref.shape[1] // HEAD_DIM
    half = STATS // 2
    for h in range(heads):
        cols = slice(h * HEAD_DIM, (h + 1) * HEAD_DIM)
        s = _scores(q_ref[:, cols], k_ref[:, cols], linked)
        m = jnp.max(s, axis=1, keepdims=True)
        e = jnp.exp(s - m)
        l = jnp.sum(e, axis=1, keepdims=True)
        p = (e / l).astype(jnp.bfloat16)
        ctx = jnp.dot(p, v_ref[:, cols], preferred_element_type=jnp.float32)
        ctx_ref[:, cols] = ctx.astype(ctx_ref.dtype)
        stats_ref[:, h : h + 1] = m
        stats_ref[:, half + h : half + h + 1] = l


def attn_bwd_kernel(parts, q_ref, k_ref, v_ref, dctx_ref, segq_ref, segk_ref, stats_ref, x_ref, xall_ref,
                    out_t_ref, dq_ref, dk_ref, dv_ref, wgrad_ref, bias_ref, dk_acc, dv_acc, dwq_acc):
    step = pl.program_id(0)

    @pl.when(step == 0)
    def _():
        dk_acc[...] = jnp.zeros_like(dk_acc)
        dv_acc[...] = jnp.zeros_like(dv_acc)
        dwq_acc[...] = jnp.zeros_like(dwq_acc)
        bias_ref[...] = jnp.zeros_like(bias_ref)

    linked = segq_ref[...] == segk_ref[...]
    heads = q_ref.shape[1] // HEAD_DIM
    half = STATS // 2
    dq_parts = []
    for h in range(heads):
        cols = slice(h * HEAD_DIM, (h + 1) * HEAD_DIM)
        q = q_ref[:, cols]
        k = k_ref[:, cols]
        dctx = dctx_ref[:, cols]
        s = _scores(q, k, linked)
        p = jnp.exp(s - stats_ref[:, h : h + 1]) / stats_ref[:, half + h : half + h + 1]
        dp = lax.dot_general(dctx, v_ref[:, cols], (((1,), (1,)), ((), ())), preferred_element_type=jnp.float32)
        inner = jnp.sum(p * dp, axis=1, keepdims=True)
        ds = (p * (dp - inner)).astype(jnp.bfloat16)
        dq = (jnp.dot(ds, k, preferred_element_type=jnp.float32) * SCALE).astype(dq_ref.dtype)
        dq_ref[:, cols] = dq
        dq_parts.append(dq)
        dk_acc[:, cols] += lax.dot_general(ds, q, (((0,), (0,)), ((), ())), preferred_element_type=jnp.float32)
        dv_acc[:, cols] += lax.dot_general(p.astype(jnp.bfloat16), dctx, (((0,), (0,)), ((), ())), preferred_element_type=jnp.float32)
    dq_block = jnp.concatenate(dq_parts, axis=1)
    dwq_acc[...] += lax.dot_general(x_ref[...], dq_block, (((0,), (0,)), ((), ())), preferred_element_type=jnp.float32)
    bias_ref[0:1, :] += jnp.sum(dq_block.astype(jnp.float32), axis=0, keepdims=True)

    @pl.when(step == pl.num_programs(0) - 1)
    def _():
        width = dk_ref.shape[1]
        dk = (dk_acc[...] * SCALE).astype(dk_ref.dtype)
        dv = dv_acc[...].astype(dv_ref.dtype)
        dk_ref[...] = dk
        dv_ref[...] = dv
        bias_ref[1:2, :] = jnp.sum(dv.astype(jnp.float32), axis=0, keepdims=True)
        xall = xall_ref[...]
        grads = (
            dwq_acc[...].astype(wgrad_ref.dtype),
            lax.dot_general(xall, dk, (((0,), (0,)), ((), ())),
                            preferred_element_type=jnp.float32).astype(wgrad_ref.dtype),
            lax.dot_general(xall, dv, (((0,), (0,)), ((), ())),
                            preferred_element_type=jnp.float32).astype(wgrad_ref.dtype),
            out_t_ref[...],
        )
        piece = width // parts
        for part in range(parts):
            for index, grad in enumerate(grads):
                start = (part * len(grads) + index) * piece
                wgrad_ref[:, start : start + piece] = grad[:, part * piece : (part + 1) * piece]


def attention_forward(queries, key_side, value_proj, segment_row, block=256):
    length, width = queries.shape
    segq = segment_row.reshape(length, 1)
    segk = segment_row.reshape(1, length)
    full = pl.BlockSpec((length, width), lambda i: (0, 0))
    return pl.pallas_call(
        attn_fwd_kernel,
        out_shape=(jax.ShapeDtypeStruct((length, width), jnp.bfloat16),
                   jax.ShapeDtypeStruct((length, STATS), jnp.float32)),
        grid=(length // block,),
        in_specs=[pl.BlockSpec((block, width), lambda i: (i, 0)), full, full,
                  pl.BlockSpec((block, 1), lambda i: (i, 0)),
                  pl.BlockSpec((1, length), lambda i: (0, 0))],
        out_specs=(pl.BlockSpec((block, width), lambda i: (i, 0)),
                   pl.BlockSpec((block, STATS), lambda i: (i, 0))),
        compiler_params=pltpu.CompilerParams(dimension_semantics=("arbitrary",)),
        cost_estimate=pl.CostEstimate(flops=4 * length * length * width, transcendentals=length * length * width // HEAD_DIM,
                                      bytes_accessed=8 * length * width),
    )(queries, key_side, value_proj, segq, segk)


def attention_backward(queries, key_side, value_proj, segment_row, stats, grad_context, inputs, out_t, parts,
                       block=256):
    length, width = queries.shape
    features = inputs.shape[1]
    segq = segment_row.reshape(length, 1)
    segk = segment_row.reshape(1, length)
    full = pl.BlockSpec((length, width), lambda i: (0, 0))
    rows = pl.BlockSpec((block, width), lambda i: (i, 0))
    return pl.pallas_call(
        functools.partial(attn_bwd_kernel, parts),
        out_shape=tuple(jax.ShapeDtypeStruct((length, width), jnp.bfloat16) for _ in range(3))
        + (jax.ShapeDtypeStruct((features, 4 * width), jnp.bfloat16),
           jax.ShapeDtypeStruct((8, width), jnp.float32)),
        grid=(length // block,),
        in_specs=[rows, full, full, rows,
                  pl.BlockSpec((block, 1), lambda i: (i, 0)),
                  pl.BlockSpec((1, length), lambda i: (0, 0)),
                  pl.BlockSpec((block, STATS), lambda i: (i, 0)),
                  pl.BlockSpec((block, features), lambda i: (i, 0)),
                  pl.BlockSpec((length, features), lambda i: (0, 0)),
                  pl.BlockSpec((features, width), lambda i: (0, 0))],
        out_specs=(rows, full, full,
                   pl.BlockSpec((features, 4 * width), lambda i: (0, 0)),
                   pl.BlockSpec((8, width), lambda i: (0, 0))),
        scratch_shapes=[pltpu.VMEM((length, width), jnp.float32), pltpu.VMEM((length, width), jnp.float32),
                        pltpu.VMEM((features, width), jnp.float32)],
        compiler_params=pltpu.CompilerParams(dimension_semantics=("arbitrary",), vmem_limit_bytes=60 * 1024 * 1024),
        cost_estimate=pl.CostEstimate(flops=10 * length * length * width + 6 * length * features * width,
                                      transcendentals=length * length * width // HEAD_DIM,
                                      bytes_accessed=14 * length * width + 10 * features * width),
    )(queries, key_side, value_proj, grad_context, segq, segk, stats, inputs, inputs, out_t)


def gather_shards(first_pieces, second_pieces, after=None):
    dp_count = lax.axis_size("dp")
    core = lax.rem(lax.axis_index("dp"), 2)
    first, second = jnp.stack(first_pieces), jnp.stack(second_pieces)
    mine = jnp.where(core == 0, first, second)
    gathered = lax.all_gather(mine, "tensor", axis=0, tiled=False)
    if after is not None:
        gathered, after = lax.optimization_barrier((gathered, after))
    other = lax.ppermute(gathered, "dp", perm=[(i, i ^ 1) for i in range(dp_count)])
    halves = (jnp.where(core == 0, gathered, other), jnp.where(core == 0, other, gathered))
    return [half[:, index] for half in halves for index in range(half.shape[1])]


def gather_pieces(pieces, after):
    dp_count = lax.axis_size("dp")
    part_count = lax.axis_size("tensor")
    rows = pieces[0].shape[0] // dp_count
    own = lax.dynamic_slice_in_dim(jnp.stack(pieces), lax.axis_index("dp") * rows, rows, 1)
    gathered = lax.all_gather(own, ("dp", "tensor"), axis=0, tiled=False)
    gathered, after = lax.optimization_barrier((gathered, after))
    gathered = gathered.reshape((dp_count, part_count) + own.shape)
    stacks = gathered.transpose(2, 1, 0, 3, 4).reshape(
        (len(pieces), part_count, dp_count * rows) + own.shape[2:]
    )
    return [stacks[index] for index in range(len(pieces))]


def scatter_rows(grads):
    joined = jnp.concatenate([grad.astype(jnp.bfloat16) for grad in grads], axis=1)
    return lax.psum_scatter(joined, "dp", scatter_dimension=0, tiled=True)


def part_major(grads):
    parts = lax.axis_size("tensor")
    columns = []
    for part in range(parts):
        for grad in grads:
            width = grad.shape[1] // parts
            columns.append(grad[:, part * width : (part + 1) * width].astype(jnp.bfloat16))
    return jnp.concatenate(columns, axis=1)


def scatter_parts(partials, widths):
    parts = lax.axis_size("tensor")
    joined = jnp.concatenate(
        [partial.reshape(partial.shape[0], parts, -1) for partial in partials], axis=2
    )
    summed = lax.psum_scatter(joined, "tensor", scatter_dimension=1, tiled=True)[:, 0]
    pieces = []
    start = 0
    for group in widths:
        for width in group:
            pieces.append(summed[:, start : start + width].astype(jnp.float32))
            start += width
    return pieces


def on_device(
    layer_input,
    segments,
    query_weight,
    query_bias,
    key_weight,
    value_weight,
    value_bias,
    output_weight,
    output_bias,
    first_gain,
    first_shift,
    up_weight,
    up_bias,
    down_weight,
    down_bias,
    second_gain,
    second_shift,
    output_grad,
):
    part_count = lax.axis_size("tensor")
    part_id = lax.axis_index("tensor")
    row_len = segments.shape[1]

    input_rows = lax.dynamic_slice_in_dim(layer_input, part_id * row_len, row_len, 0)
    segment_row = lax.dynamic_index_in_dim(segments, part_id, 0, keepdims=False)
    grad_out = lax.dynamic_slice_in_dim(output_grad, part_id * row_len, row_len, 0).astype(
        jnp.float32
    )

    qt_sh, kt_sh, vt_sh, o_sh = gather_shards(
        [query_weight.T, key_weight.T], [value_weight.T, output_weight]
    )
    bias_sh = lax.all_gather(
        jnp.concatenate([query_bias, value_bias, up_bias]), "tensor", axis=0, tiled=False
    )
    head_width = query_bias.shape[0]
    qb = bias_sh[:, :head_width].reshape(-1)
    vb = bias_sh[:, head_width : 2 * head_width].reshape(-1)
    ub = bias_sh[:, 2 * head_width :]
    width = qt_sh.shape[2]
    qt_full = qt_sh.reshape(-1, width)
    kt_full = kt_sh.reshape(-1, width)
    vt_full = vt_sh.reshape(-1, width)

    input_f32 = input_rows.astype(jnp.float32)
    queries = (contract_last(input_rows, qt_full) + qb).astype(jnp.bfloat16)
    key_side = contract_last(input_rows, kt_full).astype(jnp.bfloat16)
    value_proj = (contract_last(input_rows, vt_full) + vb).astype(jnp.bfloat16)
    context, softmax_stats = attention_forward(queries, key_side, value_proj, segment_row)
    u_sh, d_sh = gather_pieces([up_weight, down_weight], context)

    group_width = o_sh.shape[1]
    attn_total = input_f32
    for member in range(part_count):
        cols = slice(member * group_width, (member + 1) * group_width)
        attn_total = attn_total + product(context[:, cols], o_sh[member]).astype(
            jnp.bfloat16
        ).astype(jnp.float32)
    first_in = attn_total + output_bias
    first_out, first_unit, first_inv = normalize(first_in, first_gain, first_shift)
    first_low = first_out.astype(jnp.bfloat16)
    second_in = first_out
    pulls = []
    hidden_parts = []
    for member in range(part_count):
        pre_part = product(first_low, u_sh[member]) + ub[member]
        gelu_out, pull_gelu = jax.vjp(gelu_tanh, pre_part)
        pulls.append(pull_gelu)
        hidden_part = gelu_out.astype(jnp.bfloat16)
        hidden_parts.append(hidden_part)
        second_in = second_in + product(hidden_part, d_sh[member]).astype(
            jnp.bfloat16
        ).astype(jnp.float32)
    second_in = second_in + down_bias
    second_out, second_unit, second_inv = normalize(second_in, second_gain, second_shift)
    layer_output = second_out.astype(jnp.bfloat16)

    grad_second = normalize_back(grad_out, second_unit, second_inv, second_gain)
    grad_second_gain = jnp.sum(grad_out * second_unit, 0)
    grad_second_shift = jnp.sum(grad_out, 0)
    grad_down_bias = jnp.sum(grad_second, 0)
    down_low = grad_second.astype(jnp.bfloat16)
    first_grad = grad_second
    grad_pre_parts = []
    for member in range(part_count):
        grad_hidden = contract_last(down_low, d_sh[member])
        grad_pre = pulls[member](grad_hidden)[0].astype(jnp.bfloat16)
        grad_pre_parts.append(grad_pre)
        first_grad = first_grad + contract_last(grad_pre, u_sh[member])
    grad_pre = jnp.concatenate(grad_pre_parts, axis=1)
    hidden_low = jnp.concatenate(hidden_parts, axis=1)
    grad_up_bias = jnp.sum(grad_pre, 0, dtype=jnp.float32)
    ffn_grads = [contract_rows(first_low, grad_pre), contract_rows(down_low, hidden_low)]
    ffn_joined, first_grad = lax.optimization_barrier(
        (jnp.stack([grad.astype(jnp.bfloat16) for grad in ffn_grads]), first_grad)
    )
    ffn_rows = lax.psum_scatter(ffn_joined, "dp", scatter_dimension=1, tiled=True)
    grad_first_gain = jnp.sum(first_grad * first_unit, 0)
    grad_first_shift = jnp.sum(first_grad, 0)
    attn_grad = normalize_back(first_grad, first_unit, first_inv, first_gain)
    grad_output_bias = jnp.sum(attn_grad, 0)
    attn_grad_low = attn_grad.astype(jnp.bfloat16)
    grad_context = contract_last(attn_grad_low, o_sh.reshape(-1, o_sh.shape[2])).astype(
        jnp.bfloat16
    )
    output_grad_t = contract_rows(attn_grad_low, context).astype(jnp.bfloat16)
    query_low, key_low, value_low, attn_joined, qv_bias = attention_backward(
        queries, key_side, value_proj, segment_row, softmax_stats, grad_context, input_rows,
        output_grad_t, part_count,
    )
    ffn_rows, attn_joined, qv_bias = lax.optimization_barrier((ffn_rows, attn_joined, qv_bias))
    grad_query_bias = qv_bias[0]
    grad_value_bias = qv_bias[1]
    attn_rows = scatter_rows([attn_joined])
    small = lax.psum(
        jnp.concatenate(
            [
                grad_query_bias,
                grad_value_bias,
                grad_up_bias,
                grad_output_bias,
                grad_first_gain,
                grad_first_shift,
                grad_down_bias,
                grad_second_gain,
                grad_second_shift,
            ]
        ),
        ("dp", "tensor"),
    )
    small, query_low, key_low, value_low = lax.optimization_barrier(
        (small, query_low, key_low, value_low)
    )
    input_grad = (
        attn_grad
        + product(query_low, qt_full)
        + product(key_low, kt_full)
        + product(value_low, vt_full)
    )
    attn_rows, small, input_grad = lax.optimization_barrier((attn_rows, small, input_grad))
    ffn_width = up_weight.shape[1]
    grads_count, ffn_rows_count, _ = ffn_rows.shape
    ffn_rows = ffn_rows.reshape(grads_count, ffn_rows_count, part_count, -1).transpose(1, 2, 0, 3)
    ffn_rows = ffn_rows.reshape(ffn_rows_count, -1)
    summed = scatter_parts([ffn_rows, attn_rows], [[ffn_width] * 2, [head_width] * 4])
    split_width = 2 * head_width * part_count + up_bias.shape[0] * part_count
    split = small[:split_width]
    shared = small[split_width:].reshape(6, -1)
    device_id = lax.axis_index("dp") * part_count + part_id
    piece = shared.shape[1] // (lax.axis_size("dp") * part_count)
    shared = lax.dynamic_slice_in_dim(shared, device_id * piece, piece, 1)

    def own_block(vector, offset, width):
        return lax.dynamic_slice_in_dim(vector, offset + part_id * width, width, 0)

    query_bias_grad = own_block(split, 0, head_width)
    value_bias_grad = own_block(split, head_width * part_count, head_width)
    up_bias_grad = own_block(split, 2 * head_width * part_count, up_bias.shape[0])
    return (
        layer_output,
        input_grad,
        summed[2],
        query_bias_grad,
        summed[3],
        summed[4],
        value_bias_grad,
        summed[5].T,
        shared[0],
        shared[1],
        shared[2],
        summed[0],
        up_bias_grad,
        summed[1].T,
        shared[3],
        shared[4],
        shared[5],
    )


def solution(mesh):
    in_specs = (
        P("dp", None),
        P("dp", None),
        P(None, "tensor"),
        P("tensor"),
        P(None, "tensor"),
        P(None, "tensor"),
        P("tensor"),
        P("tensor", None),
        P(),
        P(),
        P(),
        P(None, "tensor"),
        P("tensor"),
        P("tensor", None),
        P(),
        P(),
        P(),
        P("dp", None),
    )
    out_specs = (
        P(("dp", "tensor"), None),
        P(("dp", "tensor"), None),
        P("dp", "tensor"),
        P("tensor"),
        P("dp", "tensor"),
        P("dp", "tensor"),
        P("tensor"),
        P("tensor", "dp"),
        P(("dp", "tensor")),
        P(("dp", "tensor")),
        P(("dp", "tensor")),
        P("dp", "tensor"),
        P("tensor"),
        P("tensor", "dp"),
        P(("dp", "tensor")),
        P(("dp", "tensor")),
        P(("dp", "tensor")),
    )
    return jax.shard_map(
        on_device, mesh=mesh, in_specs=in_specs, out_specs=out_specs, check_vma=False
    )
```

```python
import functools

import jax
import jax.numpy as jnp
from jax import lax
from jax.experimental import pallas as pl
from jax.experimental.pallas import tpu as pltpu
from jax.sharding import PartitionSpec as P

HEAD_DIM = 64
GROUP_HEADS = 3

norm_eps = 1e-06


def product(left_side, right_side):
    return jnp.dot(left_side, right_side, preferred_element_type=jnp.float32)


def contract_rows(left_side, right_side):
    return lax.dot_general(
        left_side, right_side, (((0,), (0,)), ((), ())), preferred_element_type=jnp.float32
    )


def contract_last(left_side, right_side):
    return lax.dot_general(
        left_side, right_side, (((1,), (1,)), ((), ())), preferred_element_type=jnp.float32
    )


def normalize(summed, norm_gain, offset):
    centred = summed - jnp.mean(summed, -1, keepdims=True)
    inverse = lax.rsqrt(jnp.mean(centred * centred, -1, keepdims=True) + norm_eps)
    scaled = centred * inverse
    return (scaled * norm_gain + offset, scaled, inverse)


def normalize_back(grad_out, scaled, inverse, norm_gain):
    grad_scaled = grad_out * norm_gain
    mean_grad = jnp.mean(grad_scaled, -1, keepdims=True)
    mean_cross = jnp.mean(grad_scaled * scaled, -1, keepdims=True)
    return inverse * (grad_scaled - mean_grad - scaled * mean_cross)


def gelu_tanh(pre_act):
    return jax.nn.gelu(pre_act, approximate=True)


SCALE = HEAD_DIM ** (-0.5)
STATS = 128


def _scores(q, k, linked):
    s = lax.dot_general(q, k, (((1,), (1,)), ((), ())), preferred_element_type=jnp.float32) * SCALE
    return jnp.where(linked, s, -1e30)


def attn_fwd_kernel(q_ref, k_ref, v_ref, segq_ref, segk_ref, ctx_ref, stats_ref):
    linked = segq_ref[...] == segk_ref[...]
    heads = q_ref.shape[1] // HEAD_DIM
    half = STATS // 2
    for h in range(heads):
        cols = slice(h * HEAD_DIM, (h + 1) * HEAD_DIM)
        s = _scores(q_ref[:, cols], k_ref[:, cols], linked)
        m = jnp.max(s, axis=1, keepdims=True)
        e = jnp.exp(s - m)
        l = jnp.sum(e, axis=1, keepdims=True)
        p = (e / l).astype(jnp.bfloat16)
        ctx = jnp.dot(p, v_ref[:, cols], preferred_element_type=jnp.float32)
        ctx_ref[:, cols] = ctx.astype(ctx_ref.dtype)
        stats_ref[:, h : h + 1] = m
        stats_ref[:, half + h : half + h + 1] = l


def attn_bwd_kernel(parts, q_ref, k_ref, v_ref, dctx_ref, segq_ref, segk_ref, stats_ref, x_ref, xall_ref,
                    out_t_ref, dq_ref, dk_ref, dv_ref, wgrad_ref, bias_ref, dk_acc, dv_acc, dwq_acc):
    step = pl.program_id(0)

    @pl.when(step == 0)
    def _():
        dk_acc[...] = jnp.zeros_like(dk_acc)
        dv_acc[...] = jnp.zeros_like(dv_acc)
        dwq_acc[...] = jnp.zeros_like(dwq_acc)
        bias_ref[...] = jnp.zeros_like(bias_ref)

    linked = segq_ref[...] == segk_ref[...]
    heads = q_ref.shape[1] // HEAD_DIM
    half = STATS // 2
    dq_parts = []
    for h in range(heads):
        cols = slice(h * HEAD_DIM, (h + 1) * HEAD_DIM)
        q = q_ref[:, cols]
        k = k_ref[:, cols]
        dctx = dctx_ref[:, cols]
        s = _scores(q, k, linked)
        p = jnp.exp(s - stats_ref[:, h : h + 1]) / stats_ref[:, half + h : half + h + 1]
        dp = lax.dot_general(dctx, v_ref[:, cols], (((1,), (1,)), ((), ())), preferred_element_type=jnp.float32)
        inner = jnp.sum(p * dp, axis=1, keepdims=True)
        ds = (p * (dp - inner)).astype(jnp.bfloat16)
        dq = (jnp.dot(ds, k, preferred_element_type=jnp.float32) * SCALE).astype(dq_ref.dtype)
        dq_ref[:, cols] = dq
        dq_parts.append(dq)
        dk_acc[:, cols] += lax.dot_general(ds, q, (((0,), (0,)), ((), ())), preferred_element_type=jnp.float32)
        dv_acc[:, cols] += lax.dot_general(p.astype(jnp.bfloat16), dctx, (((0,), (0,)), ((), ())), preferred_element_type=jnp.float32)
    dq_block = jnp.concatenate(dq_parts, axis=1)
    dwq_acc[...] += lax.dot_general(x_ref[...], dq_block, (((0,), (0,)), ((), ())), preferred_element_type=jnp.float32)
    bias_ref[0:1, :] += jnp.sum(dq_block.astype(jnp.float32), axis=0, keepdims=True)

    @pl.when(step == pl.num_programs(0) - 1)
    def _():
        width = dk_ref.shape[1]
        dk = (dk_acc[...] * SCALE).astype(dk_ref.dtype)
        dv = dv_acc[...].astype(dv_ref.dtype)
        dk_ref[...] = dk
        dv_ref[...] = dv
        bias_ref[1:2, :] = jnp.sum(dv.astype(jnp.float32), axis=0, keepdims=True)
        xall = xall_ref[...]
        grads = (
            dwq_acc[...].astype(wgrad_ref.dtype),
            lax.dot_general(xall, dk, (((0,), (0,)), ((), ())),
                            preferred_element_type=jnp.float32).astype(wgrad_ref.dtype),
            lax.dot_general(xall, dv, (((0,), (0,)), ((), ())),
                            preferred_element_type=jnp.float32).astype(wgrad_ref.dtype),
            out_t_ref[...],
        )
        piece = width // parts
        for part in range(parts):
            for index, grad in enumerate(grads):
                start = (part * len(grads) + index) * piece
                wgrad_ref[:, start : start + piece] = grad[:, part * piece : (part + 1) * piece]


def attention_forward(queries, key_side, value_proj, segment_row, block=256):
    length, width = queries.shape
    segq = segment_row.reshape(length, 1)
    segk = segment_row.reshape(1, length)
    full = pl.BlockSpec((length, width), lambda i: (0, 0))
    return pl.pallas_call(
        attn_fwd_kernel,
        out_shape=(jax.ShapeDtypeStruct((length, width), jnp.bfloat16),
                   jax.ShapeDtypeStruct((length, STATS), jnp.float32)),
        grid=(length // block,),
        in_specs=[pl.BlockSpec((block, width), lambda i: (i, 0)), full, full,
                  pl.BlockSpec((block, 1), lambda i: (i, 0)),
                  pl.BlockSpec((1, length), lambda i: (0, 0))],
        out_specs=(pl.BlockSpec((block, width), lambda i: (i, 0)),
                   pl.BlockSpec((block, STATS), lambda i: (i, 0))),
        compiler_params=pltpu.CompilerParams(dimension_semantics=("arbitrary",)),
        cost_estimate=pl.CostEstimate(flops=4 * length * length * width, transcendentals=length * length * width // HEAD_DIM,
                                      bytes_accessed=8 * length * width),
    )(queries, key_side, value_proj, segq, segk)


def attention_backward(queries, key_side, value_proj, segment_row, stats, grad_context, inputs, out_t, parts,
                       block=256):
    length, width = queries.shape
    features = inputs.shape[1]
    segq = segment_row.reshape(length, 1)
    segk = segment_row.reshape(1, length)
    full = pl.BlockSpec((length, width), lambda i: (0, 0))
    rows = pl.BlockSpec((block, width), lambda i: (i, 0))
    return pl.pallas_call(
        functools.partial(attn_bwd_kernel, parts),
        out_shape=tuple(jax.ShapeDtypeStruct((length, width), jnp.bfloat16) for _ in range(3))
        + (jax.ShapeDtypeStruct((features, 4 * width), jnp.bfloat16),
           jax.ShapeDtypeStruct((8, width), jnp.float32)),
        grid=(length // block,),
        in_specs=[rows, full, full, rows,
                  pl.BlockSpec((block, 1), lambda i: (i, 0)),
                  pl.BlockSpec((1, length), lambda i: (0, 0)),
                  pl.BlockSpec((block, STATS), lambda i: (i, 0)),
                  pl.BlockSpec((block, features), lambda i: (i, 0)),
                  pl.BlockSpec((length, features), lambda i: (0, 0)),
                  pl.BlockSpec((features, width), lambda i: (0, 0))],
        out_specs=(rows, full, full,
                   pl.BlockSpec((features, 4 * width), lambda i: (0, 0)),
                   pl.BlockSpec((8, width), lambda i: (0, 0))),
        scratch_shapes=[pltpu.VMEM((length, width), jnp.float32), pltpu.VMEM((length, width), jnp.float32),
                        pltpu.VMEM((features, width), jnp.float32)],
        compiler_params=pltpu.CompilerParams(dimension_semantics=("arbitrary",), vmem_limit_bytes=60 * 1024 * 1024),
        cost_estimate=pl.CostEstimate(flops=10 * length * length * width + 6 * length * features * width,
                                      transcendentals=length * length * width // HEAD_DIM,
                                      bytes_accessed=14 * length * width + 10 * features * width),
    )(queries, key_side, value_proj, grad_context, segq, segk, stats, inputs, inputs, out_t)


def gather_shards(first_pieces, second_pieces, after=None):
    dp_count = lax.axis_size("dp")
    core = lax.rem(lax.axis_index("dp"), 2)
    first, second = jnp.stack(first_pieces), jnp.stack(second_pieces)
    mine = jnp.where(core == 0, first, second)
    gathered = lax.all_gather(mine, "tensor", axis=0, tiled=False)
    if after is not None:
        gathered, after = lax.optimization_barrier((gathered, after))
    other = lax.ppermute(gathered, "dp", perm=[(i, i ^ 1) for i in range(dp_count)])
    halves = (jnp.where(core == 0, gathered, other), jnp.where(core == 0, other, gathered))
    return [half[:, index] for half in halves for index in range(half.shape[1])]


def gather_pieces(pieces, after):
    dp_count = lax.axis_size("dp")
    part_count = lax.axis_size("tensor")
    rows = pieces[0].shape[0] // dp_count
    own = lax.dynamic_slice_in_dim(jnp.stack(pieces), lax.axis_index("dp") * rows, rows, 1)
    gathered = lax.all_gather(own, ("dp", "tensor"), axis=0, tiled=False)
    gathered, after = lax.optimization_barrier((gathered, after))
    gathered = gathered.reshape((dp_count, part_count) + own.shape)
    stacks = gathered.transpose(2, 1, 0, 3, 4).reshape(
        (len(pieces), part_count, dp_count * rows) + own.shape[2:]
    )
    return [stacks[index] for index in range(len(pieces))]


def scatter_rows(grads):
    joined = jnp.concatenate([grad.astype(jnp.bfloat16) for grad in grads], axis=1)
    return lax.psum_scatter(joined, "dp", scatter_dimension=0, tiled=True)


def part_major(grads):
    parts = lax.axis_size("tensor")
    columns = []
    for part in range(parts):
        for grad in grads:
            width = grad.shape[1] // parts
            columns.append(grad[:, part * width : (part + 1) * width].astype(jnp.bfloat16))
    return jnp.concatenate(columns, axis=1)


def scatter_parts(partials, widths):
    parts = lax.axis_size("tensor")
    joined = jnp.concatenate(
        [partial.reshape(partial.shape[0], parts, -1) for partial in partials], axis=2
    )
    summed = lax.psum_scatter(joined, "tensor", scatter_dimension=1, tiled=True)[:, 0]
    pieces = []
    start = 0
    for group in widths:
        for width in group:
            pieces.append(summed[:, start : start + width].astype(jnp.float32))
            start += width
    return pieces


def on_device(
    layer_input,
    segments,
    query_weight,
    query_bias,
    key_weight,
    value_weight,
    value_bias,
    output_weight,
    output_bias,
    first_gain,
    first_shift,
    up_weight,
    up_bias,
    down_weight,
    down_bias,
    second_gain,
    second_shift,
    output_grad,
):
    part_count = lax.axis_size("tensor")
    part_id = lax.axis_index("tensor")
    row_len = segments.shape[1]

    input_rows = lax.dynamic_slice_in_dim(layer_input, part_id * row_len, row_len, 0)
    segment_row = lax.dynamic_index_in_dim(segments, part_id, 0, keepdims=False)
    grad_out = lax.dynamic_slice_in_dim(output_grad, part_id * row_len, row_len, 0).astype(
        jnp.float32
    )

    qt_sh, kt_sh, vt_sh, o_sh = gather_shards(
        [query_weight.T, key_weight.T], [value_weight.T, output_weight]
    )
    bias_sh = lax.all_gather(
        jnp.concatenate([query_bias, value_bias, up_bias]), "tensor", axis=0, tiled=False
    )
    head_width = query_bias.shape[0]
    qb = bias_sh[:, :head_width].reshape(-1)
    vb = bias_sh[:, head_width : 2 * head_width].reshape(-1)
    ub = bias_sh[:, 2 * head_width :]
    width = qt_sh.shape[2]
    qt_full = qt_sh.reshape(-1, width)
    kt_full = kt_sh.reshape(-1, width)
    vt_full = vt_sh.reshape(-1, width)

    input_f32 = input_rows.astype(jnp.float32)
    queries = (contract_last(input_rows, qt_full) + qb).astype(jnp.bfloat16)
    key_side = contract_last(input_rows, kt_full).astype(jnp.bfloat16)
    value_proj = (contract_last(input_rows, vt_full) + vb).astype(jnp.bfloat16)
    context, softmax_stats = attention_forward(queries, key_side, value_proj, segment_row)
    u_sh, d_sh = gather_pieces([up_weight, down_weight], context)

    group_width = o_sh.shape[1]
    attn_total = input_f32
    for member in range(part_count):
        cols = slice(member * group_width, (member + 1) * group_width)
        attn_total = attn_total + product(context[:, cols], o_sh[member]).astype(
            jnp.bfloat16
        ).astype(jnp.float32)
    first_in = attn_total + output_bias
    first_out, first_unit, first_inv = normalize(first_in, first_gain, first_shift)
    first_low = first_out.astype(jnp.bfloat16)
    second_in = first_out
    pulls = []
    hidden_parts = []
    for member in range(part_count):
        pre_part = product(first_low, u_sh[member]) + ub[member]
        gelu_out, pull_gelu = jax.vjp(gelu_tanh, pre_part)
        pulls.append(pull_gelu)
        hidden_part = gelu_out.astype(jnp.bfloat16)
        hidden_parts.append(hidden_part)
        second_in = second_in + product(hidden_part, d_sh[member]).astype(
            jnp.bfloat16
        ).astype(jnp.float32)
    second_in = second_in + down_bias
    second_out, second_unit, second_inv = normalize(second_in, second_gain, second_shift)
    layer_output = second_out.astype(jnp.bfloat16)

    grad_second = normalize_back(grad_out, second_unit, second_inv, second_gain)
    grad_second_gain = jnp.sum(grad_out * second_unit, 0)
    grad_second_shift = jnp.sum(grad_out, 0)
    grad_down_bias = jnp.sum(grad_second, 0)
    down_low = grad_second.astype(jnp.bfloat16)
    first_grad = grad_second
    grad_pre_parts = []
    for member in range(part_count):
        grad_hidden = contract_last(down_low, d_sh[member])
        grad_pre_parts.append(pulls[member](grad_hidden)[0].astype(jnp.bfloat16))
    grad_pre_parts = lax.optimization_barrier(grad_pre_parts)
    for member in range(part_count):
        first_grad = first_grad + contract_last(grad_pre_parts[member], u_sh[member])
    grad_pre = jnp.concatenate(grad_pre_parts, axis=1)
    hidden_low = jnp.concatenate(hidden_parts, axis=1)
    grad_up_bias = jnp.sum(grad_pre, 0, dtype=jnp.float32)
    ffn_grads = [contract_rows(first_low, grad_pre), contract_rows(down_low, hidden_low)]
    ffn_joined, first_grad = lax.optimization_barrier((part_major(ffn_grads), first_grad))
    ffn_rows = scatter_rows([ffn_joined])
    grad_first_gain = jnp.sum(first_grad * first_unit, 0)
    grad_first_shift = jnp.sum(first_grad, 0)
    attn_grad = normalize_back(first_grad, first_unit, first_inv, first_gain)
    grad_output_bias = jnp.sum(attn_grad, 0)
    attn_grad_low = attn_grad.astype(jnp.bfloat16)
    grad_context = contract_last(attn_grad_low, o_sh.reshape(-1, o_sh.shape[2])).astype(
        jnp.bfloat16
    )
    output_grad_t = contract_rows(attn_grad_low, context).astype(jnp.bfloat16)
    query_low, key_low, value_low, attn_joined, qv_bias = attention_backward(
        queries, key_side, value_proj, segment_row, softmax_stats, grad_context, input_rows,
        output_grad_t, part_count,
    )
    ffn_rows, attn_joined, qv_bias = lax.optimization_barrier((ffn_rows, attn_joined, qv_bias))
    grad_query_bias = qv_bias[0]
    grad_value_bias = qv_bias[1]
    attn_rows = scatter_rows([attn_joined])
    small = lax.psum(
        jnp.concatenate(
            [
                grad_query_bias,
                grad_value_bias,
                grad_up_bias,
                grad_output_bias,
                grad_first_gain,
                grad_first_shift,
                grad_down_bias,
                grad_second_gain,
                grad_second_shift,
            ]
        ),
        ("dp", "tensor"),
    )
    small, query_low, key_low, value_low = lax.optimization_barrier(
        (small, query_low, key_low, value_low)
    )
    input_grad = (
        attn_grad
        + product(query_low, qt_full)
        + product(key_low, kt_full)
        + product(value_low, vt_full)
    )
    attn_rows, small, input_grad = lax.optimization_barrier((attn_rows, small, input_grad))
    ffn_width = up_weight.shape[1]
    summed = scatter_parts([ffn_rows, attn_rows], [[ffn_width] * 2, [head_width] * 4])
    split_width = 2 * head_width * part_count + up_bias.shape[0] * part_count
    split = small[:split_width]
    shared = small[split_width:].reshape(6, -1)
    device_id = lax.axis_index("dp") * part_count + part_id
    piece = shared.shape[1] // (lax.axis_size("dp") * part_count)
    shared = lax.dynamic_slice_in_dim(shared, device_id * piece, piece, 1)

    def own_block(vector, offset, width):
        return lax.dynamic_slice_in_dim(vector, offset + part_id * width, width, 0)

    query_bias_grad = own_block(split, 0, head_width)
    value_bias_grad = own_block(split, head_width * part_count, head_width)
    up_bias_grad = own_block(split, 2 * head_width * part_count, up_bias.shape[0])
    return (
        layer_output,
        input_grad,
        summed[2],
        query_bias_grad,
        summed[3],
        summed[4],
        value_bias_grad,
        summed[5].T,
        shared[0],
        shared[1],
        shared[2],
        summed[0],
        up_bias_grad,
        summed[1].T,
        shared[3],
        shared[4],
        shared[5],
    )


def solution(mesh):
    in_specs = (
        P("dp", None),
        P("dp", None),
        P(None, "tensor"),
        P("tensor"),
        P(None, "tensor"),
        P(None, "tensor"),
        P("tensor"),
        P("tensor", None),
        P(),
        P(),
        P(),
        P(None, "tensor"),
        P("tensor"),
        P("tensor", None),
        P(),
        P(),
        P(),
        P("dp", None),
    )
    out_specs = (
        P(("dp", "tensor"), None),
        P(("dp", "tensor"), None),
        P("dp", "tensor"),
        P("tensor"),
        P("dp", "tensor"),
        P("dp", "tensor"),
        P("tensor"),
        P("tensor", "dp"),
        P(("dp", "tensor")),
        P(("dp", "tensor")),
        P(("dp", "tensor")),
        P("dp", "tensor"),
        P("tensor"),
        P("tensor", "dp"),
        P(("dp", "tensor")),
        P(("dp", "tensor")),
        P(("dp", "tensor")),
    )
    return jax.shard_map(
        on_device, mesh=mesh, in_specs=in_specs, out_specs=out_specs, check_vma=False
    )
```

```python
import functools

import jax
import jax.numpy as jnp
from jax import lax
from jax.experimental import pallas as pl
from jax.experimental.pallas import tpu as pltpu
from jax.sharding import PartitionSpec as P

HEAD_DIM = 64
GROUP_HEADS = 3

norm_eps = 1e-06


def product(left_side, right_side):
    return jnp.dot(left_side, right_side, preferred_element_type=jnp.float32)


def contract_rows(left_side, right_side):
    return lax.dot_general(
        left_side, right_side, (((0,), (0,)), ((), ())), preferred_element_type=jnp.float32
    )


def contract_last(left_side, right_side):
    return lax.dot_general(
        left_side, right_side, (((1,), (1,)), ((), ())), preferred_element_type=jnp.float32
    )


def normalize(summed, norm_gain, offset):
    centred = summed - jnp.mean(summed, -1, keepdims=True)
    inverse = lax.rsqrt(jnp.mean(centred * centred, -1, keepdims=True) + norm_eps)
    scaled = centred * inverse
    return (scaled * norm_gain + offset, scaled, inverse)


def normalize_back(grad_out, scaled, inverse, norm_gain):
    grad_scaled = grad_out * norm_gain
    mean_grad = jnp.mean(grad_scaled, -1, keepdims=True)
    mean_cross = jnp.mean(grad_scaled * scaled, -1, keepdims=True)
    return inverse * (grad_scaled - mean_grad - scaled * mean_cross)


def gelu_tanh(pre_act):
    return jax.nn.gelu(pre_act, approximate=True)


SCALE = HEAD_DIM ** (-0.5)
STATS = 128


def _scores(q, k, linked):
    s = lax.dot_general(q, k, (((1,), (1,)), ((), ())), preferred_element_type=jnp.float32) * SCALE
    return jnp.where(linked, s, -1e30)


def attn_fwd_kernel(q_ref, k_ref, v_ref, segq_ref, segk_ref, ctx_ref, stats_ref):
    linked = segq_ref[...] == segk_ref[...]
    heads = q_ref.shape[1] // HEAD_DIM
    half = STATS // 2
    for h in range(heads):
        cols = slice(h * HEAD_DIM, (h + 1) * HEAD_DIM)
        s = _scores(q_ref[:, cols], k_ref[:, cols], linked)
        m = jnp.max(s, axis=1, keepdims=True)
        e = jnp.exp(s - m)
        l = jnp.sum(e, axis=1, keepdims=True)
        p = (e / l).astype(jnp.bfloat16)
        ctx = jnp.dot(p, v_ref[:, cols], preferred_element_type=jnp.float32)
        ctx_ref[:, cols] = ctx.astype(ctx_ref.dtype)
        stats_ref[:, h : h + 1] = m
        stats_ref[:, half + h : half + h + 1] = l


def attn_bwd_kernel(parts, q_ref, k_ref, v_ref, dctx_ref, segq_ref, segk_ref, stats_ref, x_ref, xall_ref,
                    out_t_ref, dq_ref, dk_ref, dv_ref, wgrad_ref, bias_ref, dk_acc, dv_acc, dwq_acc):
    step = pl.program_id(0)

    @pl.when(step == 0)
    def _():
        dk_acc[...] = jnp.zeros_like(dk_acc)
        dv_acc[...] = jnp.zeros_like(dv_acc)
        dwq_acc[...] = jnp.zeros_like(dwq_acc)
        bias_ref[...] = jnp.zeros_like(bias_ref)

    linked = segq_ref[...] == segk_ref[...]
    heads = q_ref.shape[1] // HEAD_DIM
    half = STATS // 2
    dq_parts = []
    for h in range(heads):
        cols = slice(h * HEAD_DIM, (h + 1) * HEAD_DIM)
        q = q_ref[:, cols]
        k = k_ref[:, cols]
        dctx = dctx_ref[:, cols]
        s = _scores(q, k, linked)
        p = jnp.exp(s - stats_ref[:, h : h + 1]) / stats_ref[:, half + h : half + h + 1]
        dp = lax.dot_general(dctx, v_ref[:, cols], (((1,), (1,)), ((), ())), preferred_element_type=jnp.float32)
        inner = jnp.sum(p * dp, axis=1, keepdims=True)
        ds = (p * (dp - inner)).astype(jnp.bfloat16)
        dq = (jnp.dot(ds, k, preferred_element_type=jnp.float32) * SCALE).astype(dq_ref.dtype)
        dq_ref[:, cols] = dq
        dq_parts.append(dq)
        dk_acc[:, cols] += lax.dot_general(ds, q, (((0,), (0,)), ((), ())), preferred_element_type=jnp.float32)
        dv_acc[:, cols] += lax.dot_general(p.astype(jnp.bfloat16), dctx, (((0,), (0,)), ((), ())), preferred_element_type=jnp.float32)
    dq_block = jnp.concatenate(dq_parts, axis=1)
    dwq_acc[...] += lax.dot_general(x_ref[...], dq_block, (((0,), (0,)), ((), ())), preferred_element_type=jnp.float32)
    bias_ref[0:1, :] += jnp.sum(dq_block.astype(jnp.float32), axis=0, keepdims=True)

    @pl.when(step == pl.num_programs(0) - 1)
    def _():
        width = dk_ref.shape[1]
        dk = (dk_acc[...] * SCALE).astype(dk_ref.dtype)
        dv = dv_acc[...].astype(dv_ref.dtype)
        dk_ref[...] = dk
        dv_ref[...] = dv
        bias_ref[1:2, :] = jnp.sum(dv.astype(jnp.float32), axis=0, keepdims=True)
        xall = xall_ref[...]
        grads = (
            dwq_acc[...].astype(wgrad_ref.dtype),
            lax.dot_general(xall, dk, (((0,), (0,)), ((), ())),
                            preferred_element_type=jnp.float32).astype(wgrad_ref.dtype),
            lax.dot_general(xall, dv, (((0,), (0,)), ((), ())),
                            preferred_element_type=jnp.float32).astype(wgrad_ref.dtype),
            out_t_ref[...],
        )
        piece = width // parts
        for part in range(parts):
            for index, grad in enumerate(grads):
                start = (part * len(grads) + index) * piece
                wgrad_ref[:, start : start + piece] = grad[:, part * piece : (part + 1) * piece]


def attention_forward(queries, key_side, value_proj, segment_row, block=256):
    length, width = queries.shape
    segq = segment_row.reshape(length, 1)
    segk = segment_row.reshape(1, length)
    full = pl.BlockSpec((length, width), lambda i: (0, 0))
    return pl.pallas_call(
        attn_fwd_kernel,
        out_shape=(jax.ShapeDtypeStruct((length, width), jnp.bfloat16),
                   jax.ShapeDtypeStruct((length, STATS), jnp.float32)),
        grid=(length // block,),
        in_specs=[pl.BlockSpec((block, width), lambda i: (i, 0)), full, full,
                  pl.BlockSpec((block, 1), lambda i: (i, 0)),
                  pl.BlockSpec((1, length), lambda i: (0, 0))],
        out_specs=(pl.BlockSpec((block, width), lambda i: (i, 0)),
                   pl.BlockSpec((block, STATS), lambda i: (i, 0))),
        compiler_params=pltpu.CompilerParams(dimension_semantics=("arbitrary",)),
        cost_estimate=pl.CostEstimate(flops=4 * length * length * width, transcendentals=length * length * width // HEAD_DIM,
                                      bytes_accessed=8 * length * width),
    )(queries, key_side, value_proj, segq, segk)


def attention_backward(queries, key_side, value_proj, segment_row, stats, grad_context, inputs, out_t, parts,
                       block=256):
    length, width = queries.shape
    features = inputs.shape[1]
    segq = segment_row.reshape(length, 1)
    segk = segment_row.reshape(1, length)
    full = pl.BlockSpec((length, width), lambda i: (0, 0))
    rows = pl.BlockSpec((block, width), lambda i: (i, 0))
    return pl.pallas_call(
        functools.partial(attn_bwd_kernel, parts),
        out_shape=tuple(jax.ShapeDtypeStruct((length, width), jnp.bfloat16) for _ in range(3))
        + (jax.ShapeDtypeStruct((features, 4 * width), jnp.bfloat16),
           jax.ShapeDtypeStruct((8, width), jnp.float32)),
        grid=(length // block,),
        in_specs=[rows, full, full, rows,
                  pl.BlockSpec((block, 1), lambda i: (i, 0)),
                  pl.BlockSpec((1, length), lambda i: (0, 0)),
                  pl.BlockSpec((block, STATS), lambda i: (i, 0)),
                  pl.BlockSpec((block, features), lambda i: (i, 0)),
                  pl.BlockSpec((length, features), lambda i: (0, 0)),
                  pl.BlockSpec((features, width), lambda i: (0, 0))],
        out_specs=(rows, full, full,
                   pl.BlockSpec((features, 4 * width), lambda i: (0, 0)),
                   pl.BlockSpec((8, width), lambda i: (0, 0))),
        scratch_shapes=[pltpu.VMEM((length, width), jnp.float32), pltpu.VMEM((length, width), jnp.float32),
                        pltpu.VMEM((features, width), jnp.float32)],
        compiler_params=pltpu.CompilerParams(dimension_semantics=("arbitrary",), vmem_limit_bytes=60 * 1024 * 1024),
        cost_estimate=pl.CostEstimate(flops=10 * length * length * width + 6 * length * features * width,
                                      transcendentals=length * length * width // HEAD_DIM,
                                      bytes_accessed=14 * length * width + 10 * features * width),
    )(queries, key_side, value_proj, grad_context, segq, segk, stats, inputs, inputs, out_t)


def gather_shards(first_pieces, second_pieces, after=None):
    dp_count = lax.axis_size("dp")
    core = lax.rem(lax.axis_index("dp"), 2)
    first, second = jnp.stack(first_pieces), jnp.stack(second_pieces)
    mine = jnp.where(core == 0, first, second)
    gathered = lax.all_gather(mine, "tensor", axis=0, tiled=False)
    if after is not None:
        gathered, after = lax.optimization_barrier((gathered, after))
    other = lax.ppermute(gathered, "dp", perm=[(i, i ^ 1) for i in range(dp_count)])
    halves = (jnp.where(core == 0, gathered, other), jnp.where(core == 0, other, gathered))
    return [half[:, index] for half in halves for index in range(half.shape[1])]


def gather_pieces(pieces, after):
    dp_count = lax.axis_size("dp")
    part_count = lax.axis_size("tensor")
    rows = pieces[0].shape[0] // dp_count
    own = lax.dynamic_slice_in_dim(jnp.stack(pieces), lax.axis_index("dp") * rows, rows, 1)
    gathered = lax.all_gather(own, ("dp", "tensor"), axis=0, tiled=False)
    gathered, after = lax.optimization_barrier((gathered, after))
    gathered = gathered.reshape((dp_count, part_count) + own.shape)
    stacks = gathered.transpose(2, 1, 0, 3, 4).reshape(
        (len(pieces), part_count, dp_count * rows) + own.shape[2:]
    )
    first_whole = gathered[:, :, 0].transpose(0, 2, 1, 3).reshape(dp_count * rows, -1)
    return [stacks[index] for index in range(len(pieces))], first_whole


def scatter_rows(grads):
    joined = jnp.concatenate([grad.astype(jnp.bfloat16) for grad in grads], axis=1)
    return lax.psum_scatter(joined, "dp", scatter_dimension=0, tiled=True)


def part_major(grads):
    parts = lax.axis_size("tensor")
    columns = []
    for part in range(parts):
        for grad in grads:
            width = grad.shape[1] // parts
            columns.append(grad[:, part * width : (part + 1) * width].astype(jnp.bfloat16))
    return jnp.concatenate(columns, axis=1)


def scatter_parts(partials, widths):
    parts = lax.axis_size("tensor")
    joined = jnp.concatenate(
        [partial.reshape(partial.shape[0], parts, -1) for partial in partials], axis=2
    )
    summed = lax.psum_scatter(joined, "tensor", scatter_dimension=1, tiled=True)[:, 0]
    pieces = []
    start = 0
    for group in widths:
        for width in group:
            pieces.append(summed[:, start : start + width].astype(jnp.float32))
            start += width
    return pieces


def on_device(
    layer_input,
    segments,
    query_weight,
    query_bias,
    key_weight,
    value_weight,
    value_bias,
    output_weight,
    output_bias,
    first_gain,
    first_shift,
    up_weight,
    up_bias,
    down_weight,
    down_bias,
    second_gain,
    second_shift,
    output_grad,
):
    part_count = lax.axis_size("tensor")
    part_id = lax.axis_index("tensor")
    row_len = segments.shape[1]

    input_rows = lax.dynamic_slice_in_dim(layer_input, part_id * row_len, row_len, 0)
    segment_row = lax.dynamic_index_in_dim(segments, part_id, 0, keepdims=False)
    grad_out = lax.dynamic_slice_in_dim(output_grad, part_id * row_len, row_len, 0).astype(
        jnp.float32
    )

    qt_sh, kt_sh, vt_sh, o_sh = gather_shards(
        [query_weight.T, key_weight.T], [value_weight.T, output_weight]
    )
    bias_sh = lax.all_gather(
        jnp.concatenate([query_bias, value_bias, up_bias]), "tensor", axis=0, tiled=False
    )
    head_width = query_bias.shape[0]
    qb = bias_sh[:, :head_width].reshape(-1)
    vb = bias_sh[:, head_width : 2 * head_width].reshape(-1)
    ub = bias_sh[:, 2 * head_width :]
    width = qt_sh.shape[2]
    qt_full = qt_sh.reshape(-1, width)
    kt_full = kt_sh.reshape(-1, width)
    vt_full = vt_sh.reshape(-1, width)

    input_f32 = input_rows.astype(jnp.float32)
    queries = (contract_last(input_rows, qt_full) + qb).astype(jnp.bfloat16)
    key_side = contract_last(input_rows, kt_full).astype(jnp.bfloat16)
    value_proj = (contract_last(input_rows, vt_full) + vb).astype(jnp.bfloat16)
    context, softmax_stats = attention_forward(queries, key_side, value_proj, segment_row)
    (u_sh, d_sh), up_whole = gather_pieces([up_weight, down_weight], context)

    group_width = o_sh.shape[1]
    attn_total = input_f32
    for member in range(part_count):
        cols = slice(member * group_width, (member + 1) * group_width)
        attn_total = attn_total + product(context[:, cols], o_sh[member]).astype(
            jnp.bfloat16
        ).astype(jnp.float32)
    first_in = attn_total + output_bias
    first_out, first_unit, first_inv = normalize(first_in, first_gain, first_shift)
    first_low = first_out.astype(jnp.bfloat16)
    second_in = first_out
    pulls = []
    hidden_parts = []
    for member in range(part_count):
        pre_part = product(first_low, u_sh[member]) + ub[member]
        gelu_out, pull_gelu = jax.vjp(gelu_tanh, pre_part)
        pulls.append(pull_gelu)
        hidden_part = gelu_out.astype(jnp.bfloat16)
        hidden_parts.append(hidden_part)
        second_in = second_in + product(hidden_part, d_sh[member]).astype(
            jnp.bfloat16
        ).astype(jnp.float32)
    second_in = second_in + down_bias
    second_out, second_unit, second_inv = normalize(second_in, second_gain, second_shift)
    layer_output = second_out.astype(jnp.bfloat16)

    grad_second = normalize_back(grad_out, second_unit, second_inv, second_gain)
    grad_second_gain = jnp.sum(grad_out * second_unit, 0)
    grad_second_shift = jnp.sum(grad_out, 0)
    grad_down_bias = jnp.sum(grad_second, 0)
    down_low = grad_second.astype(jnp.bfloat16)
    first_grad = grad_second
    grad_pre_parts = []
    for member in range(part_count):
        grad_hidden = contract_last(down_low, d_sh[member])
        grad_pre_parts.append(pulls[member](grad_hidden)[0].astype(jnp.bfloat16))
    grad_pre_parts = lax.optimization_barrier(grad_pre_parts)
    grad_pre = jnp.concatenate(grad_pre_parts, axis=1)
    first_grad = first_grad + contract_last(grad_pre, up_whole)
    hidden_low = jnp.concatenate(lax.optimization_barrier(hidden_parts), axis=1)
    grad_up_bias = jnp.sum(grad_pre, 0, dtype=jnp.float32)
    ffn_grads = [contract_rows(first_low, grad_pre), contract_rows(down_low, hidden_low)]
    ffn_joined, first_grad = lax.optimization_barrier((part_major(ffn_grads), first_grad))
    ffn_rows = scatter_rows([ffn_joined])
    grad_first_gain = jnp.sum(first_grad * first_unit, 0)
    grad_first_shift = jnp.sum(first_grad, 0)
    attn_grad = normalize_back(first_grad, first_unit, first_inv, first_gain)
    grad_output_bias = jnp.sum(attn_grad, 0)
    attn_grad_low = attn_grad.astype(jnp.bfloat16)
    grad_context = contract_last(attn_grad_low, o_sh.reshape(-1, o_sh.shape[2])).astype(
        jnp.bfloat16
    )
    output_grad_t = contract_rows(attn_grad_low, context).astype(jnp.bfloat16)
    query_low, key_low, value_low, attn_joined, qv_bias = attention_backward(
        queries, key_side, value_proj, segment_row, softmax_stats, grad_context, input_rows,
        output_grad_t, part_count,
    )
    ffn_rows, attn_joined, qv_bias = lax.optimization_barrier((ffn_rows, attn_joined, qv_bias))
    grad_query_bias = qv_bias[0]
    grad_value_bias = qv_bias[1]
    attn_rows = scatter_rows([attn_joined])
    small = lax.psum(
        jnp.concatenate(
            [
                grad_query_bias,
                grad_value_bias,
                grad_up_bias,
                grad_output_bias,
                grad_first_gain,
                grad_first_shift,
                grad_down_bias,
                grad_second_gain,
                grad_second_shift,
            ]
        ),
        ("dp", "tensor"),
    )
    small, query_low, key_low, value_low = lax.optimization_barrier(
        (small, query_low, key_low, value_low)
    )
    input_grad = (
        attn_grad
        + product(query_low, qt_full)
        + product(key_low, kt_full)
        + product(value_low, vt_full)
    )
    attn_rows, small, input_grad = lax.optimization_barrier((attn_rows, small, input_grad))
    ffn_width = up_weight.shape[1]
    summed = scatter_parts([ffn_rows, attn_rows], [[ffn_width] * 2, [head_width] * 4])
    split_width = 2 * head_width * part_count + up_bias.shape[0] * part_count
    split = small[:split_width]
    shared = small[split_width:].reshape(6, -1)
    device_id = lax.axis_index("dp") * part_count + part_id
    piece = shared.shape[1] // (lax.axis_size("dp") * part_count)
    shared = lax.dynamic_slice_in_dim(shared, device_id * piece, piece, 1)

    def own_block(vector, offset, width):
        return lax.dynamic_slice_in_dim(vector, offset + part_id * width, width, 0)

    query_bias_grad = own_block(split, 0, head_width)
    value_bias_grad = own_block(split, head_width * part_count, head_width)
    up_bias_grad = own_block(split, 2 * head_width * part_count, up_bias.shape[0])
    return (
        layer_output,
        input_grad,
        summed[2],
        query_bias_grad,
        summed[3],
        summed[4],
        value_bias_grad,
        summed[5].T,
        shared[0],
        shared[1],
        shared[2],
        summed[0],
        up_bias_grad,
        summed[1].T,
        shared[3],
        shared[4],
        shared[5],
    )


def solution(mesh):
    in_specs = (
        P("dp", None),
        P("dp", None),
        P(None, "tensor"),
        P("tensor"),
        P(None, "tensor"),
        P(None, "tensor"),
        P("tensor"),
        P("tensor", None),
        P(),
        P(),
        P(),
        P(None, "tensor"),
        P("tensor"),
        P("tensor", None),
        P(),
        P(),
        P(),
        P("dp", None),
    )
    out_specs = (
        P(("dp", "tensor"), None),
        P(("dp", "tensor"), None),
        P("dp", "tensor"),
        P("tensor"),
        P("dp", "tensor"),
        P("dp", "tensor"),
        P("tensor"),
        P("tensor", "dp"),
        P(("dp", "tensor")),
        P(("dp", "tensor")),
        P(("dp", "tensor")),
        P("dp", "tensor"),
        P("tensor"),
        P("tensor", "dp"),
        P(("dp", "tensor")),
        P(("dp", "tensor")),
        P(("dp", "tensor")),
    )
    return jax.shard_map(
        on_device, mesh=mesh, in_specs=in_specs, out_specs=out_specs, check_vma=False
    )
```

```python
import functools

import jax
import jax.numpy as jnp
from jax import lax
from jax.experimental import pallas as pl
from jax.experimental.pallas import tpu as pltpu
from jax.sharding import PartitionSpec as P

HEAD_DIM = 64
GROUP_HEADS = 3

norm_eps = 1e-06


def product(left_side, right_side):
    return jnp.dot(left_side, right_side, preferred_element_type=jnp.float32)


def contract_rows(left_side, right_side):
    return lax.dot_general(
        left_side, right_side, (((0,), (0,)), ((), ())), preferred_element_type=jnp.float32
    )


def contract_last(left_side, right_side):
    return lax.dot_general(
        left_side, right_side, (((1,), (1,)), ((), ())), preferred_element_type=jnp.float32
    )


def normalize(summed, norm_gain, offset):
    centred = summed - jnp.mean(summed, -1, keepdims=True)
    inverse = lax.rsqrt(jnp.mean(centred * centred, -1, keepdims=True) + norm_eps)
    scaled = centred * inverse
    return (scaled * norm_gain + offset, scaled, inverse)


def normalize_back(grad_out, scaled, inverse, norm_gain):
    grad_scaled = grad_out * norm_gain
    mean_grad = jnp.mean(grad_scaled, -1, keepdims=True)
    mean_cross = jnp.mean(grad_scaled * scaled, -1, keepdims=True)
    return inverse * (grad_scaled - mean_grad - scaled * mean_cross)


def gelu_tanh(pre_act):
    return jax.nn.gelu(pre_act, approximate=True)


SCALE = HEAD_DIM ** (-0.5)
STATS = 128


def _scores(q, k, linked):
    s = lax.dot_general(q, k, (((1,), (1,)), ((), ())), preferred_element_type=jnp.float32) * SCALE
    return jnp.where(linked, s, -1e30)


def attn_fwd_kernel(q_ref, k_ref, v_ref, segq_ref, segk_ref, ctx_ref, stats_ref):
    linked = segq_ref[...] == segk_ref[...]
    heads = q_ref.shape[1] // HEAD_DIM
    half = STATS // 2
    for h in range(heads):
        cols = slice(h * HEAD_DIM, (h + 1) * HEAD_DIM)
        s = _scores(q_ref[:, cols], k_ref[:, cols], linked)
        m = jnp.max(s, axis=1, keepdims=True)
        e = jnp.exp(s - m)
        l = jnp.sum(e, axis=1, keepdims=True)
        p = (e / l).astype(jnp.bfloat16)
        ctx = jnp.dot(p, v_ref[:, cols], preferred_element_type=jnp.float32)
        ctx_ref[:, cols] = ctx.astype(ctx_ref.dtype)
        stats_ref[:, h : h + 1] = m
        stats_ref[:, half + h : half + h + 1] = l


def attn_bwd_kernel(parts, q_ref, k_ref, v_ref, dctx_ref, segq_ref, segk_ref, stats_ref, x_ref, xall_ref,
                    out_t_ref, dq_ref, dk_ref, dv_ref, wgrad_ref, bias_ref, dk_acc, dv_acc, dwq_acc):
    step = pl.program_id(0)

    @pl.when(step == 0)
    def _():
        dk_acc[...] = jnp.zeros_like(dk_acc)
        dv_acc[...] = jnp.zeros_like(dv_acc)
        dwq_acc[...] = jnp.zeros_like(dwq_acc)
        bias_ref[...] = jnp.zeros_like(bias_ref)

    linked = segq_ref[...] == segk_ref[...]
    heads = q_ref.shape[1] // HEAD_DIM
    half = STATS // 2
    dq_parts = []
    for h in range(heads):
        cols = slice(h * HEAD_DIM, (h + 1) * HEAD_DIM)
        q = q_ref[:, cols]
        k = k_ref[:, cols]
        dctx = dctx_ref[:, cols]
        s = _scores(q, k, linked)
        p = jnp.exp(s - stats_ref[:, h : h + 1]) / stats_ref[:, half + h : half + h + 1]
        dp = lax.dot_general(dctx, v_ref[:, cols], (((1,), (1,)), ((), ())), preferred_element_type=jnp.float32)
        inner = jnp.sum(p * dp, axis=1, keepdims=True)
        ds = (p * (dp - inner)).astype(jnp.bfloat16)
        dq = (jnp.dot(ds, k, preferred_element_type=jnp.float32) * SCALE).astype(dq_ref.dtype)
        dq_ref[:, cols] = dq
        dq_parts.append(dq)
        dk_acc[:, cols] += lax.dot_general(ds, q, (((0,), (0,)), ((), ())), preferred_element_type=jnp.float32)
        dv_acc[:, cols] += lax.dot_general(p.astype(jnp.bfloat16), dctx, (((0,), (0,)), ((), ())), preferred_element_type=jnp.float32)
    dq_block = jnp.concatenate(dq_parts, axis=1)
    dwq_acc[...] += lax.dot_general(x_ref[...], dq_block, (((0,), (0,)), ((), ())), preferred_element_type=jnp.float32)
    bias_ref[0:1, :] += jnp.sum(dq_block.astype(jnp.float32), axis=0, keepdims=True)

    @pl.when(step == pl.num_programs(0) - 1)
    def _():
        width = dk_ref.shape[1]
        dk = (dk_acc[...] * SCALE).astype(dk_ref.dtype)
        dv = dv_acc[...].astype(dv_ref.dtype)
        dk_ref[...] = dk
        dv_ref[...] = dv
        bias_ref[1:2, :] = jnp.sum(dv.astype(jnp.float32), axis=0, keepdims=True)
        xall = xall_ref[...]
        grads = (
            dwq_acc[...].astype(wgrad_ref.dtype),
            lax.dot_general(xall, dk, (((0,), (0,)), ((), ())),
                            preferred_element_type=jnp.float32).astype(wgrad_ref.dtype),
            lax.dot_general(xall, dv, (((0,), (0,)), ((), ())),
                            preferred_element_type=jnp.float32).astype(wgrad_ref.dtype),
            out_t_ref[...],
        )
        piece = width // parts
        for part in range(parts):
            for index, grad in enumerate(grads):
                start = (part * len(grads) + index) * piece
                wgrad_ref[:, start : start + piece] = grad[:, part * piece : (part + 1) * piece]


def attention_forward(queries, key_side, value_proj, segment_row, block=256):
    length, width = queries.shape
    segq = segment_row.reshape(length, 1)
    segk = segment_row.reshape(1, length)
    full = pl.BlockSpec((length, width), lambda i: (0, 0))
    return pl.pallas_call(
        attn_fwd_kernel,
        out_shape=(jax.ShapeDtypeStruct((length, width), jnp.bfloat16),
                   jax.ShapeDtypeStruct((length, STATS), jnp.float32)),
        grid=(length // block,),
        in_specs=[pl.BlockSpec((block, width), lambda i: (i, 0)), full, full,
                  pl.BlockSpec((block, 1), lambda i: (i, 0)),
                  pl.BlockSpec((1, length), lambda i: (0, 0))],
        out_specs=(pl.BlockSpec((block, width), lambda i: (i, 0)),
                   pl.BlockSpec((block, STATS), lambda i: (i, 0))),
        compiler_params=pltpu.CompilerParams(dimension_semantics=("arbitrary",)),
        cost_estimate=pl.CostEstimate(flops=4 * length * length * width, transcendentals=length * length * width // HEAD_DIM,
                                      bytes_accessed=8 * length * width),
    )(queries, key_side, value_proj, segq, segk)


def attention_backward(queries, key_side, value_proj, segment_row, stats, grad_context, inputs, out_t, parts,
                       block=256):
    length, width = queries.shape
    features = inputs.shape[1]
    segq = segment_row.reshape(length, 1)
    segk = segment_row.reshape(1, length)
    full = pl.BlockSpec((length, width), lambda i: (0, 0))
    rows = pl.BlockSpec((block, width), lambda i: (i, 0))
    return pl.pallas_call(
        functools.partial(attn_bwd_kernel, parts),
        out_shape=tuple(jax.ShapeDtypeStruct((length, width), jnp.bfloat16) for _ in range(3))
        + (jax.ShapeDtypeStruct((features, 4 * width), jnp.bfloat16),
           jax.ShapeDtypeStruct((8, width), jnp.float32)),
        grid=(length // block,),
        in_specs=[rows, full, full, rows,
                  pl.BlockSpec((block, 1), lambda i: (i, 0)),
                  pl.BlockSpec((1, length), lambda i: (0, 0)),
                  pl.BlockSpec((block, STATS), lambda i: (i, 0)),
                  pl.BlockSpec((block, features), lambda i: (i, 0)),
                  pl.BlockSpec((length, features), lambda i: (0, 0)),
                  pl.BlockSpec((features, width), lambda i: (0, 0))],
        out_specs=(rows, full, full,
                   pl.BlockSpec((features, 4 * width), lambda i: (0, 0)),
                   pl.BlockSpec((8, width), lambda i: (0, 0))),
        scratch_shapes=[pltpu.VMEM((length, width), jnp.float32), pltpu.VMEM((length, width), jnp.float32),
                        pltpu.VMEM((features, width), jnp.float32)],
        compiler_params=pltpu.CompilerParams(dimension_semantics=("arbitrary",), vmem_limit_bytes=60 * 1024 * 1024),
        cost_estimate=pl.CostEstimate(flops=10 * length * length * width + 6 * length * features * width,
                                      transcendentals=length * length * width // HEAD_DIM,
                                      bytes_accessed=14 * length * width + 10 * features * width),
    )(queries, key_side, value_proj, grad_context, segq, segk, stats, inputs, inputs, out_t)


def gather_shards(first_pieces, second_pieces, after=None):
    dp_count = lax.axis_size("dp")
    core = lax.rem(lax.axis_index("dp"), 2)
    first, second = jnp.stack(first_pieces), jnp.stack(second_pieces)
    mine = jnp.where(core == 0, first, second)
    gathered = lax.all_gather(mine, "tensor", axis=0, tiled=False)
    if after is not None:
        gathered, after = lax.optimization_barrier((gathered, after))
    other = lax.ppermute(gathered, "dp", perm=[(i, i ^ 1) for i in range(dp_count)])
    halves = (jnp.where(core == 0, gathered, other), jnp.where(core == 0, other, gathered))
    return [half[:, index] for half in halves for index in range(half.shape[1])]


def gather_pieces(pieces, after):
    dp_count = lax.axis_size("dp")
    part_count = lax.axis_size("tensor")
    rows = pieces[0].shape[0] // dp_count
    own = lax.dynamic_slice_in_dim(jnp.stack(pieces), lax.axis_index("dp") * rows, rows, 1)
    gathered = lax.all_gather(own, ("dp", "tensor"), axis=0, tiled=False)
    gathered, after = lax.optimization_barrier((gathered, after))
    gathered = gathered.reshape((dp_count, part_count) + own.shape)
    stacks = gathered.transpose(2, 1, 0, 3, 4).reshape(
        (len(pieces), part_count, dp_count * rows) + own.shape[2:]
    )
    first_whole = gathered[:, :, 0].transpose(0, 2, 1, 3).reshape(dp_count * rows, -1)
    return [stacks[index] for index in range(len(pieces))], first_whole


def scatter_rows(grads):
    joined = jnp.concatenate([grad.astype(jnp.bfloat16) for grad in grads], axis=1)
    return lax.psum_scatter(joined, "dp", scatter_dimension=0, tiled=True)


def part_major(grads):
    parts = lax.axis_size("tensor")
    columns = []
    for part in range(parts):
        for grad in grads:
            width = grad.shape[1] // parts
            columns.append(grad[:, part * width : (part + 1) * width].astype(jnp.bfloat16))
    return jnp.concatenate(columns, axis=1)


def scatter_parts(partials, widths):
    parts = lax.axis_size("tensor")
    joined = jnp.concatenate(
        [partial.reshape(partial.shape[0], parts, -1) for partial in partials], axis=2
    )
    summed = lax.psum_scatter(joined, "tensor", scatter_dimension=1, tiled=True)[:, 0]
    pieces = []
    start = 0
    for group in widths:
        for width in group:
            pieces.append(summed[:, start : start + width].astype(jnp.float32))
            start += width
    return pieces


def on_device(
    layer_input,
    segments,
    query_weight,
    query_bias,
    key_weight,
    value_weight,
    value_bias,
    output_weight,
    output_bias,
    first_gain,
    first_shift,
    up_weight,
    up_bias,
    down_weight,
    down_bias,
    second_gain,
    second_shift,
    output_grad,
):
    part_count = lax.axis_size("tensor")
    part_id = lax.axis_index("tensor")
    row_len = segments.shape[1]

    input_rows = lax.dynamic_slice_in_dim(layer_input, part_id * row_len, row_len, 0)
    segment_row = lax.dynamic_index_in_dim(segments, part_id, 0, keepdims=False)
    grad_out = lax.dynamic_slice_in_dim(output_grad, part_id * row_len, row_len, 0).astype(
        jnp.float32
    )

    qt_sh, kt_sh, vt_sh, o_sh = gather_shards(
        [query_weight.T, key_weight.T], [value_weight.T, output_weight]
    )
    bias_sh = lax.all_gather(
        jnp.concatenate([query_bias, value_bias, up_bias]), "tensor", axis=0, tiled=False
    )
    head_width = query_bias.shape[0]
    qb = bias_sh[:, :head_width].reshape(-1)
    vb = bias_sh[:, head_width : 2 * head_width].reshape(-1)
    ub = bias_sh[:, 2 * head_width :]
    width = qt_sh.shape[2]
    qt_full = qt_sh.reshape(-1, width)
    kt_full = kt_sh.reshape(-1, width)
    vt_full = vt_sh.reshape(-1, width)

    input_f32 = input_rows.astype(jnp.float32)
    queries = (contract_last(input_rows, qt_full) + qb).astype(jnp.bfloat16)
    key_side = contract_last(input_rows, kt_full).astype(jnp.bfloat16)
    value_proj = (contract_last(input_rows, vt_full) + vb).astype(jnp.bfloat16)
    context, softmax_stats = attention_forward(queries, key_side, value_proj, segment_row)
    (u_sh, d_sh), up_whole = gather_pieces([up_weight, down_weight], context)

    group_width = o_sh.shape[1]
    attn_total = input_f32
    for member in range(part_count):
        cols = slice(member * group_width, (member + 1) * group_width)
        attn_total = attn_total + product(context[:, cols], o_sh[member]).astype(
            jnp.bfloat16
        ).astype(jnp.float32)
    first_in = attn_total + output_bias
    first_out, first_unit, first_inv = normalize(first_in, first_gain, first_shift)
    first_low = first_out.astype(jnp.bfloat16)
    pre_act = product(first_low, up_whole) + ub.reshape(-1)
    gelu_out, pull_gelu = jax.vjp(gelu_tanh, pre_act)
    hidden_low = gelu_out.astype(jnp.bfloat16)
    unit_width = hidden_low.shape[1] // part_count
    second_in = first_out
    for member in range(part_count):
        units = slice(member * unit_width, (member + 1) * unit_width)
        second_in = second_in + product(hidden_low[:, units], d_sh[member]).astype(
            jnp.bfloat16
        ).astype(jnp.float32)
    second_in = second_in + down_bias
    second_out, second_unit, second_inv = normalize(second_in, second_gain, second_shift)
    layer_output = second_out.astype(jnp.bfloat16)

    grad_second = normalize_back(grad_out, second_unit, second_inv, second_gain)
    grad_second_gain = jnp.sum(grad_out * second_unit, 0)
    grad_second_shift = jnp.sum(grad_out, 0)
    grad_down_bias = jnp.sum(grad_second, 0)
    down_low = grad_second.astype(jnp.bfloat16)
    grad_hidden = contract_last(down_low, d_sh.reshape(-1, d_sh.shape[2]))
    grad_pre = lax.optimization_barrier(pull_gelu(grad_hidden)[0].astype(jnp.bfloat16))
    first_grad = grad_second + contract_last(grad_pre, up_whole)
    grad_up_bias = jnp.sum(grad_pre, 0, dtype=jnp.float32)
    ffn_grads = [contract_rows(first_low, grad_pre), contract_rows(down_low, hidden_low)]
    ffn_joined, first_grad = lax.optimization_barrier((part_major(ffn_grads), first_grad))
    ffn_rows = scatter_rows([ffn_joined])
    grad_first_gain = jnp.sum(first_grad * first_unit, 0)
    grad_first_shift = jnp.sum(first_grad, 0)
    attn_grad = normalize_back(first_grad, first_unit, first_inv, first_gain)
    grad_output_bias = jnp.sum(attn_grad, 0)
    attn_grad_low = attn_grad.astype(jnp.bfloat16)
    grad_context = contract_last(attn_grad_low, o_sh.reshape(-1, o_sh.shape[2])).astype(
        jnp.bfloat16
    )
    output_grad_t = contract_rows(attn_grad_low, context).astype(jnp.bfloat16)
    query_low, key_low, value_low, attn_joined, qv_bias = attention_backward(
        queries, key_side, value_proj, segment_row, softmax_stats, grad_context, input_rows,
        output_grad_t, part_count,
    )
    ffn_rows, attn_joined, qv_bias = lax.optimization_barrier((ffn_rows, attn_joined, qv_bias))
    grad_query_bias = qv_bias[0]
    grad_value_bias = qv_bias[1]
    attn_rows = scatter_rows([attn_joined])
    small = lax.psum(
        jnp.concatenate(
            [
                grad_query_bias,
                grad_value_bias,
                grad_up_bias,
                grad_output_bias,
                grad_first_gain,
                grad_first_shift,
                grad_down_bias,
                grad_second_gain,
                grad_second_shift,
            ]
        ),
        ("dp", "tensor"),
    )
    small, query_low, key_low, value_low = lax.optimization_barrier(
        (small, query_low, key_low, value_low)
    )
    input_grad = (
        attn_grad
        + product(query_low, qt_full)
        + product(key_low, kt_full)
        + product(value_low, vt_full)
    )
    attn_rows, small, input_grad = lax.optimization_barrier((attn_rows, small, input_grad))
    ffn_width = up_weight.shape[1]
    summed = scatter_parts([ffn_rows, attn_rows], [[ffn_width] * 2, [head_width] * 4])
    split_width = 2 * head_width * part_count + up_bias.shape[0] * part_count
    split = small[:split_width]
    shared = small[split_width:].reshape(6, -1)
    device_id = lax.axis_index("dp") * part_count + part_id
    piece = shared.shape[1] // (lax.axis_size("dp") * part_count)
    shared = lax.dynamic_slice_in_dim(shared, device_id * piece, piece, 1)

    def own_block(vector, offset, width):
        return lax.dynamic_slice_in_dim(vector, offset + part_id * width, width, 0)

    query_bias_grad = own_block(split, 0, head_width)
    value_bias_grad = own_block(split, head_width * part_count, head_width)
    up_bias_grad = own_block(split, 2 * head_width * part_count, up_bias.shape[0])
    return (
        layer_output,
        input_grad,
        summed[2],
        query_bias_grad,
        summed[3],
        summed[4],
        value_bias_grad,
        summed[5].T,
        shared[0],
        shared[1],
        shared[2],
        summed[0],
        up_bias_grad,
        summed[1].T,
        shared[3],
        shared[4],
        shared[5],
    )


def solution(mesh):
    in_specs = (
        P("dp", None),
        P("dp", None),
        P(None, "tensor"),
        P("tensor"),
        P(None, "tensor"),
        P(None, "tensor"),
        P("tensor"),
        P("tensor", None),
        P(),
        P(),
        P(),
        P(None, "tensor"),
        P("tensor"),
        P("tensor", None),
        P(),
        P(),
        P(),
        P("dp", None),
    )
    out_specs = (
        P(("dp", "tensor"), None),
        P(("dp", "tensor"), None),
        P("dp", "tensor"),
        P("tensor"),
        P("dp", "tensor"),
        P("dp", "tensor"),
        P("tensor"),
        P("tensor", "dp"),
        P(("dp", "tensor")),
        P(("dp", "tensor")),
        P(("dp", "tensor")),
        P("dp", "tensor"),
        P("tensor"),
        P("tensor", "dp"),
        P(("dp", "tensor")),
        P(("dp", "tensor")),
        P(("dp", "tensor")),
    )
    return jax.shard_map(
        on_device, mesh=mesh, in_specs=in_specs, out_specs=out_specs, check_vma=False
    )
```

```python
import functools

import jax
import jax.numpy as jnp
from jax import lax
from jax.experimental import pallas as pl
from jax.experimental.pallas import tpu as pltpu
from jax.sharding import PartitionSpec as P

HEAD_DIM = 64
GROUP_HEADS = 3

norm_eps = 1e-06


def product(left_side, right_side):
    return jnp.dot(left_side, right_side, preferred_element_type=jnp.float32)


def contract_rows(left_side, right_side):
    return lax.dot_general(
        left_side, right_side, (((0,), (0,)), ((), ())), preferred_element_type=jnp.float32
    )


def contract_last(left_side, right_side):
    return lax.dot_general(
        left_side, right_side, (((1,), (1,)), ((), ())), preferred_element_type=jnp.float32
    )


def normalize(summed, norm_gain, offset):
    centred = summed - jnp.mean(summed, -1, keepdims=True)
    inverse = lax.rsqrt(jnp.mean(centred * centred, -1, keepdims=True) + norm_eps)
    scaled = centred * inverse
    return (scaled * norm_gain + offset, scaled, inverse)


def normalize_back(grad_out, scaled, inverse, norm_gain):
    grad_scaled = grad_out * norm_gain
    mean_grad = jnp.mean(grad_scaled, -1, keepdims=True)
    mean_cross = jnp.mean(grad_scaled * scaled, -1, keepdims=True)
    return inverse * (grad_scaled - mean_grad - scaled * mean_cross)


def gelu_tanh(pre_act):
    return jax.nn.gelu(pre_act, approximate=True)


SCALE = HEAD_DIM ** (-0.5)
STATS = 128


def _scores(q, k, linked):
    s = lax.dot_general(q, k, (((1,), (1,)), ((), ())), preferred_element_type=jnp.float32) * SCALE
    return jnp.where(linked, s, -1e30)


def attn_fwd_kernel(q_ref, k_ref, v_ref, segq_ref, segk_ref, ctx_ref, stats_ref):
    linked = segq_ref[...] == segk_ref[...]
    heads = q_ref.shape[1] // HEAD_DIM
    half = STATS // 2
    for h in range(heads):
        cols = slice(h * HEAD_DIM, (h + 1) * HEAD_DIM)
        s = _scores(q_ref[:, cols], k_ref[:, cols], linked)
        m = jnp.max(s, axis=1, keepdims=True)
        e = jnp.exp(s - m)
        l = jnp.sum(e, axis=1, keepdims=True)
        p = (e / l).astype(jnp.bfloat16)
        ctx = jnp.dot(p, v_ref[:, cols], preferred_element_type=jnp.float32)
        ctx_ref[:, cols] = ctx.astype(ctx_ref.dtype)
        stats_ref[:, h : h + 1] = m
        stats_ref[:, half + h : half + h + 1] = l


def attn_bwd_kernel(parts, q_ref, k_ref, v_ref, dctx_ref, segq_ref, segk_ref, stats_ref, x_ref, xall_ref,
                    out_t_ref, dq_ref, dk_ref, dv_ref, wgrad_ref, bias_ref, dk_acc, dv_acc, dwq_acc):
    step = pl.program_id(0)

    @pl.when(step == 0)
    def _():
        dk_acc[...] = jnp.zeros_like(dk_acc)
        dv_acc[...] = jnp.zeros_like(dv_acc)
        dwq_acc[...] = jnp.zeros_like(dwq_acc)
        bias_ref[...] = jnp.zeros_like(bias_ref)

    linked = segq_ref[...] == segk_ref[...]
    heads = q_ref.shape[1] // HEAD_DIM
    half = STATS // 2
    dq_parts = []
    for h in range(heads):
        cols = slice(h * HEAD_DIM, (h + 1) * HEAD_DIM)
        q = q_ref[:, cols]
        k = k_ref[:, cols]
        dctx = dctx_ref[:, cols]
        s = _scores(q, k, linked)
        p = jnp.exp(s - stats_ref[:, h : h + 1]) / stats_ref[:, half + h : half + h + 1]
        dp = lax.dot_general(dctx, v_ref[:, cols], (((1,), (1,)), ((), ())), preferred_element_type=jnp.float32)
        inner = jnp.sum(p * dp, axis=1, keepdims=True)
        ds = (p * (dp - inner)).astype(jnp.bfloat16)
        dq = (jnp.dot(ds, k, preferred_element_type=jnp.float32) * SCALE).astype(dq_ref.dtype)
        dq_ref[:, cols] = dq
        dq_parts.append(dq)
        dk_acc[:, cols] += lax.dot_general(ds, q, (((0,), (0,)), ((), ())), preferred_element_type=jnp.float32)
        dv_acc[:, cols] += lax.dot_general(p.astype(jnp.bfloat16), dctx, (((0,), (0,)), ((), ())), preferred_element_type=jnp.float32)
    dq_block = jnp.concatenate(dq_parts, axis=1)
    dwq_acc[...] += lax.dot_general(x_ref[...], dq_block, (((0,), (0,)), ((), ())), preferred_element_type=jnp.float32)
    bias_ref[0:1, :] += jnp.sum(dq_block.astype(jnp.float32), axis=0, keepdims=True)

    @pl.when(step == pl.num_programs(0) - 1)
    def _():
        width = dk_ref.shape[1]
        dk = (dk_acc[...] * SCALE).astype(dk_ref.dtype)
        dv = dv_acc[...].astype(dv_ref.dtype)
        dk_ref[...] = dk
        dv_ref[...] = dv
        bias_ref[1:2, :] = jnp.sum(dv.astype(jnp.float32), axis=0, keepdims=True)
        xall = xall_ref[...]
        grads = (
            dwq_acc[...].astype(wgrad_ref.dtype),
            lax.dot_general(xall, dk, (((0,), (0,)), ((), ())),
                            preferred_element_type=jnp.float32).astype(wgrad_ref.dtype),
            lax.dot_general(xall, dv, (((0,), (0,)), ((), ())),
                            preferred_element_type=jnp.float32).astype(wgrad_ref.dtype),
            out_t_ref[...],
        )
        piece = width // parts
        for part in range(parts):
            for index, grad in enumerate(grads):
                start = (part * len(grads) + index) * piece
                wgrad_ref[:, start : start + piece] = grad[:, part * piece : (part + 1) * piece]


def attention_forward(queries, key_side, value_proj, segment_row, block=256):
    length, width = queries.shape
    segq = segment_row.reshape(length, 1)
    segk = segment_row.reshape(1, length)
    full = pl.BlockSpec((length, width), lambda i: (0, 0))
    return pl.pallas_call(
        attn_fwd_kernel,
        out_shape=(jax.ShapeDtypeStruct((length, width), jnp.bfloat16),
                   jax.ShapeDtypeStruct((length, STATS), jnp.float32)),
        grid=(length // block,),
        in_specs=[pl.BlockSpec((block, width), lambda i: (i, 0)), full, full,
                  pl.BlockSpec((block, 1), lambda i: (i, 0)),
                  pl.BlockSpec((1, length), lambda i: (0, 0))],
        out_specs=(pl.BlockSpec((block, width), lambda i: (i, 0)),
                   pl.BlockSpec((block, STATS), lambda i: (i, 0))),
        compiler_params=pltpu.CompilerParams(dimension_semantics=("arbitrary",)),
        cost_estimate=pl.CostEstimate(flops=4 * length * length * width, transcendentals=length * length * width // HEAD_DIM,
                                      bytes_accessed=8 * length * width),
    )(queries, key_side, value_proj, segq, segk)


def attention_backward(queries, key_side, value_proj, segment_row, stats, grad_context, inputs, out_t, parts,
                       block=256):
    length, width = queries.shape
    features = inputs.shape[1]
    segq = segment_row.reshape(length, 1)
    segk = segment_row.reshape(1, length)
    full = pl.BlockSpec((length, width), lambda i: (0, 0))
    rows = pl.BlockSpec((block, width), lambda i: (i, 0))
    return pl.pallas_call(
        functools.partial(attn_bwd_kernel, parts),
        out_shape=tuple(jax.ShapeDtypeStruct((length, width), jnp.bfloat16) for _ in range(3))
        + (jax.ShapeDtypeStruct((features, 4 * width), jnp.bfloat16),
           jax.ShapeDtypeStruct((8, width), jnp.float32)),
        grid=(length // block,),
        in_specs=[rows, full, full, rows,
                  pl.BlockSpec((block, 1), lambda i: (i, 0)),
                  pl.BlockSpec((1, length), lambda i: (0, 0)),
                  pl.BlockSpec((block, STATS), lambda i: (i, 0)),
                  pl.BlockSpec((block, features), lambda i: (i, 0)),
                  pl.BlockSpec((length, features), lambda i: (0, 0)),
                  pl.BlockSpec((features, width), lambda i: (0, 0))],
        out_specs=(rows, full, full,
                   pl.BlockSpec((features, 4 * width), lambda i: (0, 0)),
                   pl.BlockSpec((8, width), lambda i: (0, 0))),
        scratch_shapes=[pltpu.VMEM((length, width), jnp.float32), pltpu.VMEM((length, width), jnp.float32),
                        pltpu.VMEM((features, width), jnp.float32)],
        compiler_params=pltpu.CompilerParams(dimension_semantics=("arbitrary",), vmem_limit_bytes=60 * 1024 * 1024),
        cost_estimate=pl.CostEstimate(flops=10 * length * length * width + 6 * length * features * width,
                                      transcendentals=length * length * width // HEAD_DIM,
                                      bytes_accessed=14 * length * width + 10 * features * width),
    )(queries, key_side, value_proj, grad_context, segq, segk, stats, inputs, inputs, out_t)


def gather_shards(first_pieces, second_pieces, after=None):
    dp_count = lax.axis_size("dp")
    core = lax.rem(lax.axis_index("dp"), 2)
    first, second = jnp.stack(first_pieces), jnp.stack(second_pieces)
    mine = jnp.where(core == 0, first, second)
    gathered = lax.all_gather(mine, "tensor", axis=0, tiled=False)
    if after is not None:
        gathered, after = lax.optimization_barrier((gathered, after))
    other = lax.ppermute(gathered, "dp", perm=[(i, i ^ 1) for i in range(dp_count)])
    halves = (jnp.where(core == 0, gathered, other), jnp.where(core == 0, other, gathered))
    return [half[:, index] for half in halves for index in range(half.shape[1])]


def gather_pieces(pieces, after):
    dp_count = lax.axis_size("dp")
    part_count = lax.axis_size("tensor")
    rows = pieces[0].shape[0] // dp_count
    own = lax.dynamic_slice_in_dim(jnp.stack(pieces), lax.axis_index("dp") * rows, rows, 1)
    gathered = lax.all_gather(own, ("dp", "tensor"), axis=0, tiled=False)
    gathered, after = lax.optimization_barrier((gathered, after))
    gathered = gathered.reshape((dp_count, part_count) + own.shape)
    stacks = gathered.transpose(2, 1, 0, 3, 4).reshape(
        (len(pieces), part_count, dp_count * rows) + own.shape[2:]
    )
    first_whole = gathered[:, :, 0].transpose(0, 2, 1, 3).reshape(dp_count * rows, -1)
    return [stacks[index] for index in range(len(pieces))], first_whole


def scatter_rows(grads):
    joined = jnp.concatenate([grad.astype(jnp.bfloat16) for grad in grads], axis=1)
    return lax.psum_scatter(joined, "dp", scatter_dimension=0, tiled=True)


def part_major(grads):
    parts = lax.axis_size("tensor")
    columns = []
    for part in range(parts):
        for grad in grads:
            width = grad.shape[1] // parts
            columns.append(grad[:, part * width : (part + 1) * width].astype(jnp.bfloat16))
    return jnp.concatenate(columns, axis=1)


def scatter_parts(partials, widths):
    parts = lax.axis_size("tensor")
    joined = jnp.concatenate(
        [partial.reshape(partial.shape[0], parts, -1) for partial in partials], axis=2
    )
    summed = lax.psum_scatter(joined, "tensor", scatter_dimension=1, tiled=True)[:, 0]
    pieces = []
    start = 0
    for group in widths:
        for width in group:
            pieces.append(summed[:, start : start + width].astype(jnp.float32))
            start += width
    return pieces


def on_device(
    layer_input,
    segments,
    query_weight,
    query_bias,
    key_weight,
    value_weight,
    value_bias,
    output_weight,
    output_bias,
    first_gain,
    first_shift,
    up_weight,
    up_bias,
    down_weight,
    down_bias,
    second_gain,
    second_shift,
    output_grad,
):
    part_count = lax.axis_size("tensor")
    part_id = lax.axis_index("tensor")
    row_len = segments.shape[1]

    input_rows = lax.dynamic_slice_in_dim(layer_input, part_id * row_len, row_len, 0)
    segment_row = lax.dynamic_index_in_dim(segments, part_id, 0, keepdims=False)
    grad_out = lax.dynamic_slice_in_dim(output_grad, part_id * row_len, row_len, 0).astype(
        jnp.float32
    )

    qt_sh, kt_sh, vt_sh, o_sh = gather_shards(
        [query_weight.T, key_weight.T], [value_weight.T, output_weight]
    )
    bias_sh = lax.all_gather(
        jnp.concatenate([query_bias, value_bias, up_bias]), "tensor", axis=0, tiled=False
    )
    head_width = query_bias.shape[0]
    qb = bias_sh[:, :head_width].reshape(-1)
    vb = bias_sh[:, head_width : 2 * head_width].reshape(-1)
    ub = bias_sh[:, 2 * head_width :]
    width = qt_sh.shape[2]
    qt_full = qt_sh.reshape(-1, width)
    kt_full = kt_sh.reshape(-1, width)
    vt_full = vt_sh.reshape(-1, width)

    input_f32 = input_rows.astype(jnp.float32)
    queries = (contract_last(input_rows, qt_full) + qb).astype(jnp.bfloat16)
    key_side = contract_last(input_rows, kt_full).astype(jnp.bfloat16)
    value_proj = (contract_last(input_rows, vt_full) + vb).astype(jnp.bfloat16)
    context, softmax_stats = attention_forward(queries, key_side, value_proj, segment_row)
    (u_sh, d_sh), up_whole = gather_pieces([up_weight, down_weight], context)

    group_width = o_sh.shape[1]
    attn_total = input_f32
    for member in range(part_count):
        cols = slice(member * group_width, (member + 1) * group_width)
        attn_total = attn_total + product(context[:, cols], o_sh[member]).astype(
            jnp.bfloat16
        ).astype(jnp.float32)
    first_in = attn_total + output_bias
    first_out, first_unit, first_inv = normalize(first_in, first_gain, first_shift)
    first_low = first_out.astype(jnp.bfloat16)
    pre_act = product(first_low, up_whole) + ub.reshape(-1)
    gelu_out, pull_gelu = jax.vjp(gelu_tanh, pre_act)
    hidden_low = gelu_out.astype(jnp.bfloat16)
    unit_width = hidden_low.shape[1] // part_count
    second_in = first_out
    for member in range(part_count):
        units = slice(member * unit_width, (member + 1) * unit_width)
        second_in = second_in + product(hidden_low[:, units], d_sh[member]).astype(
            jnp.bfloat16
        ).astype(jnp.float32)
    second_in = second_in + down_bias
    second_out, second_unit, second_inv = normalize(second_in, second_gain, second_shift)
    layer_output = second_out.astype(jnp.bfloat16)

    grad_second = normalize_back(grad_out, second_unit, second_inv, second_gain)
    grad_second_gain = jnp.sum(grad_out * second_unit, 0)
    grad_second_shift = jnp.sum(grad_out, 0)
    grad_down_bias = jnp.sum(grad_second, 0)
    down_low = grad_second.astype(jnp.bfloat16)
    grad_hidden = contract_last(down_low, d_sh.reshape(-1, d_sh.shape[2]))
    grad_pre = lax.optimization_barrier(pull_gelu(grad_hidden)[0].astype(jnp.bfloat16))
    first_grad = grad_second + contract_last(grad_pre, up_whole)
    grad_up_bias = jnp.sum(grad_pre, 0, dtype=jnp.float32)
    ffn_grads = [contract_rows(first_low, grad_pre), contract_rows(down_low, hidden_low)]
    ffn_joined, first_grad = lax.optimization_barrier((part_major(ffn_grads), first_grad))
    ffn_rows = scatter_rows([ffn_joined])
    grad_first_gain = jnp.sum(first_grad * first_unit, 0)
    grad_first_shift = jnp.sum(first_grad, 0)
    attn_grad = normalize_back(first_grad, first_unit, first_inv, first_gain)
    grad_output_bias = jnp.sum(attn_grad, 0)
    attn_grad_low = attn_grad.astype(jnp.bfloat16)
    grad_context = contract_last(attn_grad_low, o_sh.reshape(-1, o_sh.shape[2])).astype(
        jnp.bfloat16
    )
    output_grad_t = contract_rows(attn_grad_low, context).astype(jnp.bfloat16)
    query_low, key_low, value_low, attn_joined, qv_bias = attention_backward(
        queries, key_side, value_proj, segment_row, softmax_stats, grad_context, input_rows,
        output_grad_t, part_count,
    )
    ffn_rows, attn_joined, qv_bias = lax.optimization_barrier((ffn_rows, attn_joined, qv_bias))
    grad_query_bias = qv_bias[0]
    grad_value_bias = qv_bias[1]
    attn_rows = scatter_rows([attn_joined])
    small = lax.psum(
        jnp.concatenate(
            [
                grad_query_bias,
                grad_value_bias,
                grad_up_bias,
                grad_output_bias,
                grad_first_gain,
                grad_first_shift,
                grad_down_bias,
                grad_second_gain,
                grad_second_shift,
            ]
        ),
        ("dp", "tensor"),
    )
    small, query_low, key_low, value_low = lax.optimization_barrier(
        (small, query_low, key_low, value_low)
    )
    input_grad = (
        attn_grad
        + product(query_low, qt_full)
        + product(key_low, kt_full)
        + product(value_low, vt_full)
    )
    attn_rows, small = lax.optimization_barrier((attn_rows, small))
    ffn_width = up_weight.shape[1]
    summed = scatter_parts([ffn_rows, attn_rows], [[ffn_width] * 2, [head_width] * 4])
    split_width = 2 * head_width * part_count + up_bias.shape[0] * part_count
    split = small[:split_width]
    shared = small[split_width:].reshape(6, -1)
    device_id = lax.axis_index("dp") * part_count + part_id
    piece = shared.shape[1] // (lax.axis_size("dp") * part_count)
    shared = lax.dynamic_slice_in_dim(shared, device_id * piece, piece, 1)

    def own_block(vector, offset, width):
        return lax.dynamic_slice_in_dim(vector, offset + part_id * width, width, 0)

    query_bias_grad = own_block(split, 0, head_width)
    value_bias_grad = own_block(split, head_width * part_count, head_width)
    up_bias_grad = own_block(split, 2 * head_width * part_count, up_bias.shape[0])
    return (
        layer_output,
        input_grad,
        summed[2],
        query_bias_grad,
        summed[3],
        summed[4],
        value_bias_grad,
        summed[5].T,
        shared[0],
        shared[1],
        shared[2],
        summed[0],
        up_bias_grad,
        summed[1].T,
        shared[3],
        shared[4],
        shared[5],
    )


def solution(mesh):
    in_specs = (
        P("dp", None),
        P("dp", None),
        P(None, "tensor"),
        P("tensor"),
        P(None, "tensor"),
        P(None, "tensor"),
        P("tensor"),
        P("tensor", None),
        P(),
        P(),
        P(),
        P(None, "tensor"),
        P("tensor"),
        P("tensor", None),
        P(),
        P(),
        P(),
        P("dp", None),
    )
    out_specs = (
        P(("dp", "tensor"), None),
        P(("dp", "tensor"), None),
        P("dp", "tensor"),
        P("tensor"),
        P("dp", "tensor"),
        P("dp", "tensor"),
        P("tensor"),
        P("tensor", "dp"),
        P(("dp", "tensor")),
        P(("dp", "tensor")),
        P(("dp", "tensor")),
        P("dp", "tensor"),
        P("tensor"),
        P("tensor", "dp"),
        P(("dp", "tensor")),
        P(("dp", "tensor")),
        P(("dp", "tensor")),
    )
    return jax.shard_map(
        on_device, mesh=mesh, in_specs=in_specs, out_specs=out_specs, check_vma=False
    )
```

```python
import functools

import jax
import jax.numpy as jnp
from jax import lax
from jax.experimental import pallas as pl
from jax.experimental.pallas import tpu as pltpu
from jax.sharding import PartitionSpec as P

HEAD_DIM = 64
GROUP_HEADS = 3

norm_eps = 1e-06


def product(left_side, right_side):
    return jnp.dot(left_side, right_side, preferred_element_type=jnp.float32)


def contract_rows(left_side, right_side):
    return lax.dot_general(
        left_side, right_side, (((0,), (0,)), ((), ())), preferred_element_type=jnp.float32
    )


def contract_last(left_side, right_side):
    return lax.dot_general(
        left_side, right_side, (((1,), (1,)), ((), ())), preferred_element_type=jnp.float32
    )


def normalize(summed, norm_gain, offset):
    centred = summed - jnp.mean(summed, -1, keepdims=True)
    inverse = lax.rsqrt(jnp.mean(centred * centred, -1, keepdims=True) + norm_eps)
    scaled = centred * inverse
    return (scaled * norm_gain + offset, scaled, inverse)


def normalize_back(grad_out, scaled, inverse, norm_gain):
    grad_scaled = grad_out * norm_gain
    mean_grad = jnp.mean(grad_scaled, -1, keepdims=True)
    mean_cross = jnp.mean(grad_scaled * scaled, -1, keepdims=True)
    return inverse * (grad_scaled - mean_grad - scaled * mean_cross)


def gelu_tanh(pre_act):
    return jax.nn.gelu(pre_act, approximate=True)


SCALE = HEAD_DIM ** (-0.5)
STATS = 128


def _scores(q, k, linked):
    s = lax.dot_general(q, k, (((1,), (1,)), ((), ())), preferred_element_type=jnp.float32) * SCALE
    return jnp.where(linked, s, -1e30)


def attn_fwd_kernel(q_ref, k_ref, v_ref, segq_ref, segk_ref, ctx_ref, stats_ref):
    linked = segq_ref[...] == segk_ref[...]
    heads = q_ref.shape[1] // HEAD_DIM
    half = STATS // 2
    for h in range(heads):
        cols = slice(h * HEAD_DIM, (h + 1) * HEAD_DIM)
        s = _scores(q_ref[:, cols], k_ref[:, cols], linked)
        m = jnp.max(s, axis=1, keepdims=True)
        e = jnp.exp(s - m)
        l = jnp.sum(e, axis=1, keepdims=True)
        p = (e / l).astype(jnp.bfloat16)
        ctx = jnp.dot(p, v_ref[:, cols], preferred_element_type=jnp.float32)
        ctx_ref[:, cols] = ctx.astype(ctx_ref.dtype)
        stats_ref[:, h : h + 1] = m
        stats_ref[:, half + h : half + h + 1] = l


def attn_bwd_kernel(parts, q_ref, k_ref, v_ref, dctx_ref, segq_ref, segk_ref, stats_ref, x_ref, xall_ref,
                    out_t_ref, dq_ref, dk_ref, dv_ref, wgrad_ref, bias_ref, dk_acc, dv_acc, dwq_acc):
    step = pl.program_id(0)

    @pl.when(step == 0)
    def _():
        dk_acc[...] = jnp.zeros_like(dk_acc)
        dv_acc[...] = jnp.zeros_like(dv_acc)
        dwq_acc[...] = jnp.zeros_like(dwq_acc)
        bias_ref[...] = jnp.zeros_like(bias_ref)

    linked = segq_ref[...] == segk_ref[...]
    heads = q_ref.shape[1] // HEAD_DIM
    half = STATS // 2
    dq_parts = []
    for h in range(heads):
        cols = slice(h * HEAD_DIM, (h + 1) * HEAD_DIM)
        q = q_ref[:, cols]
        k = k_ref[:, cols]
        dctx = dctx_ref[:, cols]
        s = _scores(q, k, linked)
        p = jnp.exp(s - stats_ref[:, h : h + 1]) / stats_ref[:, half + h : half + h + 1]
        dp = lax.dot_general(dctx, v_ref[:, cols], (((1,), (1,)), ((), ())), preferred_element_type=jnp.float32)
        inner = jnp.sum(p * dp, axis=1, keepdims=True)
        ds = (p * (dp - inner)).astype(jnp.bfloat16)
        dq = (jnp.dot(ds, k, preferred_element_type=jnp.float32) * SCALE).astype(dq_ref.dtype)
        dq_ref[:, cols] = dq
        dq_parts.append(dq)
        dk_acc[:, cols] += lax.dot_general(ds, q, (((0,), (0,)), ((), ())), preferred_element_type=jnp.float32)
        dv_acc[:, cols] += lax.dot_general(p.astype(jnp.bfloat16), dctx, (((0,), (0,)), ((), ())), preferred_element_type=jnp.float32)
    dq_block = jnp.concatenate(dq_parts, axis=1)
    dwq_acc[...] += lax.dot_general(x_ref[...], dq_block, (((0,), (0,)), ((), ())), preferred_element_type=jnp.float32)
    bias_ref[0:1, :] += jnp.sum(dq_block.astype(jnp.float32), axis=0, keepdims=True)

    @pl.when(step == pl.num_programs(0) - 1)
    def _():
        width = dk_ref.shape[1]
        dk = (dk_acc[...] * SCALE).astype(dk_ref.dtype)
        dv = dv_acc[...].astype(dv_ref.dtype)
        dk_ref[...] = dk
        dv_ref[...] = dv
        bias_ref[1:2, :] = jnp.sum(dv.astype(jnp.float32), axis=0, keepdims=True)
        xall = xall_ref[...]
        grads = (
            dwq_acc[...].astype(wgrad_ref.dtype),
            lax.dot_general(xall, dk, (((0,), (0,)), ((), ())),
                            preferred_element_type=jnp.float32).astype(wgrad_ref.dtype),
            lax.dot_general(xall, dv, (((0,), (0,)), ((), ())),
                            preferred_element_type=jnp.float32).astype(wgrad_ref.dtype),
            out_t_ref[...],
        )
        piece = width // parts
        for part in range(parts):
            for index, grad in enumerate(grads):
                start = (part * len(grads) + index) * piece
                wgrad_ref[:, start : start + piece] = grad[:, part * piece : (part + 1) * piece]


def attention_forward(queries, key_side, value_proj, segment_row, block=256):
    length, width = queries.shape
    segq = segment_row.reshape(length, 1)
    segk = segment_row.reshape(1, length)
    full = pl.BlockSpec((length, width), lambda i: (0, 0))
    return pl.pallas_call(
        attn_fwd_kernel,
        out_shape=(jax.ShapeDtypeStruct((length, width), jnp.bfloat16),
                   jax.ShapeDtypeStruct((length, STATS), jnp.float32)),
        grid=(length // block,),
        in_specs=[pl.BlockSpec((block, width), lambda i: (i, 0)), full, full,
                  pl.BlockSpec((block, 1), lambda i: (i, 0)),
                  pl.BlockSpec((1, length), lambda i: (0, 0))],
        out_specs=(pl.BlockSpec((block, width), lambda i: (i, 0)),
                   pl.BlockSpec((block, STATS), lambda i: (i, 0))),
        compiler_params=pltpu.CompilerParams(dimension_semantics=("arbitrary",)),
        cost_estimate=pl.CostEstimate(flops=4 * length * length * width, transcendentals=length * length * width // HEAD_DIM,
                                      bytes_accessed=8 * length * width),
    )(queries, key_side, value_proj, segq, segk)


def attention_backward(queries, key_side, value_proj, segment_row, stats, grad_context, inputs, out_t, parts,
                       block=512):
    length, width = queries.shape
    features = inputs.shape[1]
    segq = segment_row.reshape(length, 1)
    segk = segment_row.reshape(1, length)
    full = pl.BlockSpec((length, width), lambda i: (0, 0))
    rows = pl.BlockSpec((block, width), lambda i: (i, 0))
    return pl.pallas_call(
        functools.partial(attn_bwd_kernel, parts),
        out_shape=tuple(jax.ShapeDtypeStruct((length, width), jnp.bfloat16) for _ in range(3))
        + (jax.ShapeDtypeStruct((features, 4 * width), jnp.bfloat16),
           jax.ShapeDtypeStruct((8, width), jnp.float32)),
        grid=(length // block,),
        in_specs=[rows, full, full, rows,
                  pl.BlockSpec((block, 1), lambda i: (i, 0)),
                  pl.BlockSpec((1, length), lambda i: (0, 0)),
                  pl.BlockSpec((block, STATS), lambda i: (i, 0)),
                  pl.BlockSpec((block, features), lambda i: (i, 0)),
                  pl.BlockSpec((length, features), lambda i: (0, 0)),
                  pl.BlockSpec((features, width), lambda i: (0, 0))],
        out_specs=(rows, full, full,
                   pl.BlockSpec((features, 4 * width), lambda i: (0, 0)),
                   pl.BlockSpec((8, width), lambda i: (0, 0))),
        scratch_shapes=[pltpu.VMEM((length, width), jnp.float32), pltpu.VMEM((length, width), jnp.float32),
                        pltpu.VMEM((features, width), jnp.float32)],
        compiler_params=pltpu.CompilerParams(dimension_semantics=("arbitrary",), vmem_limit_bytes=60 * 1024 * 1024),
        cost_estimate=pl.CostEstimate(flops=10 * length * length * width + 6 * length * features * width,
                                      transcendentals=length * length * width // HEAD_DIM,
                                      bytes_accessed=14 * length * width + 10 * features * width),
    )(queries, key_side, value_proj, grad_context, segq, segk, stats, inputs, inputs, out_t)


def gather_shards(first_pieces, second_pieces, after=None):
    dp_count = lax.axis_size("dp")
    core = lax.rem(lax.axis_index("dp"), 2)
    first, second = jnp.stack(first_pieces), jnp.stack(second_pieces)
    mine = jnp.where(core == 0, first, second)
    gathered = lax.all_gather(mine, "tensor", axis=0, tiled=False)
    if after is not None:
        gathered, after = lax.optimization_barrier((gathered, after))
    other = lax.ppermute(gathered, "dp", perm=[(i, i ^ 1) for i in range(dp_count)])
    halves = (jnp.where(core == 0, gathered, other), jnp.where(core == 0, other, gathered))
    return [half[:, index] for half in halves for index in range(half.shape[1])]


def gather_pieces(pieces, after):
    dp_count = lax.axis_size("dp")
    part_count = lax.axis_size("tensor")
    rows = pieces[0].shape[0] // dp_count
    own = lax.dynamic_slice_in_dim(jnp.stack(pieces), lax.axis_index("dp") * rows, rows, 1)
    gathered = lax.all_gather(own, ("dp", "tensor"), axis=0, tiled=False)
    gathered, after = lax.optimization_barrier((gathered, after))
    gathered = gathered.reshape((dp_count, part_count) + own.shape)
    stacks = gathered.transpose(2, 1, 0, 3, 4).reshape(
        (len(pieces), part_count, dp_count * rows) + own.shape[2:]
    )
    first_whole = gathered[:, :, 0].transpose(0, 2, 1, 3).reshape(dp_count * rows, -1)
    return [stacks[index] for index in range(len(pieces))], first_whole


def scatter_rows(grads):
    joined = jnp.concatenate([grad.astype(jnp.bfloat16) for grad in grads], axis=1)
    return lax.psum_scatter(joined, "dp", scatter_dimension=0, tiled=True)


def part_major(grads):
    parts = lax.axis_size("tensor")
    columns = []
    for part in range(parts):
        for grad in grads:
            width = grad.shape[1] // parts
            columns.append(grad[:, part * width : (part + 1) * width].astype(jnp.bfloat16))
    return jnp.concatenate(columns, axis=1)


def scatter_parts(partials, widths):
    parts = lax.axis_size("tensor")
    joined = jnp.concatenate(
        [partial.reshape(partial.shape[0], parts, -1) for partial in partials], axis=2
    )
    summed = lax.psum_scatter(joined, "tensor", scatter_dimension=1, tiled=True)[:, 0]
    pieces = []
    start = 0
    for group in widths:
        for width in group:
            pieces.append(summed[:, start : start + width].astype(jnp.float32))
            start += width
    return pieces


def on_device(
    layer_input,
    segments,
    query_weight,
    query_bias,
    key_weight,
    value_weight,
    value_bias,
    output_weight,
    output_bias,
    first_gain,
    first_shift,
    up_weight,
    up_bias,
    down_weight,
    down_bias,
    second_gain,
    second_shift,
    output_grad,
):
    part_count = lax.axis_size("tensor")
    part_id = lax.axis_index("tensor")
    row_len = segments.shape[1]

    input_rows = lax.dynamic_slice_in_dim(layer_input, part_id * row_len, row_len, 0)
    segment_row = lax.dynamic_index_in_dim(segments, part_id, 0, keepdims=False)
    grad_out = lax.dynamic_slice_in_dim(output_grad, part_id * row_len, row_len, 0).astype(
        jnp.float32
    )

    qt_sh, kt_sh, vt_sh, o_sh = gather_shards(
        [query_weight.T, key_weight.T], [value_weight.T, output_weight]
    )
    bias_sh = lax.all_gather(
        jnp.concatenate([query_bias, value_bias, up_bias]), "tensor", axis=0, tiled=False
    )
    head_width = query_bias.shape[0]
    qb = bias_sh[:, :head_width].reshape(-1)
    vb = bias_sh[:, head_width : 2 * head_width].reshape(-1)
    ub = bias_sh[:, 2 * head_width :]
    width = qt_sh.shape[2]
    qt_full = qt_sh.reshape(-1, width)
    kt_full = kt_sh.reshape(-1, width)
    vt_full = vt_sh.reshape(-1, width)

    input_f32 = input_rows.astype(jnp.float32)
    queries = (contract_last(input_rows, qt_full) + qb).astype(jnp.bfloat16)
    key_side = contract_last(input_rows, kt_full).astype(jnp.bfloat16)
    value_proj = (contract_last(input_rows, vt_full) + vb).astype(jnp.bfloat16)
    context, softmax_stats = attention_forward(queries, key_side, value_proj, segment_row)
    (u_sh, d_sh), up_whole = gather_pieces([up_weight, down_weight], context)

    group_width = o_sh.shape[1]
    attn_total = input_f32
    for member in range(part_count):
        cols = slice(member * group_width, (member + 1) * group_width)
        attn_total = attn_total + product(context[:, cols], o_sh[member]).astype(
            jnp.bfloat16
        ).astype(jnp.float32)
    first_in = attn_total + output_bias
    first_out, first_unit, first_inv = normalize(first_in, first_gain, first_shift)
    first_low = first_out.astype(jnp.bfloat16)
    pre_act = product(first_low, up_whole) + ub.reshape(-1)
    gelu_out, pull_gelu = jax.vjp(gelu_tanh, pre_act)
    hidden_low = gelu_out.astype(jnp.bfloat16)
    unit_width = hidden_low.shape[1] // part_count
    second_in = first_out
    for member in range(part_count):
        units = slice(member * unit_width, (member + 1) * unit_width)
        second_in = second_in + product(hidden_low[:, units], d_sh[member]).astype(
            jnp.bfloat16
        ).astype(jnp.float32)
    second_in = second_in + down_bias
    second_out, second_unit, second_inv = normalize(second_in, second_gain, second_shift)
    layer_output = second_out.astype(jnp.bfloat16)

    grad_second = normalize_back(grad_out, second_unit, second_inv, second_gain)
    grad_second_gain = jnp.sum(grad_out * second_unit, 0)
    grad_second_shift = jnp.sum(grad_out, 0)
    grad_down_bias = jnp.sum(grad_second, 0)
    down_low = grad_second.astype(jnp.bfloat16)
    grad_hidden = contract_last(down_low, d_sh.reshape(-1, d_sh.shape[2]))
    grad_pre = lax.optimization_barrier(pull_gelu(grad_hidden)[0].astype(jnp.bfloat16))
    first_grad = grad_second + contract_last(grad_pre, up_whole)
    grad_up_bias = jnp.sum(grad_pre, 0, dtype=jnp.float32)
    ffn_grads = [contract_rows(first_low, grad_pre), contract_rows(down_low, hidden_low)]
    ffn_joined, first_grad = lax.optimization_barrier((part_major(ffn_grads), first_grad))
    ffn_rows = scatter_rows([ffn_joined])
    grad_first_gain = jnp.sum(first_grad * first_unit, 0)
    grad_first_shift = jnp.sum(first_grad, 0)
    attn_grad = normalize_back(first_grad, first_unit, first_inv, first_gain)
    grad_output_bias = jnp.sum(attn_grad, 0)
    attn_grad_low = attn_grad.astype(jnp.bfloat16)
    grad_context = contract_last(attn_grad_low, o_sh.reshape(-1, o_sh.shape[2])).astype(
        jnp.bfloat16
    )
    output_grad_t = contract_rows(attn_grad_low, context).astype(jnp.bfloat16)
    query_low, key_low, value_low, attn_joined, qv_bias = attention_backward(
        queries, key_side, value_proj, segment_row, softmax_stats, grad_context, input_rows,
        output_grad_t, part_count,
    )
    ffn_rows, attn_joined, qv_bias = lax.optimization_barrier((ffn_rows, attn_joined, qv_bias))
    grad_query_bias = qv_bias[0]
    grad_value_bias = qv_bias[1]
    attn_rows = scatter_rows([attn_joined])
    small = lax.psum(
        jnp.concatenate(
            [
                grad_query_bias,
                grad_value_bias,
                grad_up_bias,
                grad_output_bias,
                grad_first_gain,
                grad_first_shift,
                grad_down_bias,
                grad_second_gain,
                grad_second_shift,
            ]
        ),
        ("dp", "tensor"),
    )
    small, query_low, key_low, value_low = lax.optimization_barrier(
        (small, query_low, key_low, value_low)
    )
    input_grad = (
        attn_grad
        + product(query_low, qt_full)
        + product(key_low, kt_full)
        + product(value_low, vt_full)
    )
    attn_rows, small = lax.optimization_barrier((attn_rows, small))
    ffn_width = up_weight.shape[1]
    summed = scatter_parts([ffn_rows, attn_rows], [[ffn_width] * 2, [head_width] * 4])
    split_width = 2 * head_width * part_count + up_bias.shape[0] * part_count
    split = small[:split_width]
    shared = small[split_width:].reshape(6, -1)
    device_id = lax.axis_index("dp") * part_count + part_id
    piece = shared.shape[1] // (lax.axis_size("dp") * part_count)
    shared = lax.dynamic_slice_in_dim(shared, device_id * piece, piece, 1)

    def own_block(vector, offset, width):
        return lax.dynamic_slice_in_dim(vector, offset + part_id * width, width, 0)

    query_bias_grad = own_block(split, 0, head_width)
    value_bias_grad = own_block(split, head_width * part_count, head_width)
    up_bias_grad = own_block(split, 2 * head_width * part_count, up_bias.shape[0])
    return (
        layer_output,
        input_grad,
        summed[2],
        query_bias_grad,
        summed[3],
        summed[4],
        value_bias_grad,
        summed[5].T,
        shared[0],
        shared[1],
        shared[2],
        summed[0],
        up_bias_grad,
        summed[1].T,
        shared[3],
        shared[4],
        shared[5],
    )


def solution(mesh):
    in_specs = (
        P("dp", None),
        P("dp", None),
        P(None, "tensor"),
        P("tensor"),
        P(None, "tensor"),
        P(None, "tensor"),
        P("tensor"),
        P("tensor", None),
        P(),
        P(),
        P(),
        P(None, "tensor"),
        P("tensor"),
        P("tensor", None),
        P(),
        P(),
        P(),
        P("dp", None),
    )
    out_specs = (
        P(("dp", "tensor"), None),
        P(("dp", "tensor"), None),
        P("dp", "tensor"),
        P("tensor"),
        P("dp", "tensor"),
        P("dp", "tensor"),
        P("tensor"),
        P("tensor", "dp"),
        P(("dp", "tensor")),
        P(("dp", "tensor")),
        P(("dp", "tensor")),
        P("dp", "tensor"),
        P("tensor"),
        P("tensor", "dp"),
        P(("dp", "tensor")),
        P(("dp", "tensor")),
        P(("dp", "tensor")),
    )
    return jax.shard_map(
        on_device, mesh=mesh, in_specs=in_specs, out_specs=out_specs, check_vma=False
    )
```
